32 devices in a mesh: grp: 2 (over y), dom: 8 (over z, x), segment: 2 (over core).
Axes of the slice: x: 2, y: 2, z: 4, core: 2. Of those that a mesh axis runs over, the one named last changes fastest.
Arguments:
- section_inputs: bfloat16 [2, 2, 4096, 512], P('segment', None, ('grp', 'dom')), parts along dimension 2, may hold values from -6 to 6
- out_cot: bfloat16 [2, 4096, 512], P(None, ('grp', 'dom')), parts along dimension 1, may hold values from -2 to 2
- w_node: bfloat16 [2, 512, 512], P('segment'), may hold values from -0.25 to 0.25
- w_agg: bfloat16 [2, 512, 512], P('segment'), may hold values from -0.25 to 0.25
- w_out: bfloat16 [2, 512, 512], P('segment'), may hold values from -0.25 to 0.25
- bias: bfloat16 [2, 512], P('segment'), may hold values from -3 to 3
- gain: bfloat16 [2, 512], P('segment'), may hold values from 0.25 to 1.75
- send_rows: int32 [8, 4, 32], P('dom'), may hold values from 0 to 255
- blk_pairs: int32 [8, 2, 7], P('dom'), may hold values from 0 to 2, as said below
- blk_count: int32 [8], P('dom'), may hold values from 3 to 7, as said below
- blk_values: bfloat16 [8, 7, 128, 128], P('dom'), may hold values from -0.375 to 0.375
Outputs:
- cotangents: bfloat16 [2, 2, 4096, 512], P('segment', None, ('grp', 'dom')), parts along dimension 2
- grad_node: float32 [2, 1024, 512], P('segment', ('grp', 'dom')), parts along dimension 1
- grad_agg: float32 [2, 1024, 512], P('segment', ('grp', 'dom')), parts along dimension 1
- grad_out: float32 [2, 1024, 512], P('segment', ('grp', 'dom')), parts along dimension 1
- grad_bias: float32 [2, 1024], P('segment', 'grp'), parts along dimension 1
- grad_gain: float32 [2, 1024], P('segment', 'grp'), parts along dimension 1
The draws below stay inside these ranges and needn't reach their ends.
There are 2 independent parts, one for each index of `grp`. The reference program is written for one: setup_inputs(seed, part) draws one part's arguments, and reference() takes and returns one part's arrays. A program takes and returns all parts, laid end to end along the dimension named above; an argument that names none is the same for every part. Nothing has to cross between parts.
Inputs may be any that keep to these rules, and one draw needn't show every extreme that they name: `blk_pairs`: slots 0 to 1 pair destination block k with source block k; slot 2 reads source block 2, the first block of halo rows; destination blocks lie below 2. `blk_count`: some partition has all 7 slots live.
All inputs are finite; a program needn't handle non-finite values.
Results may differ from the reference program's by a relative error of at most 0.0075.
Values may be sent and summed in bfloat16 or wider, within the bound.
No kernel may reach another device: no remote copies, remote signals or barrier semaphores. Data moves between devices by JAX's collectives and lax.ppermute only.
A program may use at most 64 MiB of HBM per device.

```python
import jax
import jax.numpy as jnp
from jax import lax

D = 512
ROWS_DEV = 256
HALO = 128
NEIGHBOURS = 4
MICRO = 2
BLOCKS_DEV = 7
HALO_PEER = 32
NODES = 2048
N_DOM = 8
N_SEGMENT = 2


def draw_blk_pairs(key, part):
    row_blocks = ROWS_DEV // 128
    src_blocks = row_blocks + HALO // 128
    split_keys = jax.random.split(jax.random.fold_in(key, 11), 2)
    dst_block = jax.random.randint(split_keys[0], (N_DOM, BLOCKS_DEV), 0, row_blocks)
    src_block = jax.random.randint(split_keys[1], (N_DOM, BLOCKS_DEV), 0, src_blocks)
    slot_ids = jnp.arange(BLOCKS_DEV, dtype=jnp.int32)[None, :]
    dst_block = jnp.where(slot_ids < row_blocks, slot_ids, dst_block)
    src_block = jnp.where(slot_ids < row_blocks, slot_ids, src_block)
    src_block = jnp.where(slot_ids == row_blocks, row_blocks, src_block)
    return jnp.stack([dst_block, src_block], axis=1).astype(jnp.int32)


def draw_blk_count(key, part):
    row_blocks = ROWS_DEV // 128
    spare = BLOCKS_DEV - row_blocks - 1
    split_keys = jax.random.split(jax.random.fold_in(key, 23), 3)
    first_draw = jax.random.randint(split_keys[0], (N_DOM,), 0, spare + 1)
    second_draw = jax.random.randint(split_keys[1], (N_DOM,), 0, spare + 1)
    extra = first_draw * second_draw // max(spare, 1)
    fullest = jax.random.randint(split_keys[2], (), 0, N_DOM)
    counts = jnp.where(jnp.arange(N_DOM, dtype=jnp.int32) == fullest, BLOCKS_DEV, row_blocks + 1 + extra)
    return counts.astype(jnp.int32)


def with_ends(values, own_key, low, largest):
    index_at = [jax.random.randint(jax.random.fold_in(own_key, axis), (), 0, length) for axis, length in enumerate(values.shape)]
    longest = values.shape.index(max(values.shape))
    neighbour = index_at[:longest] + [(index_at[longest] + 1) % values.shape[longest]] + index_at[longest + 1:]
    return values.at[tuple(index_at)].set(low).at[tuple(neighbour)].set(largest)


def block_levels(rng, extent, pieces, smallest, high):
    def one(dim, blocks):
        draws = jax.random.uniform(jax.random.fold_in(jax.random.fold_in(rng, 6), dim), (blocks,), jnp.float32, smallest / len(pieces), high / len(pieces))
        return jnp.repeat(jnp.exp(draws), extent[dim] // blocks).reshape((-1,) + (1,) * (len(extent) - dim - 1))

    loudness = one(*pieces[0])
    for cut in pieces[1:]:
        loudness = loudness * one(*cut)
    return loudness


def normal_values(key, shape, width, most, cuts=(), kind=jnp.bfloat16):
    values = width * jax.random.normal(key, shape, jnp.float32)
    if cuts:
        values = values * block_levels(key, shape, cuts, -0.22, 0.18)
    return jnp.clip(values, -most, most).astype(kind)


def setup_inputs(seed: int = 0, part: int = 0) -> dict:
    arg_keys = jax.random.split(jax.random.key(seed), 12)
    part_splits = jax.random.split(jax.random.fold_in(arg_keys[11], part), 12)
    return {
        "section_inputs": normal_values(part_splits[0], (N_SEGMENT, MICRO, NODES, D), 1.0, 6.0, ((0, 2), (2, 8))),
        "out_cot": normal_values(part_splits[1], (MICRO, NODES, D), ((MICRO * NODES) ** -0.25), 2.0, ((1, 8),)),
        "w_node": normal_values(arg_keys[2], (N_SEGMENT, D, D), D ** -0.5, 0.25, ((0, 2),)),
        "w_agg": normal_values(arg_keys[3], (N_SEGMENT, D, D), D ** -0.5, 0.25, ((0, 2),)),
        "w_out": normal_values(arg_keys[4], (N_SEGMENT, D, D), D ** -0.5, 0.25, ((0, 2),)),
        "bias": normal_values(arg_keys[5], (N_SEGMENT, D), 0.5, 3.0, ((0, 2),)),
        "gain": jnp.clip(1.0 + 0.15 * jax.random.normal(arg_keys[6], (N_SEGMENT, D), jnp.float32), 0.25, 1.75).astype(jnp.bfloat16),
        "send_rows": with_ends(jax.random.randint(arg_keys[7], (N_DOM, NEIGHBOURS, HALO_PEER), 0, ROWS_DEV), jax.random.fold_in(arg_keys[7], 1), 0, ROWS_DEV - 1).astype(jnp.int32),
        "blk_pairs": draw_blk_pairs(jax.random.fold_in(arg_keys[11], 71), part),
        "blk_count": draw_blk_count(jax.random.fold_in(arg_keys[11], 71), part),
        "blk_values": normal_values(arg_keys[10], (N_DOM, BLOCKS_DEV, 128, 128), 256 ** -0.5, 0.375, ((0, 8),)),
    }


EPSILON = 1e-05
PRECISE = lax.Precision.HIGHEST
OFFSETS = (1, -1, 2, -2)

def aggregate(source, values, pairs, live_count, out_blocks):
    feat_width = source.shape[1]
    blocks = source.reshape(-1, 128, feat_width)
    picked = blocks[pairs[1]].astype(jnp.float32)
    products = jnp.einsum('kij,kjd->kid', values.astype(jnp.float32), picked, precision=PRECISE)
    is_live = jnp.arange(pairs.shape[1], dtype=jnp.int32) < live_count
    onehot = ((pairs[0][None, :] == jnp.arange(out_blocks, dtype=jnp.int32)[:, None]) & is_live[None, :]).astype(jnp.float32)
    summed = jnp.einsum('bk,kid->bid', onehot, products, precision=PRECISE)
    return summed.reshape(out_blocks * 128, feat_width)

def spread(grad_rows, values, pairs, live_count, out_blocks):
    feat_width = grad_rows.shape[1]
    blocks = grad_rows.reshape(-1, 128, feat_width)
    picked = blocks[pairs[0]].astype(jnp.float32)
    products = jnp.einsum('kij,kid->kjd', values.astype(jnp.float32), picked, precision=PRECISE)
    is_live = jnp.arange(pairs.shape[1], dtype=jnp.int32) < live_count
    onehot = ((pairs[1][None, :] == jnp.arange(out_blocks, dtype=jnp.int32)[:, None]) & is_live[None, :]).astype(jnp.float32)
    summed = jnp.einsum('sk,kjd->sjd', onehot, products, precision=PRECISE)
    return summed.reshape(out_blocks * 128, feat_width)

def layer_backward(x_rows, halo_rows, grad_in, values, pairs, live_count, node_mat, agg_mat, out_mat, bias_row, gain_row):
    num_rows = x_rows.shape[0]
    source = jnp.concatenate([x_rows, halo_rows], 0)
    agg = aggregate(source, values, pairs, live_count, num_rows // 128).astype(jnp.bfloat16)
    preact = jnp.dot(x_rows, node_mat, preferred_element_type=jnp.float32) + jnp.dot(agg, agg_mat, preferred_element_type=jnp.float32) + bias_row
    sigmoid_z = jax.nn.sigmoid(preact)
    hidden = (preact * sigmoid_z).astype(jnp.bfloat16)
    output = jnp.dot(hidden, out_mat, preferred_element_type=jnp.float32)
    centred = output - lax.optimization_barrier(jnp.mean(output, axis=1, keepdims=True))
    inv_std = lax.rsqrt(lax.optimization_barrier(jnp.mean(centred * centred, axis=1, keepdims=True)) + EPSILON)
    normed = centred * inv_std
    grad_f32 = grad_in.astype(jnp.float32)
    grad_normed = grad_f32 * gain_row
    grad_pre_norm = (inv_std * (grad_normed - lax.optimization_barrier(jnp.mean(grad_normed, axis=1, keepdims=True)) - normed * lax.optimization_barrier(jnp.mean(grad_normed * normed, axis=1, keepdims=True)))).astype(jnp.bfloat16)
    grad_hidden = jnp.dot(grad_pre_norm, out_mat.T, preferred_element_type=jnp.float32)
    grad_preact = (grad_hidden * sigmoid_z * (1.0 + preact * (1.0 - sigmoid_z))).astype(jnp.bfloat16)
    grad_x = grad_f32 + jnp.dot(grad_preact, node_mat.T, preferred_element_type=jnp.float32)
    grad_messages = jnp.dot(grad_preact, agg_mat.T, preferred_element_type=jnp.float32).astype(jnp.bfloat16)
    grad_source = spread(grad_messages, values, pairs, live_count, source.shape[0] // 128)
    grad_x = grad_x + grad_source[:num_rows]
    grad_halo = grad_source[num_rows:].astype(jnp.bfloat16)
    gain_terms = lax.optimization_barrier(jnp.sum(grad_f32 * normed, axis=0))
    bias_terms = lax.optimization_barrier(jnp.sum(grad_preact.astype(jnp.float32), axis=0))
    return (grad_x, grad_halo, agg, hidden, grad_pre_norm, grad_preact, gain_terms, bias_terms)

def sender_table(partitions):
    offsets = jnp.array(OFFSETS, dtype=jnp.int32)
    return (jnp.arange(partitions, dtype=jnp.int32)[:, None] - offsets[None, :]) % partitions

def gather_halo(x_parts, send_rows):
    partitions = x_parts.shape[0]
    senders = sender_table(partitions)
    slot_ids = jnp.arange(len(OFFSETS), dtype=jnp.int32)[None, :]
    rows = send_rows[senders, slot_ids]
    picked = x_parts[senders[:, :, None], rows]
    return picked.reshape(partitions, -1, x_parts.shape[2])

def return_halo(grad_halo, send_rows, num_rows):
    partitions = grad_halo.shape[0]
    per_peer = send_rows.shape[2]
    feat_width = grad_halo.shape[2]
    senders = sender_table(partitions)
    slot_ids = jnp.arange(len(OFFSETS), dtype=jnp.int32)[None, :]
    rows = send_rows[senders, slot_ids]
    returned = grad_halo.reshape(partitions, len(OFFSETS), per_peer, feat_width)
    empty = jnp.zeros((partitions, num_rows, feat_width), jnp.float32)
    return empty.at[senders[:, :, None], rows].add(returned)

def flatten(parts_array):
    return parts_array.reshape(-1, parts_array.shape[-1])

def reference(section_inputs, out_cot, w_node, w_agg, w_out, bias, gain, send_rows, blk_pairs, blk_count, blk_values):
    partitions = N_DOM
    upstream = out_cot.reshape(MICRO, partitions, ROWS_DEV, D)
    segment_cots = [None] * N_SEGMENT
    node_grads = [None] * N_SEGMENT
    agg_grads = [None] * N_SEGMENT
    out_grads = [None] * N_SEGMENT
    bias_grads = [None] * N_SEGMENT
    gain_grads = [None] * N_SEGMENT
    for segment_num in range(N_SEGMENT - 1, -1, -1):
        node_mat = w_node[segment_num]
        agg_mat = w_agg[segment_num]
        out_mat = w_out[segment_num]
        bias_row = bias[segment_num].astype(jnp.float32)
        gain_row = gain[segment_num].astype(jnp.float32)
        grad_node_acc = jnp.zeros((D, D), jnp.float32)
        grad_agg_acc = jnp.zeros((D, D), jnp.float32)
        grad_out_acc = jnp.zeros((D, D), jnp.float32)
        bias_acc = jnp.zeros((D,), jnp.float32)
        gain_acc = jnp.zeros((D,), jnp.float32)
        results = []
        for micro_num in range(MICRO):
            x_parts = section_inputs[segment_num, micro_num].reshape(partitions, ROWS_DEV, D)
            halo_parts = gather_halo(x_parts, send_rows)

            def per_partition(packed):
                x_rows, halo_rows, grad_in, values, pairs, live_count = packed
                return layer_backward(x_rows, halo_rows, grad_in, values, pairs, live_count, node_mat, agg_mat, out_mat, bias_row, gain_row)
            grad_x, grad_halo, agg, hidden, grad_pre_norm, grad_preact, gain_terms, bias_terms = lax.map(per_partition, (x_parts, halo_parts, upstream[micro_num], blk_values, blk_pairs, blk_count))
            grad_x = grad_x + return_halo(grad_halo.astype(jnp.float32), send_rows, ROWS_DEV)
            results.append(grad_x.astype(jnp.bfloat16))
            grad_node_acc = grad_node_acc + jnp.dot(flatten(x_parts).T, flatten(grad_preact), preferred_element_type=jnp.float32)
            grad_agg_acc = grad_agg_acc + jnp.dot(flatten(agg).T, flatten(grad_preact), preferred_element_type=jnp.float32)
            grad_out_acc = grad_out_acc + jnp.dot(flatten(hidden).T, flatten(grad_pre_norm), preferred_element_type=jnp.float32)
            bias_acc = bias_acc + lax.optimization_barrier(jnp.sum(bias_terms, axis=0))
            gain_acc = gain_acc + lax.optimization_barrier(jnp.sum(gain_terms, axis=0))
        upstream = jnp.stack(results)
        segment_cots[segment_num] = upstream.reshape(MICRO, partitions * ROWS_DEV, D)
        node_grads[segment_num] = grad_node_acc
        agg_grads[segment_num] = grad_agg_acc
        out_grads[segment_num] = grad_out_acc
        bias_grads[segment_num] = bias_acc
        gain_grads[segment_num] = gain_acc
    return (jnp.stack(segment_cots), jnp.stack(node_grads), jnp.stack(agg_grads), jnp.stack(out_grads), jnp.stack(bias_grads), jnp.stack(gain_grads))
```

```python
import functools

import jax
import jax.numpy as jnp
from jax import lax
from jax.experimental import pallas as pl
from jax.experimental.pallas import tpu as pltpu
from jax.sharding import PartitionSpec as P

EPSILON = 1e-05
OFFSETS = (1, -1, 2, -2)
F32 = jnp.float32
BF16 = jnp.bfloat16
VMEM = pl.BlockSpec(memory_space=pltpu.VMEM)
SMEM = pl.BlockSpec(memory_space=pltpu.SMEM)
EXTRA = 8


def nt_dot(a, b):
    return lax.dot_general(a, b, (((1,), (1,)), ((), ())), preferred_element_type=F32)


def tn_dot(a, b):
    return lax.dot_general(a, b, (((0,), (0,)), ((), ())), preferred_element_type=F32)


def call(kernel, outs, scratch, flops, byts, *args):
    specs = [SMEM if a.dtype == jnp.int32 and a.ndim < 3 and a.size < 64 else VMEM for a in args]
    return pl.pallas_call(
        kernel,
        out_shape=outs,
        in_specs=specs,
        out_specs=jax.tree.map(lambda _: VMEM, outs),
        scratch_shapes=scratch,
        compiler_params=pltpu.CompilerParams(vmem_limit_bytes=48 * 1024 * 1024),
        cost_estimate=pl.CostEstimate(flops=flops, bytes_accessed=byts, transcendentals=0),
    )(*args)


def gather_kernel(targets_ref, x_ref, *outs):
    micro, rows, _ = x_ref.shape
    for k in range(len(OFFSETS)):
        per_peer = outs[k].shape[0] // micro
        ids = targets_ref[k]
        onehot = (lax.broadcasted_iota(jnp.int32, (per_peer, rows), 1) == ids).astype(BF16)
        for m in range(micro):
            outs[k][m * per_peer : (m + 1) * per_peer, :] = jnp.dot(
                onehot, x_ref[m], preferred_element_type=F32
            ).astype(BF16)


def node_kernel(x_ref, w_ref, bias_ref, z_ref):
    micro, rows, _ = x_ref.shape
    for m in range(micro):
        z_ref[m * rows : (m + 1) * rows, :] = (
            jnp.dot(x_ref[m], w_ref[...], preferred_element_type=F32) + bias_ref[...].astype(F32)
        )


def layer_back(g, dact, normed, inv_std, gain, w_out_ref):
    e = g * gain
    gpn = (
        inv_std
        * (
            e
            - jnp.mean(e, axis=1, keepdims=True)
            - normed * jnp.mean(e * normed, axis=1, keepdims=True)
        )
    ).astype(BF16)
    gpre = (nt_dot(gpn, w_out_ref[...]) * dact).astype(BF16)
    return gpn, gpre


def spread_out(pairs_ref, count_ref, values_ref, gm_ref, t_ref, cpart_ref, halo_outs):
    slots = values_ref.shape[0]
    micro_rows = cpart_ref.shape[0] // 2
    feat = cpart_ref.shape[1]
    t_ref[...] = jnp.zeros_like(t_ref)
    for k in range(slots):

        @pl.when(k < count_ref[0])
        def _():
            src = pairs_ref[1, k]
            t_ref[src] += tn_dot(values_ref[k], gm_ref[pairs_ref[0, k]])

    row_blocks = micro_rows // 128
    for m in range(2):
        cols = slice(m * feat, (m + 1) * feat)
        for b in range(row_blocks):
            rows = slice(m * micro_rows + b * 128, m * micro_rows + (b + 1) * 128)
            cpart_ref[rows, :] += t_ref[b, :, cols]
        for k in range(len(halo_outs)):
            per_peer = halo_outs[k].shape[0] // 2
            first = k * per_peer
            blk, off = row_blocks + first // 128, first % 128
            halo_outs[k][m * per_peer : (m + 1) * per_peer, :] = t_ref[
                blk, off : off + per_peer, cols
            ].astype(BF16)


def tail(m, rows, g, gpre, w_node_ref, w_agg_ref, cpart_ref, gm_ref):
    feat = w_node_ref.shape[0]
    cpart_ref[m * rows : (m + 1) * rows, :] = g + nt_dot(gpre, w_node_ref[...])
    gm = nt_dot(gpre, w_agg_ref[...]).astype(BF16)
    for b in range(rows // 128):
        gm_ref[b, :, m * feat : (m + 1) * feat] = gm[b * 128 : (b + 1) * 128]


def first_kernel(
    pairs_ref, count_ref, x_ref, h0, h1, h2, h3, values_ref, z_ref, g_ref, w_node_ref, w_agg_ref,
    w_out_ref, gain_ref,
    o0, o1, o2, o3, cpart_ref, dact_ref, normed_ref, inv_ref, agg_ref, hidden_ref, gpn_ref,
    gpre_ref, sums_ref,
    src_ref, acc_ref, gm_ref, t_ref,
):
    micro, rows, feat = x_ref.shape
    row_blocks = rows // 128
    halos = (h0, h1, h2, h3)
    for m in range(micro):
        cols = slice(m * feat, (m + 1) * feat)
        for b in range(row_blocks):
            src_ref[b, :, cols] = x_ref[m, b * 128 : (b + 1) * 128, :]
        for k, h in enumerate(halos):
            per_peer = h.shape[0] // micro
            first = k * per_peer
            blk, off = row_blocks + first // 128, first % 128
            src_ref[blk, off : off + per_peer, cols] = h[m * per_peer : (m + 1) * per_peer, :]
    acc_ref[...] = jnp.zeros_like(acc_ref)
    for k in range(values_ref.shape[0]):

        @pl.when(k < count_ref[0])
        def _():
            dst = pairs_ref[0, k]
            acc_ref[dst] += jnp.dot(
                values_ref[k], src_ref[pairs_ref[1, k]], preferred_element_type=F32
            )

    gain = gain_ref[...].astype(F32)
    gain_sum = jnp.zeros((1, feat), F32)
    bias_sum = jnp.zeros((1, feat), F32)
    for m in range(micro):
        part = slice(m * rows, (m + 1) * rows)
        agg = jnp.concatenate(
            [acc_ref[b, :, m * feat : (m + 1) * feat] for b in range(row_blocks)], 0
        ).astype(BF16)
        agg_ref[part, :] = agg
        preact = z_ref[part, :] + jnp.dot(agg, w_agg_ref[...], preferred_element_type=F32)
        sig = 1.0 / (1.0 + jnp.exp(-preact))
        hidden = (preact * sig).astype(BF16)
        dact = sig * (1.0 + preact * (1.0 - sig))
        dact_ref[part, :] = dact
        hidden_ref[part, :] = hidden
        output = jnp.dot(hidden, w_out_ref[...], preferred_element_type=F32)
        centred = output - jnp.mean(output, axis=1, keepdims=True)
        inv_std = lax.rsqrt(jnp.mean(centred * centred, axis=1, keepdims=True) + EPSILON)
        normed = centred * inv_std
        normed_ref[part, :] = normed
        inv_ref[part, :] = jnp.broadcast_to(inv_std, (rows, 128))
        g = g_ref[m].astype(F32)
        gpn, gpre = layer_back(g, dact, normed, inv_std, gain, w_out_ref)
        gpn_ref[part, :] = gpn
        gpre_ref[part, :] = gpre
        gain_sum += jnp.sum(g * normed, axis=0, keepdims=True)
        bias_sum += jnp.sum(gpre.astype(F32), axis=0, keepdims=True)
        tail(m, rows, g, gpre, w_node_ref, w_agg_ref, cpart_ref, gm_ref)
    sums_ref[0:1, :] = bias_sum
    sums_ref[1:2, :] = gain_sum
    spread_out(pairs_ref, count_ref, values_ref, gm_ref, t_ref, cpart_ref, (o0, o1, o2, o3))


def scatter_onehot(targets_ref, rows):
    ids = targets_ref[...]
    return (lax.broadcasted_iota(jnp.int32, (ids.shape[0], rows), 1) == ids).astype(BF16)


def scatter_add(onehot, rets, m):
    per_peer = rets[0].shape[0] // 2
    ret = jnp.concatenate([r[m * per_peer : (m + 1) * per_peer, :] for r in rets], 0)
    return tn_dot(onehot, ret)


def second_kernel(
    me_ref, pairs_ref, count_ref, targets_ref, r0, r1, r2, r3, cin_ref, values_ref, dact_ref,
    normed_ref, inv_ref, gpn1_ref, gpre1_ref, sums1_ref, w_node_ref, w_agg_ref, w_out_ref, gain_ref,
    o0, o1, o2, o3, cpart_ref, g_out_ref, gpn_ref, gpre_ref, sums_ref,
    gm_ref, t_ref,
):
    rows = dact_ref.shape[0] // 2
    feat = dact_ref.shape[1]
    onehot = scatter_onehot(targets_ref, rows)
    gain = gain_ref[...].astype(F32)
    is_last = me_ref[0] == 1
    gain_sum = jnp.zeros((1, feat), F32)
    bias_sum = jnp.zeros((1, feat), F32)
    for m in range(2):
        part = slice(m * rows, (m + 1) * rows)
        g16 = (cin_ref[part, :] + scatter_add(onehot, (r0, r1, r2, r3), m)).astype(BF16)
        g_out_ref[part, :] = g16
        g = g16.astype(F32)
        normed = normed_ref[part, :]
        gpn, gpre = layer_back(
            g, dact_ref[part, :], normed, inv_ref[part, 0:1], gain, w_out_ref
        )
        gpn_ref[part, :] = jnp.where(is_last, gpn1_ref[part, :], gpn)
        gpre_ref[part, :] = jnp.where(is_last, gpre1_ref[part, :], gpre)
        gain_sum += jnp.sum(g * normed, axis=0, keepdims=True)
        bias_sum += jnp.sum(gpre.astype(F32), axis=0, keepdims=True)
        tail(m, rows, g, gpre, w_node_ref, w_agg_ref, cpart_ref, gm_ref)
    sums_ref[0:1, :] = jnp.where(is_last, sums1_ref[0:1, :], bias_sum)
    sums_ref[1:2, :] = jnp.where(is_last, sums1_ref[1:2, :], gain_sum)
    spread_out(pairs_ref, count_ref, values_ref, gm_ref, t_ref, cpart_ref, (o0, o1, o2, o3))


def split_chunks(refs_at, keep_ref, send_ref, bit, mine):
    count = 2 * keep_ref.shape[0]
    step = 1 << bit
    low = [d for d in range(count) if not d & step]
    for i, d in enumerate(low):
        refs_at(d + mine * step, i, keep_ref, False)
        refs_at(d + (1 - mine) * step, i, send_ref, True)


def weight_kernel(
    me_ref, x_ref, agg_ref, hidden_ref, gpn_ref, gpre_ref, sums_ref,
    keep_a, keep_b, send_a, send_b, node_s, agg_s, out_s,
):
    micro, rows, feat = x_ref.shape
    chunks = node_s.shape[0]
    share = feat // chunks
    half = share // 2
    gpre = gpre_ref[...]
    node = tn_dot(x_ref[0], gpre[:rows]) + tn_dot(x_ref[1], gpre[rows:])
    node_s[...] = node.reshape(chunks, share, feat)
    agg_s[...] = tn_dot(agg_ref[...], gpre).reshape(chunks, share, feat)

    def put_a(d, i, ref, narrow):
        ref[i, 0:share, :] = node_s[d].astype(ref.dtype)
        ref[i, share : share + half, :] = agg_s[d, 0:half, :].astype(ref.dtype)

    split_chunks(put_a, keep_a, send_a, 0, me_ref[1])
    out_s[...] = tn_dot(hidden_ref[...], gpn_ref[...]).reshape(chunks, share, feat)
    sums = jnp.concatenate([sums_ref[0:2, :], jnp.zeros((EXTRA - 2, feat), F32)], 0)

    def put_b(d, i, ref, narrow):
        ref[i, 0:half, :] = agg_s[d, half:share, :].astype(ref.dtype)
        ref[i, half : half + share, :] = out_s[d].astype(ref.dtype)
        ref[i, half + share : half + share + EXTRA, :] = sums.astype(ref.dtype)

    split_chunks(put_b, keep_b, send_b, 1, me_ref[2])


def halve_kernel(bits, me_ref, keep_a, keep_b, recv_a, recv_b, keep_a2, keep_b2, send_a2, send_b2):
    for (pos, which), keep, recv, keep2, send2 in (
        (bits[0], keep_a, recv_a, keep_a2, send_a2),
        (bits[1], keep_b, recv_b, keep_b2, send_b2),
    ):

        def put(d, i, ref, narrow):
            ref[i] = (keep[d] + recv[d].astype(F32)).astype(ref.dtype)

        split_chunks(put, keep2, send2, pos, me_ref[which])


def last_kernel(keep_a, keep_b, recv_a, recv_b, node_ref, agg_ref, out_ref, sums_ref):
    share = node_ref.shape[0]
    half = share // 2
    a = keep_a[0] + recv_a[0].astype(F32)
    b = keep_b[0] + recv_b[0].astype(F32)
    node_ref[...] = a[0:share]
    agg_ref[0:half, :] = a[share : share + half]
    agg_ref[half:share, :] = b[0:half]
    out_ref[...] = b[half : half + share]
    sums_ref[...] = b[half + share : half + share + EXTRA]


def cot_kernel(me_ref, targets_ref, r0, r1, r2, r3, cpart_ref, other_ref, cot_ref):
    micro, rows, feat = cot_ref.shape

    @pl.when(me_ref[0] == 1)
    def _():
        for m in range(micro):
            cot_ref[m] = other_ref[m * rows : (m + 1) * rows, :]

    @pl.when(me_ref[0] != 1)
    def _():
        onehot = scatter_onehot(targets_ref, rows)
        for m in range(micro):
            cot_ref[m] = (
                cpart_ref[m * rows : (m + 1) * rows, :] + scatter_add(onehot, (r0, r1, r2, r3), m)
            ).astype(BF16)


def whole_kernel(x_ref, agg_ref, hidden_ref, gpn_ref, gpre_ref, node_ref, agg_out, out_ref):
    rows = x_ref.shape[1]
    gpre = gpre_ref[...]
    node_ref[...] = tn_dot(x_ref[0], gpre[:rows]) + tn_dot(x_ref[1], gpre[rows:])
    agg_out[...] = tn_dot(agg_ref[...], gpre)
    out_ref[...] = tn_dot(hidden_ref[...], gpn_ref[...])


def shape(dims, dtype):
    return jax.ShapeDtypeStruct(dims, dtype)


def body(
    section_inputs,
    out_cot,
    w_node,
    w_agg,
    w_out,
    bias,
    gain,
    send_rows,
    blk_pairs,
    blk_count,
    blk_values,
):
    assert lax.axis_size("segment") == 2
    segment = lax.axis_index("segment")
    peers = lax.axis_size("dom")
    dom = lax.axis_index("dom")
    x = section_inputs[0]
    micro, rows, feat = x.shape
    targets = send_rows[0]
    slots, per_peer = targets.shape
    total = micro * rows
    pairs = blk_pairs[0]
    values = blk_values[0]
    halo_blocks = slots * per_peer // 128
    row_blocks = rows // 128
    blocks = row_blocks + halo_blocks
    wide = micro * feat
    flat_targets = targets.reshape(slots * per_peer, 1)
    w_n, w_a, w_o = w_node[0], w_agg[0], w_out[0]
    me = jnp.stack([segment, dom & 1, (dom >> 1) & 1, (dom >> 2) & 1]).astype(jnp.int32)
    matmul = 2 * total * feat * feat
    size = total * feat
    chunk = shape((micro * per_peer, feat), BF16)

    def moved(v, offset, src, dst):
        return lax.ppermute(
            v,
            ("dom", "segment"),
            [(2 * p + src, 2 * ((p + offset) % peers) + dst) for p in range(peers)],
        )

    def shifted(v, offset):
        return lax.ppermute(v, "dom", [(p, (p + offset) % peers) for p in range(peers)])

    def flipped(v, bit):
        return lax.ppermute(v, "dom", [(p, p ^ (1 << bit)) for p in range(peers)])

    outgoing = call(
        gather_kernel, [chunk] * slots, [], matmul // 8, 2 * size,
        targets.reshape(slots, per_peer, 1), x,
    )
    halos = [shifted(v, o) for v, o in zip(outgoing, OFFSETS)]
    z = call(node_kernel, shape((total, feat), F32), [], matmul, 8 * size, x, w_n, bias)
    f_full, b_full = shape((total, feat), F32), shape((total, feat), BF16)
    s_sums = shape((EXTRA, feat), F32)
    scr_gm = pltpu.VMEM((row_blocks, 128, wide), BF16)
    scr_t = pltpu.VMEM((blocks, 128, wide), F32)
    first = call(
        first_kernel,
        [chunk] * slots
        + [f_full, f_full, f_full, shape((total, 128), F32), b_full, b_full, b_full, b_full, s_sums],
        [
            pltpu.VMEM((blocks, 128, wide), BF16),
            pltpu.VMEM((row_blocks, 128, wide), F32),
            scr_gm,
            scr_t,
        ],
        6 * matmul, 24 * size,
        pairs, blk_count, x, *halos, values, z, out_cot, w_n, w_a, w_o, gain,
    )
    to_return, (cpart1, dact, normed, inv_std, agg, hidden, gpn1, gpre1, sums1) = (
        first[:slots], first[slots:],
    )
    returned = [moved(v, -o, 1, 0) for v, o in zip(to_return, OFFSETS)]
    c_in = moved(cpart1, 0, 1, 0)
    second = call(
        second_kernel,
        [chunk] * slots + [f_full, b_full, b_full, b_full, s_sums],
        [scr_gm, scr_t],
        4 * matmul, 24 * size,
        me, pairs, blk_count, flat_targets, *returned, c_in, values, dact, normed, inv_std, gpn1, gpre1,
        sums1, w_n, w_a, w_o, gain,
    )
    to_return, (cpart0, g_low, gpn, gpre, sums) = second[:slots], second[slots:]
    returned = [moved(v, -o, 0, 0) for v, o in zip(to_return, OFFSETS)]
    other = moved(g_low, 0, 0, 1)
    share = feat // peers
    if peers == 8:
        half = share // 2
        na, nb = share + half, share + half + EXTRA

        def parts(n):
            return [
                shape((n, na, feat), F32), shape((n, nb, feat), F32),
                shape((n, na, feat), BF16), shape((n, nb, feat), BF16),
            ]

        keep_a, keep_b, send_a, send_b = call(
            weight_kernel, parts(4), [pltpu.VMEM((8, share, feat), F32)] * 3,
            3 * matmul, 12 * size, me, x, agg, hidden, gpn, gpre, sums,
        )
        recv_a, recv_b = flipped(send_a, 0), flipped(send_b, 1)
        keep_a, keep_b, send_a, send_b = call(
            functools.partial(halve_kernel, ((0, 2), (0, 1))), parts(2), [], size, 8 * size,
            me, keep_a, keep_b, recv_a, recv_b,
        )
        recv_a, recv_b = flipped(send_a, 1), flipped(send_b, 0)
        keep_a, keep_b, send_a, send_b = call(
            functools.partial(halve_kernel, ((0, 3), (0, 3))), parts(1), [], size, 4 * size,
            me, keep_a, keep_b, recv_a, recv_b,
        )
        recv_a, recv_b = flipped(send_a, 2), flipped(send_b, 2)
        part = shape((share, feat), F32)
        grad_node, grad_agg, grad_out, sums = call(
            last_kernel, [part, part, part, s_sums], [], size, 2 * size,
            keep_a, keep_b, recv_a, recv_b,
        )
    else:
        square = shape((feat, feat), F32)
        full = call(
            whole_kernel, [square] * 3, [], 3 * matmul, 12 * size, x, agg, hidden, gpn, gpre
        )
        grad_node, grad_agg, grad_out = [
            lax.psum_scatter(v, "dom", scatter_dimension=0, tiled=True) for v in full
        ]
        sums = lax.psum(sums, "dom")
    cot = call(
        cot_kernel, shape((micro, rows, feat), BF16), [], matmul // 4, 4 * size,
        me, flat_targets, *returned, cpart0, other,
    )
    return (
        cot[None],
        grad_node[None],
        grad_agg[None],
        grad_out[None],
        sums[0:1],
        sums[1:2],
    )


def solution(mesh):
    placed = (
        P("segment", None, ("grp", "dom"), None),
        P(None, ("grp", "dom"), None),
        P("segment", None, None),
        P("segment", None, None),
        P("segment", None, None),
        P("segment", None),
        P("segment", None),
        P("dom", None, None),
        P("dom", None, None),
        P("dom"),
        P("dom", None, None, None),
    )
    return jax.shard_map(
        body,
        mesh=mesh,
        in_specs=placed,
        out_specs=(
            P("segment", None, ("grp", "dom"), None),
            P("segment", ("grp", "dom"), None),
            P("segment", ("grp", "dom"), None),
            P("segment", ("grp", "dom"), None),
            P("segment", "grp"),
            P("segment", "grp"),
        ),
        check_vma=False,
    )
```

```python
import functools

import jax
import jax.numpy as jnp
from jax import lax
from jax.experimental import pallas as pl
from jax.experimental.pallas import tpu as pltpu
from jax.sharding import PartitionSpec as P

EPSILON = 1e-05
F32 = jnp.float32
BF16 = jnp.bfloat16
VMEM = pl.BlockSpec(memory_space=pltpu.VMEM)
SMEM = pl.BlockSpec(memory_space=pltpu.SMEM)
PEERS = 4
EXTRA = 8
PIECE = 64


def nn_dot(a, b):
    return jnp.dot(a, b, preferred_element_type=F32)


def nt_dot(a, b):
    return lax.dot_general(a, b, (((1,), (1,)), ((), ())), preferred_element_type=F32)


def tn_dot(a, b):
    return lax.dot_general(a, b, (((0,), (0,)), ((), ())), preferred_element_type=F32)


def shape(dims, dtype):
    return jax.ShapeDtypeStruct(dims, dtype)


def call(kernel, outs, scratch, flops, byts, *args, scalars=0):
    return pl.pallas_call(
        kernel,
        out_shape=outs,
        in_specs=[SMEM] * scalars + [VMEM] * (len(args) - scalars),
        out_specs=jax.tree.map(lambda _: VMEM, outs),
        scratch_shapes=scratch,
        compiler_params=pltpu.CompilerParams(vmem_limit_bytes=24 * 1024 * 1024),
        cost_estimate=pl.CostEstimate(flops=flops, bytes_accessed=byts, transcendentals=0),
    )(*args)


def dom_bit(i):
    return (lax.axis_index("dom") >> i) & 1


def sent_slots():
    x, z = dom_bit(0), dom_bit(1)
    return x, 1 - x, 2 + z, 3 - z


def read_slots():
    x, z = dom_bit(0), dom_bit(1)
    return 1 - x, x, 3 - z, 2 + z


def target_onehot(targets_ref, rows):
    ids = jnp.concatenate([targets_ref[0, pl.ds(s, 1), :] for s in sent_slots()], 1)
    return (lax.broadcasted_iota(jnp.int32, (rows, ids.shape[1]), 0) == ids).astype(BF16)


def gather_kernel(targets_ref, x_ref, *outs):
    micro, rows, _ = x_ref.shape
    per_peer = outs[0].shape[0] // micro
    onehot = target_onehot(targets_ref, rows)
    for m in range(micro):
        picked = tn_dot(onehot, x_ref[m]).astype(BF16)
        for k, out in enumerate(outs):
            out[m * per_peer : (m + 1) * per_peer, :] = picked[k * per_peer : (k + 1) * per_peer]


def node_kernel(pairs_ref, count_ref, x_ref, values_ref, w_ref, bias_ref, z_ref, acc_ref, src_ref):
    micro, rows, feat = x_ref.shape
    row_blocks = rows // 128
    for m in range(micro):
        z_ref[m * rows : (m + 1) * rows, :] = nn_dot(x_ref[m], w_ref[...]) + bias_ref[
            ...
        ].astype(F32)
        for b in range(row_blocks):
            src_ref[b, :, m * feat : (m + 1) * feat] = x_ref[m, b * 128 : (b + 1) * 128, :]
    acc_ref[...] = jnp.zeros_like(acc_ref)
    for k in range(values_ref.shape[0]):
        src = pairs_ref[1, k]

        @pl.when((k < count_ref[0]) & (src < row_blocks))
        def _():
            acc_ref[pairs_ref[0, k]] += nn_dot(values_ref[k], src_ref[src])


def pieces(part):
    return [slice(r, r + PIECE) for r in range(part.start, part.stop, PIECE)]


def row_mean(v):
    return jnp.mean(v, axis=1, keepdims=True)


def norm_back(g, normed, inv_std, gain):
    e = g * gain
    return (inv_std * (e - row_mean(e) - normed * row_mean(e * normed))).astype(BF16)


def parts_of(total, micro):
    rows = total // micro
    return [slice(m * rows, (m + 1) * rows) for m in range(micro)]


def wide_blocks(part, m, feat):
    cols = slice(m * feat, (m + 1) * feat)
    return [
        (b, slice(part.start + b * 128, part.start + (b + 1) * 128), cols)
        for b in range((part.stop - part.start) // 128)
    ]


def halo_spread(pairs_ref, count_ref, values_ref, gm_ref, t_ref, row_blocks):
    t_ref[...] = jnp.zeros_like(t_ref)
    for k in range(values_ref.shape[0]):
        src = pairs_ref[1, k]

        @pl.when((k < count_ref[0]) & (src >= row_blocks))
        def _():
            t_ref[src - row_blocks] += tn_dot(values_ref[k], gm_ref[pairs_ref[0, k]])


def local_spread(pairs_ref, count_ref, values_ref, gm_ref, t_ref, row_blocks):
    t_ref[...] = jnp.zeros_like(t_ref)
    for k in range(values_ref.shape[0]):
        src = pairs_ref[1, k]

        @pl.when((k < count_ref[0]) & (src < row_blocks))
        def _():
            t_ref[src] += tn_dot(values_ref[k], gm_ref[pairs_ref[0, k]])


def put_halo_grads(t_ref, outs):
    feat = outs[0].shape[1]
    per_peer = outs[0].shape[0] // 2
    for slot, out in zip(read_slots(), outs):
        for m in range(2):
            at = pl.ds(pl.multiple_of(slot * per_peer, per_peer), per_peer)
            out[m * per_peer : (m + 1) * per_peer, :] = t_ref[
                0, at, m * feat : (m + 1) * feat
            ].astype(BF16)


def first_kernel(
    pairs_ref, count_ref, h0, h1, h2, h3, values_ref, z_ref, accin_ref, g_ref, w_agg_ref,
    w_out_ref, gain_ref,
    o0, o1, o2, o3, gm_ref, dact_ref, normed_ref, inv_ref, agg_ref, hidden_ref, gpn_ref,
    gpre_ref, sums_ref,
    src_ref, acc_ref, s0_ref, t_ref,
):
    micro, rows, feat = g_ref.shape
    row_blocks = rows // 128
    per_peer = h0.shape[0] // micro
    for slot, h in zip(read_slots(), (h0, h1, h2, h3)):
        for m in range(micro):
            at = pl.ds(pl.multiple_of(slot * per_peer, per_peer), per_peer)
            src_ref[0, at, m * feat : (m + 1) * feat] = h[m * per_peer : (m + 1) * per_peer, :]
    acc_ref[...] = jnp.zeros_like(acc_ref)
    for k in range(values_ref.shape[0]):
        src = pairs_ref[1, k]

        @pl.when((k < count_ref[0]) & (src >= row_blocks))
        def _():
            acc_ref[pairs_ref[0, k]] += nn_dot(values_ref[k], src_ref[src - row_blocks])

    gain = gain_ref[...].astype(F32)
    parts = parts_of(micro * rows, micro)
    for m, part in enumerate(parts):
        for b, at, cols in wide_blocks(part, m, feat):
            agg_ref[at, :] = (accin_ref[b, :, cols] + acc_ref[b, :, cols]).astype(BF16)
    for part in parts:
        s0_ref[part, :] = nn_dot(agg_ref[part, :], w_agg_ref[...])
    for part in parts:
        for at in pieces(part):
            preact = z_ref[at, :] + s0_ref[at, :]
            sig = 1.0 / (1.0 + jnp.exp(-preact))
            hidden_ref[at, :] = (preact * sig).astype(BF16)
            dact_ref[at, :] = sig * (1.0 + preact * (1.0 - sig))
    for part in parts:
        s0_ref[part, :] = nn_dot(hidden_ref[part, :], w_out_ref[...])
    gain_sum = jnp.zeros((1, feat), F32)
    for m, part in enumerate(parts):
        for at in pieces(part):
            output = s0_ref[at, :]
            centred = output - row_mean(output)
            inv_std = lax.rsqrt(row_mean(centred * centred) + EPSILON)
            normed = centred * inv_std
            normed_ref[at, :] = normed
            inv_ref[at, :] = jnp.broadcast_to(inv_std, (PIECE, 128))
            g = g_ref[m, at.start - part.start : at.stop - part.start, :].astype(F32)
            gpn_ref[at, :] = norm_back(g, normed, inv_std, gain)
            gain_sum += jnp.sum(g * normed, axis=0, keepdims=True)
    for part in parts:
        s0_ref[part, :] = nt_dot(gpn_ref[part, :], w_out_ref[...])
    bias_sum = jnp.zeros((1, feat), F32)
    for part in parts:
        for at in pieces(part):
            gpre = (s0_ref[at, :] * dact_ref[at, :]).astype(BF16)
            gpre_ref[at, :] = gpre
            bias_sum += jnp.sum(gpre.astype(F32), axis=0, keepdims=True)
    for m, part in enumerate(parts):
        gm = nt_dot(gpre_ref[part, :], w_agg_ref[...]).astype(BF16)
        for b, at, cols in wide_blocks(part, m, feat):
            gm_ref[b, :, cols] = gm[b * 128 : (b + 1) * 128]
    halo_spread(pairs_ref, count_ref, values_ref, gm_ref, t_ref, row_blocks)
    put_halo_grads(t_ref, (o0, o1, o2, o3))
    sums_ref[0:1, :] = bias_sum
    sums_ref[1:2, :] = gain_sum


def cpart_kernel(pairs_ref, count_ref, g_ref, gpre_ref, gm_ref, values_ref, w_node_ref, cpart_ref, t_ref):
    micro, rows, feat = g_ref.shape
    local_spread(pairs_ref, count_ref, values_ref, gm_ref, t_ref, rows // 128)
    for m, part in enumerate(parts_of(micro * rows, micro)):
        back = nt_dot(gpre_ref[part, :], w_node_ref[...])
        for b, at, cols in wide_blocks(part, m, feat):
            here = slice(b * 128, (b + 1) * 128)
            cpart_ref[at, :] = g_ref[m, here, :].astype(F32) + back[here] + t_ref[b, :, cols]


def order_of(bit, chunks):
    step = 1 << bit
    low = [d for d in range(chunks) if not d & step]
    mine = dom_bit(bit)
    return [d + mine * step for d in low] + [d + (1 - mine) * step for d in low]


def turn_kernel(chunks, x_ref, agg_ref, hidden_ref, la_ref, lb_ref, lc_ref, turned_ref):
    micro, rows, feat = x_ref.shape
    share = feat // chunks
    half = share // 2
    na = share + half

    def at(d, n, off=0):
        return pl.ds(pl.multiple_of(d * share + off, half), n)

    for m in range(micro):
        turned_ref[:, m * rows : (m + 1) * rows] = x_ref[m].T
    for i, d in enumerate(order_of(0, chunks)):
        la_ref[i * na : i * na + share, :] = turned_ref[at(d, share), :]
    turned_ref[...] = agg_ref[...].T
    for i, d in enumerate(order_of(0, chunks)):
        la_ref[i * na + share : (i + 1) * na, :] = turned_ref[at(d, half), :]
    for i, d in enumerate(order_of(1, chunks)):
        lb_ref[i * half : (i + 1) * half, :] = turned_ref[at(d, half, half), :]
    turned_ref[...] = hidden_ref[...].T
    for i, d in enumerate(order_of(1, chunks)):
        lc_ref[i * share : (i + 1) * share, :] = turned_ref[at(d, share), :]


def second_kernel(
    targets_ref, r0, r1, r2, r3, cin_ref, dact_ref, normed_ref, inv_ref, gpn1_ref, gpre1_ref,
    sums1_ref, w_out_ref, gain_ref, *rest,
):
    weights = len(rest) > 6
    if weights:
        la_ref, lb_ref, lc_ref = rest[:3]
        keep_a, keep_b, send_a, send_b = rest[3:7]
        rest = rest[7:]
    g_ref, gpn_ref, gpre_ref, sums_ref, onehot_ref, s0_ref = rest[-6:]
    total, feat = dact_ref.shape
    parts = parts_of(total, 2)
    rows = total // 2
    per_peer = r0.shape[0] // 2
    onehot_ref[...] = target_onehot(targets_ref, rows)
    gain = gain_ref[...].astype(F32)
    is_last = lax.axis_index("segment") == 1
    for m, part in enumerate(parts):
        ret = jnp.concatenate([r[m * per_peer : (m + 1) * per_peer, :] for r in (r0, r1, r2, r3)], 0)
        s0_ref[part, :] = nn_dot(onehot_ref[...], ret)
    gain_sum = jnp.zeros((1, feat), F32)
    for part in parts:
        for at in pieces(part):
            g16 = (cin_ref[at, :] + s0_ref[at, :]).astype(BF16)
            g_ref[at, :] = g16
            g = g16.astype(F32)
            normed = normed_ref[at, :]
            gpn = norm_back(g, normed, inv_ref[at, 0:1], gain)
            gpn_ref[at, :] = jnp.where(is_last, gpn1_ref[at, :], gpn)
            gain_sum += jnp.sum(g * normed, axis=0, keepdims=True)
    for part in parts:
        s0_ref[part, :] = nt_dot(gpn_ref[part, :], w_out_ref[...])
    bias_sum = jnp.zeros((1, feat), F32)
    for part in parts:
        for at in pieces(part):
            gpre = (s0_ref[at, :] * dact_ref[at, :]).astype(BF16)
            gpre = jnp.where(is_last, gpre1_ref[at, :], gpre)
            gpre_ref[at, :] = gpre
            bias_sum += jnp.sum(gpre.astype(F32), axis=0, keepdims=True)
    gain_sum = jnp.where(is_last, sums1_ref[1:2, :], gain_sum)
    sums = jnp.concatenate([bias_sum, gain_sum, jnp.zeros((EXTRA - 2, feat), F32)], 0)
    sums_ref[...] = sums
    if not weights:
        return
    n = keep_a.shape[0]
    na, nb = keep_a.shape[1], keep_b.shape[1]
    half = lb_ref.shape[0] // (2 * n)
    share = 2 * half
    mid = n * na
    keep_a[...] = nn_dot(la_ref[:mid, :], gpre_ref[...]).reshape(n, na, feat)
    send_a[...] = nn_dot(la_ref[mid:, :], gpre_ref[...]).astype(BF16)
    for base, fill in (
        (0, lambda i, lo, v: put(keep_b, i, lo, v)),
        (n, lambda i, lo, v: put_flat(send_b, nb, i, lo, v)),
    ):
        b = nn_dot(lb_ref[base * half : (base + n) * half, :], gpre_ref[...])
        c = nn_dot(lc_ref[base * share : (base + n) * share, :], gpn_ref[...])
        for i in range(n):
            fill(i, 0, b[i * half : (i + 1) * half])
            fill(i, half, c[i * share : (i + 1) * share])
            fill(i, half + share, sums)


def put(ref, i, lo, v):
    ref[i, lo : lo + v.shape[0], :] = v.astype(ref.dtype)


def put_flat(ref, n, i, lo, v):
    ref[i * n + lo : i * n + lo + v.shape[0], :] = v.astype(ref.dtype)


def tail_kernel(
    pairs_ref, count_ref, g_ref, gpre_ref, values_ref, w_node_ref, w_agg_ref, o0, o1, o2, o3, cpart_ref,
    gm_ref, t_ref, th_ref,
):
    total, feat = g_ref.shape
    row_blocks = total // 256
    parts = parts_of(total, 2)
    for m, part in enumerate(parts):
        gm = nt_dot(gpre_ref[part, :], w_agg_ref[...]).astype(BF16)
        for b, at, cols in wide_blocks(part, m, feat):
            gm_ref[b, :, cols] = gm[b * 128 : (b + 1) * 128]
    halo_spread(pairs_ref, count_ref, values_ref, gm_ref, th_ref, row_blocks)
    put_halo_grads(th_ref, (o0, o1, o2, o3))
    local_spread(pairs_ref, count_ref, values_ref, gm_ref, t_ref, row_blocks)
    for m, part in enumerate(parts):
        back = nt_dot(gpre_ref[part, :], w_node_ref[...])
        for b, at, cols in wide_blocks(part, m, feat):
            cpart_ref[at, :] = (
                g_ref[at, :].astype(F32) + back[b * 128 : (b + 1) * 128] + t_ref[b, :, cols]
            )


def halve_kernel(bits, riders, keep_a, keep_b, recv_a, recv_b, *rest):
    extra, (keep_a2, keep_b2, send_a2, send_b2) = rest[:riders], rest[riders:]
    jobs = (
        (bits[0], keep_a, recv_a, keep_a2, send_a2, extra[:1]),
        (bits[1], keep_b, recv_b, keep_b2, send_b2, extra[1:]),
    )
    for bit, keep, recv, keep2, send2, ride in jobs:
        n, rows, _ = keep2.shape
        mine = dom_bit(bit)
        for i in range(n):
            d, o = 2 * i + mine, 2 * i + 1 - mine
            at = pl.ds(pl.multiple_of(d * rows, 8), rows)
            keep2[i] = keep[d] + recv[at, :].astype(F32)
            at = pl.ds(pl.multiple_of(o * rows, 8), rows)
            send2[i * rows : (i + 1) * rows, :] = (keep[o] + recv[at, :].astype(F32)).astype(BF16)
        for r in ride:
            send2[n * rows :, :] = r[...]


def last_kernel(keep_a, keep_b, recv_a, recv_b, node_ref, agg_ref, out_ref, bias_ref, gain_ref):
    share = node_ref.shape[0]
    half = share // 2
    a = keep_a[0] + recv_a[...].astype(F32)
    b = keep_b[0] + recv_b[...].astype(F32)
    node_ref[...] = a[0:share]
    agg_ref[0:half, :] = a[share : share + half]
    agg_ref[half:share, :] = b[0:half]
    out_ref[...] = b[half : half + share]
    bias_ref[...] = b[half + share : half + share + 1]
    gain_ref[...] = b[half + share + 1 : half + share + 2]


def cot_kernel(skips, targets_ref, r0, r1, r2, r3, cpart_ref, other_ref, cot_ref):
    micro, rows, feat = cot_ref.shape
    is_last = lax.axis_index("segment") == 1

    @pl.when(is_last)
    def _():
        for m in range(micro):
            cot_ref[m] = other_ref[m * rows : (m + 1) * rows, :]

    @pl.when(jnp.logical_not(is_last))
    def _():
        onehot = target_onehot(targets_ref, rows)
        n = onehot.shape[1] // PEERS
        for m in range(micro):
            ret = jnp.concatenate(
                [r[s + m * n : s + (m + 1) * n, :] for r, s in zip((r0, r1, r2, r3), skips)], 0
            )
            cot_ref[m] = (cpart_ref[m * rows : (m + 1) * rows, :] + nn_dot(onehot, ret)).astype(BF16)


def whole_kernel(x_ref, agg_ref, hidden_ref, gpn_ref, gpre_ref, node_ref, agg_out, out_ref):
    rows = x_ref.shape[1]
    gpre = gpre_ref[...]
    node_ref[...] = tn_dot(x_ref[0], gpre[:rows]) + tn_dot(x_ref[1], gpre[rows:])
    agg_out[...] = tn_dot(agg_ref[...], gpre)
    out_ref[...] = tn_dot(hidden_ref[...], gpn_ref[...])


def body(
    section_inputs,
    out_cot,
    w_node,
    w_agg,
    w_out,
    bias,
    gain,
    send_rows,
    blk_pairs,
    blk_count,
    blk_values,
):
    peers = lax.axis_size("dom")
    assert lax.axis_size("segment") == 2 and peers % 4 == 0
    x = section_inputs[0]
    micro, rows, feat = x.shape
    _, slots, per_peer = send_rows.shape
    assert slots * per_peer == 128 and slots == PEERS and micro == 2
    total = micro * rows
    pairs = blk_pairs[0]
    values = blk_values[0]
    row_blocks = rows // 128
    wide = micro * feat
    w_n, w_a, w_o = w_node[0], w_agg[0], w_out[0]
    matmul = 2 * total * feat * feat
    size = total * feat
    chunk = shape((micro * per_peer, feat), BF16)

    def swap_partner(p, k):
        if k == 0:
            return p ^ 1
        if k == 1:
            return (p + 1 if p & 1 else p - 1) % peers
        up = (p >> 1) & 1
        return (p + 2 if up == (k == 3) else p - 2) % peers

    def swapped(v, k, cores):
        return lax.ppermute(
            v,
            ("dom", "segment"),
            [(2 * p + s, 2 * swap_partner(p, k) + d) for p in range(peers) for s, d in cores],
        )

    def across(v, src, dst):
        return lax.ppermute(
            v, ("dom", "segment"), [(2 * p + src, 2 * p + dst) for p in range(peers)]
        )

    def flipped(v, bit):
        return lax.ppermute(v, "dom", [(p, p ^ (1 << bit)) for p in range(peers)])

    f_full, b_full = shape((total, feat), F32), shape((total, feat), BF16)
    s_sums = shape((EXTRA, feat), F32)
    outgoing = call(gather_kernel, [chunk] * slots, [], matmul // 8, 2 * size, send_rows, x)
    halos = [swapped(v, k, ((0, 0), (1, 1))) for k, v in enumerate(outgoing)]
    z, acc = call(
        node_kernel,
        [f_full, shape((row_blocks, 128, wide), F32)],
        [pltpu.VMEM((row_blocks, 128, wide), BF16)],
        2 * matmul, 8 * size,
        pairs, blk_count, x, values, w_n, bias,
        scalars=2,
    )
    gm_shape = (row_blocks, 128, wide)
    first = call(
        first_kernel,
        [chunk] * slots
        + [shape(gm_shape, BF16), f_full, f_full, shape((total, 128), F32)]
        + [b_full] * 4 + [s_sums],
        [
            pltpu.VMEM((1, 128, wide), BF16),
            pltpu.VMEM(gm_shape, F32),
            pltpu.VMEM((total, feat), F32),
            pltpu.VMEM((1, 128, wide), F32),
        ],
        4 * matmul, 20 * size,
        pairs, blk_count, *halos, values, z, acc, out_cot, w_a, w_o, gain,
        scalars=2,
    )
    to_return = first[:slots]
    gm1, dact, normed, inv_std, agg, hidden, gpn1, gpre1, sums1 = first[slots:]
    returned = [swapped(v, k, ((1, 0),)) for k, v in enumerate(to_return)]
    cpart1 = call(
        cpart_kernel, f_full, [pltpu.VMEM(gm_shape, F32)], matmul, 10 * size,
        pairs, blk_count, out_cot, gpre1, gm1, values, w_n,
        scalars=2,
    )
    c_in = across(cpart1, 1, 0)
    share = feat // peers
    half = share // 2
    na, nb = share + half, share + half + EXTRA
    halving = peers == 8
    turned, second_outs = [], []
    if halving:
        turned = call(
            functools.partial(turn_kernel, peers),
            [shape((8 * na, total), BF16), shape((8 * half, total), BF16), shape((8 * share, total), BF16)],
            [pltpu.VMEM((feat, total), BF16)],
            size, 12 * size,
            x, agg, hidden,
        )
        second_outs = [
            shape((4, na, feat), F32), shape((4, nb, feat), F32),
            shape((4 * na, feat), BF16), shape((4 * nb, feat), BF16),
        ]
    second = call(
        second_kernel,
        second_outs + [b_full, b_full, b_full, s_sums],
        [pltpu.VMEM((rows, slots * per_peer), BF16), pltpu.VMEM((total, feat), F32)],
        4 * matmul, 20 * size,
        send_rows, *returned, c_in, dact, normed, inv_std, gpn1, gpre1, sums1, w_o, gain, *turned,
    )
    g_low, gpn, gpre, sums = second[-4:]
    if halving:
        keep_a, keep_b, send_a, send_b = second[:4]
        recv_a, recv_b = flipped(send_a, 0), flipped(send_b, 1)
    tail = call(
        tail_kernel,
        [chunk] * slots + [f_full],
        [pltpu.VMEM(gm_shape, BF16), pltpu.VMEM(gm_shape, F32), pltpu.VMEM((1, 128, wide), F32)],
        2 * matmul, 12 * size,
        pairs, blk_count, g_low, gpre, values, w_n, w_a,
        scalars=2,
    )
    to_return, cpart0 = tail[:slots], tail[slots]
    other = across(g_low, 0, 1)
    same = ((0, 0),)
    if halving:
        back_b, back_d = swapped(to_return[1], 1, same), swapped(to_return[3], 3, same)
        ride = chunk.shape[0]
        keep_a, keep_b, send_a, send_b = call(
            functools.partial(halve_kernel, (1, 0), 2),
            [
                shape((2, na, feat), F32), shape((2, nb, feat), F32),
                shape((2 * na + ride, feat), BF16), shape((2 * nb + ride, feat), BF16),
            ],
            [], size, 8 * size, keep_a, keep_b, recv_a, recv_b, to_return[2], to_return[0],
        )
        recv_a, recv_b = flipped(send_a, 1), flipped(send_b, 0)
        returned, skips = (recv_b, back_b, recv_a, back_d), (2 * nb, 0, 2 * na, 0)
        keep_a, keep_b, send_a, send_b = call(
            functools.partial(halve_kernel, (2, 2), 0),
            [
                shape((1, na, feat), F32), shape((1, nb, feat), F32),
                shape((na, feat), BF16), shape((nb, feat), BF16),
            ],
            [], size, 4 * size, keep_a, keep_b, recv_a, recv_b,
        )
        recv_a, recv_b = flipped(send_a, 2), flipped(send_b, 2)
        part, row = shape((share, feat), F32), shape((1, feat), F32)
        grad_node, grad_agg, grad_out, grad_bias, grad_gain = call(
            last_kernel, [part, part, part, row, row], [], size, 2 * size,
            keep_a, keep_b, recv_a, recv_b,
        )
    else:
        square = shape((feat, feat), F32)
        full = call(
            whole_kernel, [square] * 3, [], 3 * matmul, 12 * size, x, agg, hidden, gpn, gpre
        )
        grad_node, grad_agg, grad_out = [
            lax.psum_scatter(v, "dom", scatter_dimension=0, tiled=True) for v in full
        ]
        sums = lax.psum(sums, "dom")
        grad_bias, grad_gain = sums[0:1], sums[1:2]
        returned = [swapped(v, k, same) for k, v in enumerate(to_return)]
        skips = (0,) * slots
    cot = call(
        functools.partial(cot_kernel, skips), shape((micro, rows, feat), BF16), [], matmul // 4, 4 * size,
        send_rows, *returned, cpart0, other,
    )
    return (
        cot[None],
        grad_node[None],
        grad_agg[None],
        grad_out[None],
        grad_bias,
        grad_gain,
    )


def solution(mesh):
    placed = (
        P("segment", None, ("grp", "dom"), None),
        P(None, ("grp", "dom"), None),
        P("segment", None, None),
        P("segment", None, None),
        P("segment", None, None),
        P("segment", None),
        P("segment", None),
        P("dom", None, None),
        P("dom", None, None),
        P("dom"),
        P("dom", None, None, None),
    )
    return jax.shard_map(
        body,
        mesh=mesh,
        in_specs=placed,
        out_specs=(
            P("segment", None, ("grp", "dom"), None),
            P("segment", ("grp", "dom"), None),
            P("segment", ("grp", "dom"), None),
            P("segment", ("grp", "dom"), None),
            P("segment", "grp"),
            P("segment", "grp"),
        ),
        check_vma=False,
    )
```

```python
import functools

import jax
import jax.numpy as jnp
from jax import lax
from jax.experimental import pallas as pl
from jax.experimental.pallas import tpu as pltpu
from jax.sharding import PartitionSpec as P

EPSILON = 1e-05
F32 = jnp.float32
BF16 = jnp.bfloat16
VMEM = pl.BlockSpec(memory_space=pltpu.VMEM)
SMEM = pl.BlockSpec(memory_space=pltpu.SMEM)
HBM = pl.BlockSpec(memory_space=pltpu.HBM)
ANY = pl.BlockSpec(memory_space=pl.ANY)
PEERS = 4
EXTRA = 8
PIECE = 64


def nn_dot(a, b):
    return jnp.dot(a, b, preferred_element_type=F32)


def nt_dot(a, b):
    return lax.dot_general(a, b, (((1,), (1,)), ((), ())), preferred_element_type=F32)


def tn_dot(a, b):
    return lax.dot_general(a, b, (((0,), (0,)), ((), ())), preferred_element_type=F32)


def shape(dims, dtype):
    return jax.ShapeDtypeStruct(dims, dtype)


def call(kernel, outs, scratch, flops, byts, *args, scalars=0, raw=0, after=0):
    blocks = len(args) - scalars - raw - after
    args = list(args)
    for i in range(scalars, scalars + raw):
        args[i] = pltpu.with_memory_space_constraint(args[i], pltpu.HBM)
    return pl.pallas_call(
        kernel,
        out_shape=outs,
        in_specs=[SMEM] * scalars + [HBM] * raw + [VMEM] * blocks + [ANY] * after,
        out_specs=jax.tree.map(lambda _: VMEM, outs),
        scratch_shapes=scratch,
        compiler_params=pltpu.CompilerParams(vmem_limit_bytes=24 * 1024 * 1024),
        cost_estimate=pl.CostEstimate(flops=flops, bytes_accessed=byts, transcendentals=0),
    )(*args)


def dom_bit(i):
    return (lax.axis_index("dom") >> i) & 1


def sent_slots():
    x, z = dom_bit(0), dom_bit(1)
    return x, 1 - x, 2 + z, 3 - z


def read_slots():
    x, z = dom_bit(0), dom_bit(1)
    return 1 - x, x, 3 - z, 2 + z


def target_onehot(targets_ref, rows):
    ids = jnp.concatenate([targets_ref[0, pl.ds(s, 1), :] for s in sent_slots()], 1)
    return (lax.broadcasted_iota(jnp.int32, (rows, ids.shape[1]), 0) == ids).astype(BF16)


def gather_kernel(targets_hbm, x_hbm, o0, o1, o2, o3, x_ref, onehot_ref, targets_ref, sems):
    copies = [
        pltpu.make_async_copy(targets_hbm, targets_ref, sems.at[0]),
        pltpu.make_async_copy(x_hbm, x_ref, sems.at[1]),
    ]
    for c in copies:
        c.start()
    micro, rows, _ = x_ref.shape
    per_peer = o0.shape[0] // micro
    copies[0].wait()
    onehot = target_onehot(targets_ref, rows)
    onehot_ref[...] = onehot
    copies[1].wait()
    for m in range(micro):
        picked = tn_dot(onehot, x_ref[m]).astype(BF16)
        for k, out in enumerate((o0, o1, o2, o3)):
            out[m * per_peer : (m + 1) * per_peer, :] = picked[k * per_peer : (k + 1) * per_peer]


def node_kernel(
    pairs_ref, count_ref, values_hbm, w_hbm, bias_hbm, w_agg_hbm, w_out_hbm, gain_hbm, g_hbm, x_ref,
    z_ref, acc_ref, values_ref, turned_ref, w_ref, w_agg_ref, w_out_ref, gain_ref, g_ref,
    src_ref, bias_ref, sems,
):
    copies = [
        pltpu.make_async_copy(a, b, sems.at[i])
        for i, (a, b) in enumerate(
            (
                (values_hbm, values_ref), (w_hbm, w_ref), (bias_hbm, bias_ref),
                (w_agg_hbm, w_agg_ref), (w_out_hbm, w_out_ref), (gain_hbm, gain_ref), (g_hbm, g_ref),
            )
        )
    ]
    for c in copies:
        c.start()
    micro, rows, feat = x_ref.shape
    row_blocks = rows // 128
    for m in range(micro):
        for b in range(row_blocks):
            src_ref[b, :, m * feat : (m + 1) * feat] = x_ref[m, b * 128 : (b + 1) * 128, :]
    acc_ref[...] = jnp.zeros_like(acc_ref)
    copies[0].wait()
    for k in range(values_ref.shape[0]):
        turned_ref[k] = values_ref[k].T
        src = pairs_ref[1, k]

        @pl.when((k < count_ref[0]) & (src < row_blocks))
        def _():
            acc_ref[pairs_ref[0, k]] += nn_dot(values_ref[k], src_ref[src])

    copies[1].wait()
    copies[2].wait()
    for m in range(micro):
        z_ref[m * rows : (m + 1) * rows, :] = nn_dot(x_ref[m], w_ref[...]) + bias_ref[
            ...
        ].astype(F32)
    for c in copies[3:]:
        c.wait()


def pieces(part):
    return [slice(r, r + PIECE) for r in range(part.start, part.stop, PIECE)]


def row_mean(v):
    return jnp.mean(v, axis=1, keepdims=True)


def norm_back(g, normed, inv_std, gain):
    e = g * gain
    return (inv_std * (e - row_mean(e) - normed * row_mean(e * normed))).astype(BF16)


def parts_of(total, micro):
    rows = total // micro
    return [slice(m * rows, (m + 1) * rows) for m in range(micro)]


def wide_blocks(part, m, feat):
    cols = slice(m * feat, (m + 1) * feat)
    return [
        (b, slice(part.start + b * 128, part.start + (b + 1) * 128), cols)
        for b in range((part.stop - part.start) // 128)
    ]


def halo_spread(pairs_ref, count_ref, turned_ref, gm_ref, t_ref, row_blocks):
    t_ref[...] = jnp.zeros_like(t_ref)
    for k in range(turned_ref.shape[0]):
        src = pairs_ref[1, k]

        @pl.when((k < count_ref[0]) & (src >= row_blocks))
        def _():
            t_ref[src - row_blocks] += nn_dot(turned_ref[k], gm_ref[pairs_ref[0, k]])


def local_spread(pairs_ref, count_ref, turned_ref, gm_ref, t_ref, row_blocks):
    t_ref[...] = jnp.zeros_like(t_ref)
    for k in range(turned_ref.shape[0]):
        src = pairs_ref[1, k]

        @pl.when((k < count_ref[0]) & (src < row_blocks))
        def _():
            t_ref[src] += nn_dot(turned_ref[k], gm_ref[pairs_ref[0, k]])


def put_halo_grads(t_ref, outs):
    feat = outs[0].shape[1]
    per_peer = outs[0].shape[0] // 2
    for slot, out in zip(read_slots(), outs):
        for m in range(2):
            at = pl.ds(pl.multiple_of(slot * per_peer, per_peer), per_peer)
            out[m * per_peer : (m + 1) * per_peer, :] = t_ref[
                0, at, m * feat : (m + 1) * feat
            ].astype(BF16)


def first_kernel(
    pairs_ref, count_ref, h0, h1, h2, h3, values_ref, turned_ref, z_ref, accin_ref, g_ref, w_agg_ref,
    w_out_ref, gain_ref,
    o0, o1, o2, o3, gm_ref, dact_ref, normed_ref, inv_ref, agg_ref, hidden_ref, gpn_ref,
    gpre_ref, sums_ref,
    src_ref, acc_ref, s0_ref, t_ref,
):
    micro, rows, feat = g_ref.shape
    row_blocks = rows // 128
    per_peer = h0.shape[0] // micro
    for slot, h in zip(read_slots(), (h0, h1, h2, h3)):
        for m in range(micro):
            at = pl.ds(pl.multiple_of(slot * per_peer, per_peer), per_peer)
            src_ref[0, at, m * feat : (m + 1) * feat] = h[m * per_peer : (m + 1) * per_peer, :]
    acc_ref[...] = jnp.zeros_like(acc_ref)
    for k in range(values_ref.shape[0]):
        src = pairs_ref[1, k]

        @pl.when((k < count_ref[0]) & (src >= row_blocks))
        def _():
            acc_ref[pairs_ref[0, k]] += nn_dot(values_ref[k], src_ref[src - row_blocks])

    gain = gain_ref[...].astype(F32)
    parts = parts_of(micro * rows, micro)
    for m, part in enumerate(parts):
        for b, at, cols in wide_blocks(part, m, feat):
            agg_ref[at, :] = (accin_ref[b, :, cols] + acc_ref[b, :, cols]).astype(BF16)
    for part in parts:
        s0_ref[part, :] = nn_dot(agg_ref[part, :], w_agg_ref[...])
    for part in parts:
        for at in pieces(part):
            preact = z_ref[at, :] + s0_ref[at, :]
            sig = 1.0 / (1.0 + jnp.exp(-preact))
            hidden_ref[at, :] = (preact * sig).astype(BF16)
            dact_ref[at, :] = sig * (1.0 + preact * (1.0 - sig))
    for part in parts:
        s0_ref[part, :] = nn_dot(hidden_ref[part, :], w_out_ref[...])
    gain_sum = jnp.zeros((1, feat), F32)
    for m, part in enumerate(parts):
        for at in pieces(part):
            output = s0_ref[at, :]
            centred = output - row_mean(output)
            inv_std = lax.rsqrt(row_mean(centred * centred) + EPSILON)
            normed = centred * inv_std
            normed_ref[at, :] = normed
            inv_ref[at, :] = jnp.broadcast_to(inv_std, (PIECE, 128))
            g = g_ref[m, at.start - part.start : at.stop - part.start, :].astype(F32)
            gpn_ref[at, :] = norm_back(g, normed, inv_std, gain)
            gain_sum += jnp.sum(g * normed, axis=0, keepdims=True)
    for part in parts:
        s0_ref[part, :] = nt_dot(gpn_ref[part, :], w_out_ref[...])
    bias_sum = jnp.zeros((1, feat), F32)
    for part in parts:
        for at in pieces(part):
            gpre = (s0_ref[at, :] * dact_ref[at, :]).astype(BF16)
            gpre_ref[at, :] = gpre
            bias_sum += jnp.sum(gpre.astype(F32), axis=0, keepdims=True)
    for m, part in enumerate(parts):
        gm = nt_dot(gpre_ref[part, :], w_agg_ref[...]).astype(BF16)
        for b, at, cols in wide_blocks(part, m, feat):
            gm_ref[b, :, cols] = gm[b * 128 : (b + 1) * 128]
    halo_spread(pairs_ref, count_ref, turned_ref, gm_ref, t_ref, row_blocks)
    put_halo_grads(t_ref, (o0, o1, o2, o3))
    sums_ref[0:1, :] = bias_sum
    sums_ref[1:2, :] = gain_sum


def cpart_kernel(pairs_ref, count_ref, g_ref, gpre_ref, gm_ref, turned_ref, w_node_ref, cpart_ref, t_ref):
    total, feat = cpart_ref.shape
    local_spread(pairs_ref, count_ref, turned_ref, gm_ref, t_ref, total // 256)
    for m, part in enumerate(parts_of(total, 2)):
        back = nt_dot(gpre_ref[part, :], w_node_ref[...])
        for b, at, cols in wide_blocks(part, m, feat):
            here = slice(b * 128, (b + 1) * 128)
            g = g_ref[m, here, :] if len(g_ref.shape) == 3 else g_ref[at, :]
            cpart_ref[at, :] = g.astype(F32) + back[here] + t_ref[b, :, cols]


def order_of(bit, chunks):
    step = 1 << bit
    low = [d for d in range(chunks) if not d & step]
    mine = dom_bit(bit)
    return [d + mine * step for d in low] + [d + (1 - mine) * step for d in low]


def turn_kernel(chunks, x_ref, agg_ref, hidden_ref, la_ref, lb_ref, lc_ref, turned_ref):
    micro, rows, feat = x_ref.shape
    share = feat // chunks
    half = share // 2
    na = share + half

    def at(d, n, off=0):
        return pl.ds(pl.multiple_of(d * share + off, half), n)

    for m in range(micro):
        turned_ref[:, m * rows : (m + 1) * rows] = x_ref[m].T
    for i, d in enumerate(order_of(0, chunks)):
        la_ref[i * na : i * na + share, :] = turned_ref[at(d, share), :]
    turned_ref[...] = agg_ref[...].T
    for i, d in enumerate(order_of(0, chunks)):
        la_ref[i * na + share : (i + 1) * na, :] = turned_ref[at(d, half), :]
    for i, d in enumerate(order_of(1, chunks)):
        lb_ref[i * half : (i + 1) * half, :] = turned_ref[at(d, half, half), :]
    turned_ref[...] = hidden_ref[...].T
    for i, d in enumerate(order_of(1, chunks)):
        lc_ref[i * share : (i + 1) * share, :] = turned_ref[at(d, share), :]


def second_kernel(
    pairs_ref, count_ref, onehot_ref, r0, r1, r2, r3, cin_ref, dact_ref, normed_ref, inv_ref, gpn1_ref,
    gpre1_ref, sums1_ref, turned_ref, w_agg_ref, w_out_ref, gain_ref, *rest,
):
    weights = len(rest) > 11
    if weights:
        la_ref, lb_ref, lc_ref = rest[:3]
        keep_a, keep_b, send_a, send_b = rest[3:7]
        rest = rest[7:]
    if weights:
        far_ref, *rest = rest
    else:
        o0, o1, o2, o3, *rest = rest
    g_ref, gpn_ref, gpre_ref, gm_ref, sums_ref, s0_ref, t_ref = rest
    total, feat = dact_ref.shape
    parts = parts_of(total, 2)
    rows = total // 2
    per_peer = r0.shape[0] // 2
    gain = gain_ref[...].astype(F32)
    is_last = lax.axis_index("segment") == 1
    for m, part in enumerate(parts):
        ret = jnp.concatenate([r[m * per_peer : (m + 1) * per_peer, :] for r in (r0, r1, r2, r3)], 0)
        s0_ref[part, :] = nn_dot(onehot_ref[...], ret)
    gain_sum = jnp.zeros((1, feat), F32)
    for part in parts:
        for at in pieces(part):
            g16 = (cin_ref[at, :] + s0_ref[at, :]).astype(BF16)
            g_ref[at, :] = g16
            g = g16.astype(F32)
            normed = normed_ref[at, :]
            gpn = norm_back(g, normed, inv_ref[at, 0:1], gain)
            gpn_ref[at, :] = jnp.where(is_last, gpn1_ref[at, :], gpn)
            gain_sum += jnp.sum(g * normed, axis=0, keepdims=True)
    for part in parts:
        s0_ref[part, :] = nt_dot(gpn_ref[part, :], w_out_ref[...])
    bias_sum = jnp.zeros((1, feat), F32)
    for part in parts:
        for at in pieces(part):
            gpre = (s0_ref[at, :] * dact_ref[at, :]).astype(BF16)
            gpre = jnp.where(is_last, gpre1_ref[at, :], gpre)
            gpre_ref[at, :] = gpre
            bias_sum += jnp.sum(gpre.astype(F32), axis=0, keepdims=True)
    gain_sum = jnp.where(is_last, sums1_ref[1:2, :], gain_sum)
    sums = jnp.concatenate([bias_sum, gain_sum, jnp.zeros((EXTRA - 2, feat), F32)], 0)
    sums_ref[...] = sums
    for m, part in enumerate(parts):
        gm = nt_dot(gpre_ref[part, :], w_agg_ref[...]).astype(BF16)
        for b, at, cols in wide_blocks(part, m, feat):
            gm_ref[b, :, cols] = gm[b * 128 : (b + 1) * 128]
    halo_spread(pairs_ref, count_ref, turned_ref, gm_ref, t_ref, rows // 128)
    if not weights:
        put_halo_grads(t_ref, (o0, o1, o2, o3))
        return
    n = keep_a.shape[0]
    na, nb = keep_a.shape[1], keep_b.shape[1]
    half = lb_ref.shape[0] // (2 * n)
    share = 2 * half
    ride = 2 * per_peer
    at_a, at_b = n * na, n * nb
    put_halo_grads(
        t_ref,
        (
            send_a.at[pl.ds(at_a, ride), :], send_a.at[pl.ds(at_a + ride, ride), :],
            send_b.at[pl.ds(at_b, ride), :], far_ref,
        ),
    )
    send_b[at_b + ride :, :] = send_a[at_a + ride :, :]
    mid = n * na
    keep_a[...] = nn_dot(la_ref[:mid, :], gpre_ref[...]).reshape(n, na, feat)
    send_a[:mid, :] = nn_dot(la_ref[mid:, :], gpre_ref[...]).astype(BF16)
    for base, fill in (
        (0, lambda i, lo, v: put(keep_b, i, lo, v)),
        (n, lambda i, lo, v: put_flat(send_b, nb, i, lo, v)),
    ):
        b = nn_dot(lb_ref[base * half : (base + n) * half, :], gpre_ref[...])
        c = nn_dot(lc_ref[base * share : (base + n) * share, :], gpn_ref[...])
        for i in range(n):
            fill(i, 0, b[i * half : (i + 1) * half])
            fill(i, half, c[i * share : (i + 1) * share])
            fill(i, half + share, sums)


def put(ref, i, lo, v):
    ref[i, lo : lo + v.shape[0], :] = v.astype(ref.dtype)


def put_flat(ref, n, i, lo, v):
    ref[i * n + lo : i * n + lo + v.shape[0], :] = v.astype(ref.dtype)


def halve_kernel(bits, keep_a, keep_b, recv_a, recv_b, *rest):
    keep_a2, keep_b2, send_a2, send_b2 = rest[-4:]
    for bit, keep, recv, keep2, send2 in (
        (bits[0], keep_a, recv_a, keep_a2, send_a2),
        (bits[1], keep_b, recv_b, keep_b2, send_b2),
    ):
        n, rows, _ = keep2.shape
        mine = dom_bit(bit)
        for i in range(n):
            d, o = 2 * i + mine, 2 * i + 1 - mine
            at = pl.ds(pl.multiple_of(o * rows, 8), rows)
            send2[i * rows : (i + 1) * rows, :] = (keep[o] + recv[at, :].astype(F32)).astype(BF16)
            at = pl.ds(pl.multiple_of(d * rows, 8), rows)
            keep2[i] = keep[d] + recv[at, :].astype(F32)
        carried = send2.shape[0] - n * rows
        if carried:
            send2[n * rows :, :] = recv[recv.shape[0] - carried :, :]


def join_kernel(far_ref, recv_ref, out_ref):
    n = far_ref.shape[0]
    out_ref[:n, :] = far_ref[...]
    out_ref[n:, :] = recv_ref[recv_ref.shape[0] - n :, :]


def last_kernel(keep_a, keep_b, recv_a, recv_b, node_ref, agg_ref, out_ref, bias_ref, gain_ref):
    share = node_ref.shape[0]
    half = share // 2
    a = keep_a[0] + recv_a[...].astype(F32)
    b = keep_b[0] + recv_b[...].astype(F32)
    node_ref[...] = a[0:share]
    agg_ref[0:half, :] = a[share : share + half]
    agg_ref[half:share, :] = b[0:half]
    out_ref[...] = b[half : half + share]
    bias_ref[...] = b[half + share : half + share + 1]
    gain_ref[...] = b[half + share + 1 : half + share + 2]


def cot_kernel(skips, onehot_ref, *rest):
    *sources, cpart_ref, other_ref, cot_ref = rest
    micro, rows, feat = cot_ref.shape
    is_last = lax.axis_index("segment") == 1
    n = onehot_ref.shape[1] // PEERS
    near = dom_bit(0) != dom_bit(1)

    @pl.when(is_last)
    def _():
        for m in range(micro):
            cot_ref[m] = other_ref[m * rows : (m + 1) * rows, :]

    @pl.when(jnp.logical_not(is_last))
    def _():
        for m in range(micro):
            got = [r[s + m * n : s + (m + 1) * n, :] for r, s in zip(sources, skips)]
            if len(got) > PEERS:
                got[1] = jnp.where(near, got[1], got.pop())
            ret = jnp.concatenate(got, 0)
            cot_ref[m] = (
                cpart_ref[m * rows : (m + 1) * rows, :] + nn_dot(onehot_ref[...], ret)
            ).astype(BF16)


def whole_kernel(x_ref, agg_ref, hidden_ref, gpn_ref, gpre_ref, node_ref, agg_out, out_ref):
    rows = x_ref.shape[1]
    gpre = gpre_ref[...]
    node_ref[...] = tn_dot(x_ref[0], gpre[:rows]) + tn_dot(x_ref[1], gpre[rows:])
    agg_out[...] = tn_dot(agg_ref[...], gpre)
    out_ref[...] = tn_dot(hidden_ref[...], gpn_ref[...])


def body(
    section_inputs,
    out_cot,
    w_node,
    w_agg,
    w_out,
    bias,
    gain,
    send_rows,
    blk_pairs,
    blk_count,
    blk_values,
):
    peers = lax.axis_size("dom")
    assert lax.axis_size("segment") == 2 and peers % 4 == 0
    x = section_inputs[0]
    micro, rows, feat = x.shape
    _, slots, per_peer = send_rows.shape
    assert slots * per_peer == 128 and slots == PEERS and micro == 2
    total = micro * rows
    pairs = blk_pairs[0]
    values = blk_values[0]
    row_blocks = rows // 128
    wide = micro * feat
    w_n, w_a, w_o = w_node[0], w_agg[0], w_out[0]
    matmul = 2 * total * feat * feat
    size = total * feat
    chunk = shape((micro * per_peer, feat), BF16)

    def swap_partner(p, k):
        if k == 0:
            return p ^ 1
        if k == 1:
            return (p + 1 if p & 1 else p - 1) % peers
        up = (p >> 1) & 1
        return (p + 2 if up == (k == 3) else p - 2) % peers

    def swapped(v, k, cores):
        return lax.ppermute(
            v,
            ("dom", "segment"),
            [(2 * p + s, 2 * swap_partner(p, k) + d) for p in range(peers) for s, d in cores],
        )

    def across(v):
        return lax.ppermute(v, "segment", [(0, 1), (1, 0)])

    def flipped(v, bit):
        return lax.ppermute(v, "dom", [(p, p ^ (1 << bit)) for p in range(peers)])

    f_full, b_full = shape((total, feat), F32), shape((total, feat), BF16)
    s_sums = shape((EXTRA, feat), F32)
    dma = pltpu.SemaphoreType.DMA
    *outgoing, x, onehot = call(
        gather_kernel,
        [chunk] * slots + [shape(x.shape, BF16), shape((rows, slots * per_peer), BF16)],
        [pltpu.VMEM(send_rows.shape, jnp.int32), dma((2,))],
        matmul // 8, 2 * size, send_rows, x,
        raw=2,
    )
    same, other_core = ((0, 0), (1, 1)), ((0, 1), (1, 0))
    w_other = across(w_n)
    halos = [swapped(v, k, same) for k, v in enumerate(outgoing)]
    gm_shape = (row_blocks, 128, wide)
    loaded = (values, values, w_n, w_a, w_o, gain, out_cot)
    z, acc, values, turned_values, w_n, w_a, w_o, gain, g_last = call(
        node_kernel,
        [f_full, shape(gm_shape, F32)] + [shape(v.shape, BF16) for v in loaded],
        [pltpu.VMEM(gm_shape, BF16), pltpu.VMEM(bias.shape, BF16), dma((7,))],
        2 * matmul, 8 * size,
        pairs, blk_count, values, w_n, bias, w_a, w_o, gain, out_cot, x,
        scalars=2, raw=7,
    )
    first = call(
        first_kernel,
        [chunk] * slots
        + [shape(gm_shape, BF16), f_full, f_full, shape((total, 128), F32)]
        + [b_full] * 4 + [s_sums],
        [
            pltpu.VMEM((1, 128, wide), BF16),
            pltpu.VMEM(gm_shape, F32),
            pltpu.VMEM((total, feat), F32),
            pltpu.VMEM((1, 128, wide), F32),
        ],
        4 * matmul, 20 * size,
        pairs, blk_count, *halos, values, turned_values, z, acc, g_last, w_a, w_o, gain,
        scalars=2,
    )
    to_return = first[:slots]
    gm1, dact, normed, inv_std, agg, hidden, gpn1, gpre1, sums1 = first[slots:]
    returned = [swapped(v, k, other_core) for k, v in enumerate(to_return)]
    c_in = call(
        cpart_kernel, f_full, [pltpu.VMEM(gm_shape, F32)], matmul, 10 * size,
        pairs, blk_count, g_last, across(gpre1), across(gm1), turned_values, w_other,
        scalars=2,
    )
    share = feat // peers
    half = share // 2
    na, nb = share + half, share + half + EXTRA
    halving = peers == 8
    turned, second_outs = [], [chunk] * slots
    ride = chunk.shape[0]
    if halving:
        turned = call(
            functools.partial(turn_kernel, peers),
            [shape((8 * na, total), BF16), shape((8 * half, total), BF16), shape((8 * share, total), BF16)],
            [pltpu.VMEM((feat, total), BF16)],
            size, 12 * size,
            x, agg, hidden,
        )
        second_outs = [
            shape((4, na, feat), F32), shape((4, nb, feat), F32),
            shape((4 * na + 2 * ride, feat), BF16), shape((4 * nb + 2 * ride, feat), BF16),
            chunk,
        ]
    second = call(
        second_kernel,
        second_outs + [b_full, b_full, b_full, shape(gm_shape, BF16), s_sums],
        [pltpu.VMEM((total, feat), F32), pltpu.VMEM((1, 128, wide), F32)],
        5 * matmul, 20 * size,
        pairs, blk_count, onehot, *returned, c_in, dact, normed, inv_std, gpn1, gpre1, sums1,
        turned_values, w_a, w_o, gain, *turned,
        scalars=2,
    )
    g_low, gpn, gpre, gm, sums = second[-5:]
    if halving:
        keep_a, keep_b, send_a, send_b, far = second[:5]
        recv_a, recv_b = flipped(send_a, 0), flipped(send_b, 1)
    cpart0 = call(
        cpart_kernel, f_full, [pltpu.VMEM(gm_shape, F32)], matmul, 10 * size,
        pairs, blk_count, g_low, gpre, gm, turned_values, w_n,
        scalars=2,
    )
    other = across(g_low)
    cot_out = shape((micro, rows, feat), BF16)
    if halving:
        back_a, back_c = recv_a, recv_b
        far = call(join_kernel, shape((2 * ride, feat), BF16), [], size, size // 4, far, recv_a)
        keep_a, keep_b, send_a, send_b = call(
            functools.partial(halve_kernel, (1, 0)),
            [
                shape((2, na, feat), F32), shape((2, nb, feat), F32),
                shape((2 * na, feat), BF16), shape((2 * nb + ride, feat), BF16),
            ],
            [], size, 8 * size, keep_a, keep_b, recv_a, recv_b,
        )
        recv_a, recv_b = flipped(send_a, 1), flipped(send_b, 0)
        far = swapped(far, 3, same)
        cot = call(
            functools.partial(cot_kernel, (4 * na, 2 * nb, 4 * nb, 0, ride)),
            cot_out, [], matmul // 4, 4 * size,
            onehot, back_a, recv_b, back_c, far, far, cpart0, other,
        )
        keep_a, keep_b, send_a, send_b = call(
            functools.partial(halve_kernel, (2, 2)),
            [
                shape((1, na, feat), F32), shape((1, nb, feat), F32),
                shape((na, feat), BF16), shape((nb, feat), BF16),
            ],
            [], size, 4 * size, keep_a, keep_b, recv_a, recv_b, cot,
            after=1,
        )
        recv_a, recv_b = flipped(send_a, 2), flipped(send_b, 2)
        part, row = shape((share, feat), F32), shape((1, feat), F32)
        grad_node, grad_agg, grad_out, grad_bias, grad_gain = call(
            last_kernel, [part, part, part, row, row], [], size, 2 * size,
            keep_a, keep_b, recv_a, recv_b,
        )
    else:
        square = shape((feat, feat), F32)
        full = call(
            whole_kernel, [square] * 3, [], 3 * matmul, 12 * size, x, agg, hidden, gpn, gpre
        )
        grad_node, grad_agg, grad_out = [
            lax.psum_scatter(v, "dom", scatter_dimension=0, tiled=True) for v in full
        ]
        sums = lax.psum(sums, "dom")
        grad_bias, grad_gain = sums[0:1], sums[1:2]
        returned = [swapped(v, k, same) for k, v in enumerate(second[:slots])]
        cot = call(
            functools.partial(cot_kernel, (0,) * slots), cot_out, [], matmul // 4, 4 * size,
            onehot, *returned, cpart0, other,
        )
    return (
        cot[None],
        grad_node[None],
        grad_agg[None],
        grad_out[None],
        grad_bias,
        grad_gain,
    )


def solution(mesh):
    placed = (
        P("segment", None, ("grp", "dom"), None),
        P(None, ("grp", "dom"), None),
        P("segment", None, None),
        P("segment", None, None),
        P("segment", None, None),
        P("segment", None),
        P("segment", None),
        P("dom", None, None),
        P("dom", None, None),
        P("dom"),
        P("dom", None, None, None),
    )
    return jax.shard_map(
        body,
        mesh=mesh,
        in_specs=placed,
        out_specs=(
            P("segment", None, ("grp", "dom"), None),
            P("segment", ("grp", "dom"), None),
            P("segment", ("grp", "dom"), None),
            P("segment", ("grp", "dom"), None),
            P("segment", "grp"),
            P("segment", "grp"),
        ),
        check_vma=False,
    )
```

```python
import functools

import jax
import jax.numpy as jnp
from jax import lax
from jax.experimental import pallas as pl
from jax.experimental.pallas import tpu as pltpu
from jax.sharding import PartitionSpec as P

EPSILON = 1e-05
F32 = jnp.float32
BF16 = jnp.bfloat16
VMEM = pl.BlockSpec(memory_space=pltpu.VMEM)
SMEM = pl.BlockSpec(memory_space=pltpu.SMEM)
HBM = pl.BlockSpec(memory_space=pltpu.HBM)
ANY = pl.BlockSpec(memory_space=pl.ANY)
PEERS = 4
EXTRA = 8
PIECE = 64


def nn_dot(a, b):
    return jnp.dot(a, b, preferred_element_type=F32)


def nt_dot(a, b):
    return lax.dot_general(a, b, (((1,), (1,)), ((), ())), preferred_element_type=F32)


def tn_dot(a, b):
    return lax.dot_general(a, b, (((0,), (0,)), ((), ())), preferred_element_type=F32)


def shape(dims, dtype):
    return jax.ShapeDtypeStruct(dims, dtype)


def call(kernel, outs, scratch, flops, byts, *args, scalars=0, raw=0, after=0):
    blocks = len(args) - scalars - raw - after
    args = list(args)
    for i in range(scalars, scalars + raw):
        args[i] = pltpu.with_memory_space_constraint(args[i], pltpu.HBM)
    return pl.pallas_call(
        kernel,
        out_shape=outs,
        in_specs=[SMEM] * scalars + [HBM] * raw + [VMEM] * blocks + [ANY] * after,
        out_specs=jax.tree.map(lambda _: VMEM, outs),
        scratch_shapes=scratch,
        compiler_params=pltpu.CompilerParams(vmem_limit_bytes=24 * 1024 * 1024),
        cost_estimate=pl.CostEstimate(flops=flops, bytes_accessed=byts, transcendentals=0),
    )(*args)


def on_core(core):
    return pl.when(lax.axis_index("segment") == core)


def two_dot(pair_ref, b):
    return nn_dot(pair_ref[0], b) + nn_dot(pair_ref[1], b)


def dom_bit(i):
    return (lax.axis_index("dom") >> i) & 1


def sent_slots():
    x, z = dom_bit(0), dom_bit(1)
    return x, 1 - x, 2 + z, 3 - z


def read_slots():
    x, z = dom_bit(0), dom_bit(1)
    return 1 - x, x, 3 - z, 2 + z


def target_onehot(targets_ref, rows):
    ids = jnp.concatenate([targets_ref[0, pl.ds(s, 1), :] for s in sent_slots()], 1)
    return (lax.broadcasted_iota(jnp.int32, (rows, ids.shape[1]), 0) == ids).astype(BF16)


def gather_kernel(targets_hbm, x_hbm, o0, o1, o2, o3, x_ref, onehot_ref, targets_ref, sems):
    copies = [
        pltpu.make_async_copy(targets_hbm, targets_ref, sems.at[0]),
        pltpu.make_async_copy(x_hbm, x_ref, sems.at[1]),
    ]
    for c in copies:
        c.start()
    micro, rows, _ = x_ref.shape
    per_peer = o0.shape[0] // micro
    copies[0].wait()
    onehot = target_onehot(targets_ref, rows)
    onehot_ref[...] = onehot
    copies[1].wait()
    for m in range(micro):
        picked = tn_dot(onehot, x_ref[m]).astype(BF16)
        for k, out in enumerate((o0, o1, o2, o3)):
            out[m * per_peer : (m + 1) * per_peer, :] = picked[k * per_peer : (k + 1) * per_peer]


def node_kernel(
    pairs_ref, count_ref, values_hbm, w_hbm, bias_hbm, w_agg_hbm, w_out_hbm, gain_hbm, g_hbm, x_ref,
    z_ref, acc_ref, halo_in_ref, local_back_ref, halo_back_ref, w_ref, w_agg_ref, w_out_ref, gain_ref,
    g_ref,
    values_ref, src_ref, bias_ref, dense_ref, local_ref, sems,
):
    copies = [
        pltpu.make_async_copy(a, b, sems.at[i])
        for i, (a, b) in enumerate(
            (
                (values_hbm, values_ref), (w_hbm, w_ref), (bias_hbm, bias_ref),
                (w_agg_hbm, w_agg_ref), (w_out_hbm, w_out_ref), (gain_hbm, gain_ref), (g_hbm, g_ref),
            )
        )
    ]
    for c in copies:
        c.start()
    micro, rows, feat = x_ref.shape
    row_blocks, blocks = dense_ref.shape[:2]
    for m in range(micro):
        src_ref[:, m * feat : (m + 1) * feat] = x_ref[m]
    dense_ref[...] = jnp.zeros_like(dense_ref)
    copies[0].wait()
    for k in range(values_ref.shape[0]):

        @pl.when(k < count_ref[0])
        def _():
            dense_ref[pairs_ref[0, 0, k], pairs_ref[0, 1, k]] += values_ref[k].astype(F32)

    copies[1].wait()
    copies[2].wait()
    for m in range(micro):
        z_ref[m * rows : (m + 1) * rows, :] = nn_dot(x_ref[m], w_ref[...]) + bias_ref[
            ...
        ].astype(F32)
    for d in range(row_blocks):
        down = slice(d * 128, (d + 1) * 128)
        for c in range(blocks):
            block = dense_ref[d, c]
            high = block.astype(BF16)
            for i, v in enumerate((high, (block - high.astype(F32)).astype(BF16))):
                if c < row_blocks:
                    across_to = slice(c * 128, (c + 1) * 128)
                    local_ref[i, down, across_to] = v
                    local_back_ref[i, across_to, down] = v.T
                else:
                    halo_in_ref[i, down, :] = v
                    halo_back_ref[i, :, down] = v.T
    acc_ref[...] = two_dot(local_ref, src_ref[...])
    for c in copies[3:]:
        c.wait()


def pieces(part):
    return [slice(r, r + PIECE) for r in range(part.start, part.stop, PIECE)]


def row_mean(v):
    return jnp.mean(v, axis=1, keepdims=True)


def norm_back(g, normed, inv_std, gain):
    e = g * gain
    return (inv_std * (e - row_mean(e) - normed * row_mean(e * normed))).astype(BF16)


def parts_of(total, micro):
    rows = total // micro
    return [slice(m * rows, (m + 1) * rows) for m in range(micro)]


def put_halo_grads(t_ref, outs):
    feat = outs[0].shape[1]
    per_peer = outs[0].shape[0] // 2
    for slot, out in zip(read_slots(), outs):
        for m in range(2):
            at = pl.ds(pl.multiple_of(slot * per_peer, per_peer), per_peer)
            out[m * per_peer : (m + 1) * per_peer, :] = t_ref[
                at, m * feat : (m + 1) * feat
            ].astype(BF16)


def first_kernel(
    h0, h1, h2, h3, halo_in_ref, halo_back_ref, z_ref, acc_ref, g_ref, w_agg_ref, w_out_ref, gain_ref, _,
    o0, o1, o2, o3, both_ref, dact_ref, normed_ref, inv_ref, agg_ref, hidden_ref, gpn_ref,
    gpre_ref, sums_ref,
    src_ref, s0_ref, t_ref,
):
    micro, rows, feat = g_ref.shape
    per_peer = h0.shape[0] // micro
    for slot, h in zip(read_slots(), (h0, h1, h2, h3)):
        for m in range(micro):
            at = pl.ds(pl.multiple_of(slot * per_peer, per_peer), per_peer)
            src_ref[at, m * feat : (m + 1) * feat] = h[m * per_peer : (m + 1) * per_peer, :]
    gain = gain_ref[...].astype(F32)
    parts = parts_of(micro * rows, micro)
    for m, part in enumerate(parts):
        cols = slice(m * feat, (m + 1) * feat)
        agg_ref[part, :] = (acc_ref[:, cols] + two_dot(halo_in_ref, src_ref[:, cols])).astype(BF16)
    for part in parts:
        s0_ref[part, :] = nn_dot(agg_ref[part, :], w_agg_ref[...])
    for part in parts:
        for at in pieces(part):
            preact = z_ref[at, :] + s0_ref[at, :]
            sig = 1.0 / (1.0 + jnp.exp(-preact))
            hidden_ref[at, :] = (preact * sig).astype(BF16)
            dact_ref[at, :] = sig * (1.0 + preact * (1.0 - sig))
    for part in parts:
        s0_ref[part, :] = nn_dot(hidden_ref[part, :], w_out_ref[...])
    gain_sum = jnp.zeros((1, feat), F32)
    for m, part in enumerate(parts):
        for at in pieces(part):
            output = s0_ref[at, :]
            centred = output - row_mean(output)
            inv_std = lax.rsqrt(row_mean(centred * centred) + EPSILON)
            normed = centred * inv_std
            normed_ref[at, :] = normed
            inv_ref[at, :] = jnp.broadcast_to(inv_std, (PIECE, 128))
            g = g_ref[m, at.start - part.start : at.stop - part.start, :].astype(F32)
            gpn_ref[at, :] = norm_back(g, normed, inv_std, gain)
            gain_sum += jnp.sum(g * normed, axis=0, keepdims=True)
    for part in parts:
        s0_ref[part, :] = nt_dot(gpn_ref[part, :], w_out_ref[...])
    bias_sum = jnp.zeros((1, feat), F32)
    for part in parts:
        for at in pieces(part):
            gpre = (s0_ref[at, :] * dact_ref[at, :]).astype(BF16)
            gpre_ref[at, :] = gpre
            bias_sum += jnp.sum(gpre.astype(F32), axis=0, keepdims=True)
    for m, part in enumerate(parts):
        cols = slice(m * feat, (m + 1) * feat)
        gm = nt_dot(gpre_ref[part, :], w_agg_ref[...]).astype(BF16)
        both_ref[:rows, cols] = gm
        both_ref[rows:, cols] = gpre_ref[part, :]
        t_ref[:, cols] = two_dot(halo_back_ref, gm)
    put_halo_grads(t_ref, (o0, o1, o2, o3))
    sums_ref[...] = jnp.concatenate([bias_sum, gain_sum, jnp.zeros((EXTRA - 2, feat), F32)], 0)


def lower_kernel(g_ref, gpre_ref, gm_ref, back_ref, w_node_ref, cpart_ref, g_out):
    feat = g_ref.shape[1]

    @on_core(0)
    def _():
        g_out[...] = g_ref[...]
        for m, part in enumerate(parts_of(g_ref.shape[0], 2)):
            back = nt_dot(gpre_ref[part, :], w_node_ref[...])
            spread = two_dot(back_ref, gm_ref[:, m * feat : (m + 1) * feat])
            cpart_ref[part, :] = g_ref[part, :].astype(F32) + back + spread


def upper_kernel(g_ref, both_ref, back_ref, w_node_ref, cpart_ref):
    micro, rows, feat = g_ref.shape

    @on_core(0)
    def _():
        for m, part in enumerate(parts_of(micro * rows, micro)):
            cols = slice(m * feat, (m + 1) * feat)
            back = nt_dot(both_ref[rows:, cols], w_node_ref[...])
            spread = two_dot(back_ref, both_ref[:rows, cols])
            cpart_ref[part, :] = g_ref[m].astype(F32) + back + spread


def first_bit():
    return (lax.axis_index("dom") >> (1 - lax.axis_index("segment"))) & 1


def second_bit():
    return (lax.axis_index("dom") >> lax.axis_index("segment")) & 1


def chunk_order(chunks):
    core = lax.axis_index("segment")
    low = [d for d in range(chunks) if not d & 2]
    high = [d for d in range(chunks) if not d & 1]
    starts = [a + core * (b - a) for a, b in zip(low, high)]
    step, mine = 2 - core, first_bit()
    return [d + mine * step for d in starts] + [d + (1 - mine) * step for d in starts]


def weight_products(la_ref, lb_ref, gpre_ref, gpn_ref, sums, keep_ref, send_ref):
    n, rows, feat = keep_ref.shape
    share = (rows - EXTRA) // 3
    for base in (n, 0):
        a = nn_dot(la_ref[base * 2 * share : (base + n) * 2 * share, :], gpre_ref[...])
        b = nn_dot(lb_ref[base * share : (base + n) * share, :], gpn_ref[...])
        for i in range(n):
            for lo, v in (
                (0, a[i * 2 * share : (i + 1) * 2 * share]),
                (2 * share, b[i * share : (i + 1) * share]),
                (3 * share, sums),
            ):
                if base:
                    at = i * rows + lo
                    send_ref[at : at + v.shape[0], :] = v.astype(BF16)
                else:
                    keep_ref[i, lo : lo + v.shape[0], :] = v


def turn_kernel(
    chunks, x_ref, agg_ref, hidden_ref, gpre_ref, gpn_ref, sums_ref, la_ref, lb_ref,
    keep_ref, send_ref, turned_ref,
):
    micro, rows, feat = x_ref.shape
    share = feat // chunks
    for m in range(micro):
        turned_ref[:, m * rows : (m + 1) * rows] = x_ref[m].T
    places = [
        pl.ds(pl.multiple_of(d * share, share), share) for d in chunk_order(chunks)
    ]
    for i, at in enumerate(places):
        la_ref[2 * i * share : (2 * i + 1) * share, :] = turned_ref[at, :]
    turned_ref[...] = agg_ref[...].T
    for i, at in enumerate(places):
        la_ref[(2 * i + 1) * share : (2 * i + 2) * share, :] = turned_ref[at, :]
    turned_ref[...] = hidden_ref[...].T
    for i, at in enumerate(places):
        lb_ref[i * share : (i + 1) * share, :] = turned_ref[at, :]

    @on_core(1)
    def _():
        weight_products(la_ref, lb_ref, gpre_ref, gpn_ref, sums_ref[...], keep_ref, send_ref)


def second_kernel(*refs):
    @on_core(0)
    def _():
        second_layer(*refs)


def second_layer(
    onehot_ref, r0, r1, r2, r3, cin_ref, dact_ref, normed_ref, inv_ref, w_out_ref, gain_ref,
    g_ref, gpn_ref, gpre_ref, sums_ref, s0_ref,
):
    total, feat = dact_ref.shape
    parts = parts_of(total, 2)
    per_peer = r0.shape[0] // 2
    gain = gain_ref[...].astype(F32)
    for m, part in enumerate(parts):
        ret = jnp.concatenate([r[m * per_peer : (m + 1) * per_peer, :] for r in (r0, r1, r2, r3)], 0)
        s0_ref[part, :] = nn_dot(onehot_ref[...], ret)
    gain_sum = jnp.zeros((1, feat), F32)
    for part in parts:
        for at in pieces(part):
            g16 = (cin_ref[at, :] + s0_ref[at, :]).astype(BF16)
            g_ref[at, :] = g16
            g = g16.astype(F32)
            normed = normed_ref[at, :]
            gpn_ref[at, :] = norm_back(g, normed, inv_ref[at, 0:1], gain)
            gain_sum += jnp.sum(g * normed, axis=0, keepdims=True)
    for part in parts:
        s0_ref[part, :] = nt_dot(gpn_ref[part, :], w_out_ref[...])
    bias_sum = jnp.zeros((1, feat), F32)
    for part in parts:
        for at in pieces(part):
            gpre = (s0_ref[at, :] * dact_ref[at, :]).astype(BF16)
            gpre_ref[at, :] = gpre
            bias_sum += jnp.sum(gpre.astype(F32), axis=0, keepdims=True)
    sums_ref[...] = jnp.concatenate([bias_sum, gain_sum, jnp.zeros((EXTRA - 2, feat), F32)], 0)


def message_grads(gpre_ref, back_ref, w_agg_ref, gm_ref, t_ref):
    total, feat = gpre_ref.shape
    for m, part in enumerate(parts_of(total, 2)):
        cols = slice(m * feat, (m + 1) * feat)
        gm = nt_dot(gpre_ref[part, :], w_agg_ref[...]).astype(BF16)
        gm_ref[:, cols] = gm
        t_ref[:, cols] = two_dot(back_ref, gm)


def third_kernel(
    gpre_ref, gpn_ref, sums_ref, back_ref, w_agg_ref, la_ref, lb_ref, keep1_ref, send1_ref,
    keep_ref, send_ref, far_ref, near_ref, gm_ref, t_ref,
):
    ride = near_ref.shape[0]
    first = send1_ref.shape[0]

    @on_core(0)
    def _():
        weight_products(la_ref, lb_ref, gpre_ref, gpn_ref, sums_ref[...], keep_ref, send_ref)
        message_grads(gpre_ref, back_ref, w_agg_ref, gm_ref, t_ref)
        cross_ref = send_ref.at[pl.ds(first + ride, ride), :]
        put_halo_grads(
            t_ref,
            (near_ref, cross_ref, send_ref.at[pl.ds(first, ride), :], far_ref.at[pl.ds(0, ride), :]),
        )
        far_ref[ride:, :] = send_ref[first + ride :, :]

    @on_core(1)
    def _():
        keep_ref[...] = keep1_ref[...]
        send_ref[:first, :] = send1_ref[...]


def plain_third_kernel(gpre_ref, back_ref, w_agg_ref, o0, o1, o2, o3, gm_ref, t_ref):
    message_grads(gpre_ref, back_ref, w_agg_ref, gm_ref, t_ref)
    put_halo_grads(t_ref, (o0, o1, o2, o3))


def halve_job(mine, keep, recv, keep2, send2):
    n, rows, _ = keep2.shape
    for i in range(n):
        d, o = 2 * i + mine, 2 * i + 1 - mine
        at = pl.ds(pl.multiple_of(o * rows, 8), rows)
        send2[i * rows : (i + 1) * rows, :] = (keep[o] + recv[at, :].astype(F32)).astype(BF16)
        at = pl.ds(pl.multiple_of(d * rows, 8), rows)
        keep2[i] = keep[d] + recv[at, :].astype(F32)


def carry_kernel(keep, recv, near_ref, far_ref, _, keep2, send2):
    ride = near_ref.shape[0]
    halve_job(second_bit(), keep, recv, keep2, send2)
    at = keep2.shape[0] * keep2.shape[1]
    inner = dom_bit(0) == dom_bit(1)

    @on_core(0)
    def _():
        send2[at : at + ride, :] = near_ref[...]

        @pl.when(inner)
        def _():
            send2[at + ride :, :] = recv[recv.shape[0] - ride :, :]

        @pl.when(jnp.logical_not(inner))
        def _():
            send2[at + ride :, :] = far_ref[ride:, :]


def halve_kernel(keep, recv, keep2, send2):
    halve_job(dom_bit(2), keep, recv, keep2, send2)


def last_kernel(keep, recv, node_ref, agg_ref, out_ref, bias_ref, gain_ref):
    share = node_ref.shape[0]
    total = keep[0] + recv[...].astype(F32)
    node_ref[...] = total[0:share]
    agg_ref[...] = total[share : 2 * share]
    out_ref[...] = total[2 * share : 3 * share]
    bias_ref[...] = total[3 * share : 3 * share + 1]
    gain_ref[...] = total[3 * share + 1 : 3 * share + 2]


def cot_kernel(skips, onehot_ref, r0, r1, r2, r3, cpart_ref, other_ref, cot_ref):
    micro, rows, feat = cot_ref.shape
    n = onehot_ref.shape[1] // PEERS

    @on_core(1)
    def _():
        for m in range(micro):
            cot_ref[m] = other_ref[m * rows : (m + 1) * rows, :]

    @on_core(0)
    def _():
        for m in range(micro):
            ret = jnp.concatenate(
                [r[s + m * n : s + (m + 1) * n, :] for r, s in zip((r0, r1, r2, r3), skips)], 0
            )
            cot_ref[m] = (
                cpart_ref[m * rows : (m + 1) * rows, :] + nn_dot(onehot_ref[...], ret)
            ).astype(BF16)


def whole_kernel(x_ref, agg_ref, hidden_ref, gpn_ref, gpre_ref, node_ref, agg_out, out_ref):
    rows = x_ref.shape[1]
    gpre = gpre_ref[...]
    node_ref[...] = tn_dot(x_ref[0], gpre[:rows]) + tn_dot(x_ref[1], gpre[rows:])
    agg_out[...] = tn_dot(agg_ref[...], gpre)
    out_ref[...] = tn_dot(hidden_ref[...], gpn_ref[...])


def body(
    section_inputs,
    out_cot,
    w_node,
    w_agg,
    w_out,
    bias,
    gain,
    send_rows,
    blk_pairs,
    blk_count,
    blk_values,
):
    peers = lax.axis_size("dom")
    segment = lax.axis_index("segment")
    assert lax.axis_size("segment") == 2 and peers % 4 == 0
    x = section_inputs[0]
    micro, rows, feat = x.shape
    _, slots, per_peer = send_rows.shape
    assert slots * per_peer == 128 and slots == PEERS and micro == 2
    total = micro * rows
    values = blk_values[0]
    row_blocks = rows // 128
    wide = micro * feat
    w_n, w_a, w_o = w_node[0], w_agg[0], w_out[0]
    matmul = 2 * total * feat * feat
    size = total * feat
    chunk = shape((micro * per_peer, feat), BF16)

    def swap_partner(p, k):
        if k == 0:
            return p ^ 1
        if k == 1:
            return (p + 1 if p & 1 else p - 1) % peers
        up = (p >> 1) & 1
        return (p + 2 if up == (k == 3) else p - 2) % peers

    def swapped(v, k, cores):
        return lax.ppermute(
            v,
            ("dom", "segment"),
            [(2 * p + s, 2 * swap_partner(p, k) + d) for p in range(peers) for s, d in cores],
        )

    def across(v):
        return lax.ppermute(v, "segment", [(0, 1), (1, 0)])

    def flipped(v, bits):
        return lax.ppermute(
            v,
            ("dom", "segment"),
            [(2 * p + s, 2 * (p ^ (1 << bits[s])) + s) for p in range(peers) for s in (0, 1)],
        )

    f_full, b_full = shape((total, feat), F32), shape((total, feat), BF16)
    s_sums = shape((EXTRA, feat), F32)
    dma = pltpu.SemaphoreType.DMA
    *outgoing, x, onehot = call(
        gather_kernel,
        [chunk] * slots + [shape(x.shape, BF16), shape((rows, slots * per_peer), BF16)],
        [pltpu.VMEM(send_rows.shape, jnp.int32), dma((2,))],
        matmul // 8, 2 * size, send_rows, x,
        raw=2,
    )
    same, other_core = ((0, 0), (1, 1)), ((0, 1), (1, 0))
    w_other = across(w_n)
    halos = [swapped(v, k, same) for k, v in enumerate(outgoing)]
    halo_rows = slots * per_peer
    loaded = (w_n, w_a, w_o, gain, out_cot)
    z, acc, halo_in, local_back, halo_back, w_n, w_a, w_o, gain, g_last = call(
        node_kernel,
        [f_full, shape((rows, wide), F32), shape((2, rows, halo_rows), BF16)]
        + [shape((2, rows, rows), BF16), shape((2, halo_rows, rows), BF16)]
        + [shape(v.shape, BF16) for v in loaded],
        [
            pltpu.VMEM(values.shape, BF16), pltpu.VMEM((rows, wide), BF16), pltpu.VMEM(bias.shape, BF16),
            pltpu.VMEM((row_blocks, row_blocks + 1, 128, 128), F32), pltpu.VMEM((2, rows, rows), BF16),
            dma((7,)),
        ],
        2 * matmul, 8 * size,
        blk_pairs, blk_count, values, w_n, bias, w_a, w_o, gain, out_cot, x,
        scalars=2, raw=7,
    )
    first = call(
        first_kernel,
        [chunk] * slots
        + [shape((2 * rows, wide), BF16), f_full, f_full, shape((total, 128), F32)]
        + [b_full] * 4 + [s_sums],
        [
            pltpu.VMEM((halo_rows, wide), BF16),
            pltpu.VMEM((total, feat), F32),
            pltpu.VMEM((halo_rows, wide), F32),
        ],
        4 * matmul, 20 * size,
        *halos, halo_in, halo_back, z, acc, g_last, w_a, w_o, gain, w_other,
        after=1,
    )
    to_return = first[:slots]
    both, dact, normed, inv_std, agg, hidden, gpn1, gpre1, sums1 = first[slots:]
    returned = [swapped(v, k, other_core) for k, v in enumerate(to_return)]
    c_in = call(
        upper_kernel, f_full, [], matmul, 10 * size, g_last, across(both), local_back, w_other
    )
    share = feat // peers
    rows_each = 3 * share + EXTRA
    halving = peers == 8

    def kept(n, extra=0):
        return [shape((n, rows_each, feat), F32), shape((n * rows_each + extra, feat), BF16)]

    if halving:
        turned = call(
            functools.partial(turn_kernel, peers),
            [shape((16 * share, total), BF16), shape((8 * share, total), BF16)] + kept(4),
            [pltpu.VMEM((feat, total), BF16)],
            3 * matmul, 20 * size,
            x, agg, hidden, gpre1, gpn1, sums1,
        )
    g_low, gpn, gpre, sums = call(
        second_kernel,
        [b_full, b_full, b_full, s_sums],
        [pltpu.VMEM((total, feat), F32)],
        2 * matmul, 16 * size,
        onehot, *returned, c_in, dact, normed, inv_std, w_o, gain,
    )
    scr_t, gm_out = pltpu.VMEM((halo_rows, wide), F32), shape((rows, wide), BF16)
    if halving:
        ride = chunk.shape[0]
        keep, send, far, near, gm = call(
            third_kernel,
            kept(4, 2 * ride) + [shape((2 * ride, feat), BF16), chunk, gm_out],
            [scr_t], 4 * matmul, 16 * size,
            gpre, gpn, sums, halo_back, w_a, *turned,
        )
        recv = flipped(send, (1, 0))
        far = swapped(far, 3, ((0, 0),))
    else:
        *to_return, gm = call(
            plain_third_kernel, [chunk] * slots + [gm_out], [scr_t],
            2 * matmul, 8 * size, gpre, halo_back, w_a,
        )
    cpart0, g_low = call(
        lower_kernel, [f_full, b_full], [], matmul, 10 * size, g_low, gpre, gm, local_back, w_n
    )
    other = across(g_low)
    skips = (0,) * slots
    if halving:
        up = recv
        keep, send = call(
            carry_kernel, kept(2, 2 * ride), [], size, 8 * size, keep, recv, near, far, cpart0,
            after=1,
        )
        recv = flipped(send, (0, 1))
        first = 2 * rows_each
        returned, skips = (recv, recv, up, far), (first, first + ride, 2 * first, 0)
        keep, send = call(halve_kernel, kept(1), [], size, 4 * size, keep, recv)
        recv = flipped(send, (2, 2))
        part, row = shape((share, feat), F32), shape((1, feat), F32)
        grad_node, grad_agg, grad_out, grad_bias, grad_gain = call(
            last_kernel, [part, part, part, row, row], [], size, 2 * size, keep, recv,
        )
    else:
        is_last = segment == 1
        gpn, gpre = jnp.where(is_last, gpn1, gpn), jnp.where(is_last, gpre1, gpre)
        sums = jnp.where(is_last, sums1, sums)
        square = shape((feat, feat), F32)
        full = call(
            whole_kernel, [square] * 3, [], 3 * matmul, 12 * size, x, agg, hidden, gpn, gpre
        )
        grad_node, grad_agg, grad_out = [
            lax.psum_scatter(v, "dom", scatter_dimension=0, tiled=True) for v in full
        ]
        sums = lax.psum(sums, "dom")
        grad_bias, grad_gain = sums[0:1], sums[1:2]
        returned = [swapped(v, k, ((0, 0),)) for k, v in enumerate(to_return)]
    cot = call(
        functools.partial(cot_kernel, skips), shape((micro, rows, feat), BF16), [], matmul // 4, 4 * size,
        onehot, *returned, cpart0, other,
    )
    return (
        cot[None],
        grad_node[None],
        grad_agg[None],
        grad_out[None],
        grad_bias,
        grad_gain,
    )


def solution(mesh):
    placed = (
        P("segment", None, ("grp", "dom"), None),
        P(None, ("grp", "dom"), None),
        P("segment", None, None),
        P("segment", None, None),
        P("segment", None, None),
        P("segment", None),
        P("segment", None),
        P("dom", None, None),
        P("dom", None, None),
        P("dom"),
        P("dom", None, None, None),
    )
    return jax.shard_map(
        body,
        mesh=mesh,
        in_specs=placed,
        out_specs=(
            P("segment", None, ("grp", "dom"), None),
            P("segment", ("grp", "dom"), None),
            P("segment", ("grp", "dom"), None),
            P("segment", ("grp", "dom"), None),
            P("segment", "grp"),
            P("segment", "grp"),
        ),
        check_vma=False,
    )
```

```python
import functools

import jax
import jax.numpy as jnp
from jax import lax
from jax.experimental import pallas as pl
from jax.experimental.pallas import tpu as pltpu
from jax.sharding import PartitionSpec as P

EPSILON = 1e-05
F32 = jnp.float32
BF16 = jnp.bfloat16
VMEM = pl.BlockSpec(memory_space=pltpu.VMEM)
SMEM = pl.BlockSpec(memory_space=pltpu.SMEM)
HBM = pl.BlockSpec(memory_space=pltpu.HBM)
ANY = pl.BlockSpec(memory_space=pl.ANY)
PEERS = 4
EXTRA = 8
PIECE = 64


def nn_dot(a, b):
    return jnp.dot(a, b, preferred_element_type=F32)


def nt_dot(a, b):
    return lax.dot_general(a, b, (((1,), (1,)), ((), ())), preferred_element_type=F32)


def tn_dot(a, b):
    return lax.dot_general(a, b, (((0,), (0,)), ((), ())), preferred_element_type=F32)


def shape(dims, dtype):
    return jax.ShapeDtypeStruct(dims, dtype)


def call(kernel, outs, scratch, flops, byts, *args, scalars=0, raw=0, after=0):
    blocks = len(args) - scalars - raw - after
    args = list(args)
    for i in range(scalars, scalars + raw):
        args[i] = pltpu.with_memory_space_constraint(args[i], pltpu.HBM)
    return pl.pallas_call(
        kernel,
        out_shape=outs,
        in_specs=[SMEM] * scalars + [HBM] * raw + [VMEM] * blocks + [ANY] * after,
        out_specs=jax.tree.map(lambda _: VMEM, outs),
        scratch_shapes=scratch,
        compiler_params=pltpu.CompilerParams(vmem_limit_bytes=24 * 1024 * 1024),
        cost_estimate=pl.CostEstimate(flops=flops, bytes_accessed=byts, transcendentals=0),
    )(*args)


def on_core(core):
    return pl.when(lax.axis_index("segment") == core)


def two_dot(pair_ref, b):
    return nn_dot(pair_ref[0], b) + nn_dot(pair_ref[1], b)


def dom_bit(i):
    return (lax.axis_index("dom") >> i) & 1


def sent_slots():
    x, z = dom_bit(0), dom_bit(1)
    return x, 1 - x, 2 + z, 3 - z


def read_slots():
    x, z = dom_bit(0), dom_bit(1)
    return 1 - x, x, 3 - z, 2 + z


def target_onehot(targets_ref, rows):
    ids = jnp.concatenate([targets_ref[0, pl.ds(s, 1), :] for s in sent_slots()], 1)
    return (lax.broadcasted_iota(jnp.int32, (rows, ids.shape[1]), 0) == ids).astype(BF16)


def gather_kernel(targets_hbm, x_hbm, o0, o1, o2, o3, x_ref, onehot_ref, targets_ref, sems):
    copies = [
        pltpu.make_async_copy(targets_hbm, targets_ref, sems.at[0]),
        pltpu.make_async_copy(x_hbm, x_ref, sems.at[1]),
    ]
    for c in copies:
        c.start()
    micro, rows, _ = x_ref.shape
    per_peer = o0.shape[0] // micro
    copies[0].wait()
    onehot = target_onehot(targets_ref, rows)
    onehot_ref[...] = onehot
    copies[1].wait()
    for m in range(micro):
        picked = tn_dot(onehot, x_ref[m]).astype(BF16)
        for k, out in enumerate((o0, o1, o2, o3)):
            out[m * per_peer : (m + 1) * per_peer, :] = picked[k * per_peer : (k + 1) * per_peer]


def node_kernel(
    pairs_ref, count_ref, values_hbm, w_hbm, bias_hbm, w_agg_hbm, w_out_hbm, gain_hbm, g_hbm, x_ref,
    z_ref, acc_ref, halo_in_ref, local_back_ref, halo_back_ref, w_ref, w_agg_ref, w_out_ref, gain_ref,
    g_ref,
    values_ref, src_ref, bias_ref, dense_ref, local_ref, sems,
):
    copies = [
        pltpu.make_async_copy(a, b, sems.at[i])
        for i, (a, b) in enumerate(
            (
                (values_hbm, values_ref), (w_hbm, w_ref), (bias_hbm, bias_ref),
                (w_agg_hbm, w_agg_ref), (w_out_hbm, w_out_ref), (gain_hbm, gain_ref), (g_hbm, g_ref),
            )
        )
    ]
    for c in copies:
        c.start()
    micro, rows, feat = x_ref.shape
    row_blocks, blocks = dense_ref.shape[:2]
    for m in range(micro):
        src_ref[:, m * feat : (m + 1) * feat] = x_ref[m]
    dense_ref[...] = jnp.zeros_like(dense_ref)
    copies[0].wait()
    for k in range(values_ref.shape[0]):

        @pl.when(k < count_ref[0])
        def _():
            dense_ref[pairs_ref[0, 0, k], pairs_ref[0, 1, k]] += values_ref[k].astype(F32)

    copies[1].wait()
    copies[2].wait()
    for m in range(micro):
        z_ref[m * rows : (m + 1) * rows, :] = nn_dot(x_ref[m], w_ref[...]) + bias_ref[
            ...
        ].astype(F32)
    for d in range(row_blocks):
        down = slice(d * 128, (d + 1) * 128)
        for c in range(blocks):
            block = dense_ref[d, c]
            high = block.astype(BF16)
            for i, v in enumerate((high, (block - high.astype(F32)).astype(BF16))):
                if c < row_blocks:
                    across_to = slice(c * 128, (c + 1) * 128)
                    local_ref[i, down, across_to] = v
                    local_back_ref[i, across_to, down] = v.T
                else:
                    halo_in_ref[i, down, :] = v
                    halo_back_ref[i, :, down] = v.T
    acc_ref[...] = two_dot(local_ref, src_ref[...])
    for c in copies[3:]:
        c.wait()


def pieces(part):
    return [slice(r, r + PIECE) for r in range(part.start, part.stop, PIECE)]


def row_mean(v):
    return jnp.mean(v, axis=1, keepdims=True)


def norm_back(g, normed, inv_std, gain):
    e = g * gain
    return (inv_std * (e - row_mean(e) - normed * row_mean(e * normed))).astype(BF16)


def parts_of(total, micro):
    rows = total // micro
    return [slice(m * rows, (m + 1) * rows) for m in range(micro)]


def put_halo_grads(t_ref, outs):
    feat = outs[0].shape[1]
    per_peer = outs[0].shape[0] // 2
    for slot, out in zip(read_slots(), outs):
        for m in range(2):
            at = pl.ds(pl.multiple_of(slot * per_peer, per_peer), per_peer)
            out[m * per_peer : (m + 1) * per_peer, :] = t_ref[
                at, m * feat : (m + 1) * feat
            ].astype(BF16)


def first_kernel(
    h0, h1, h2, h3, halo_in_ref, halo_back_ref, z_ref, acc_ref, g_ref, w_agg_ref, w_out_ref, gain_ref, _,
    o0, o1, o2, o3, both_ref, dact_ref, normed_ref, inv_ref, agg_ref, hidden_ref, gpn_ref,
    gpre_ref, sums_ref,
    src_ref, s0_ref, t_ref,
):
    micro, rows, feat = g_ref.shape
    per_peer = h0.shape[0] // micro
    for slot, h in zip(read_slots(), (h0, h1, h2, h3)):
        for m in range(micro):
            at = pl.ds(pl.multiple_of(slot * per_peer, per_peer), per_peer)
            src_ref[at, m * feat : (m + 1) * feat] = h[m * per_peer : (m + 1) * per_peer, :]
    gain = gain_ref[...].astype(F32)
    parts = parts_of(micro * rows, micro)
    for m, part in enumerate(parts):
        cols = slice(m * feat, (m + 1) * feat)
        agg_ref[part, :] = (acc_ref[:, cols] + two_dot(halo_in_ref, src_ref[:, cols])).astype(BF16)
    for part in parts:
        s0_ref[part, :] = nn_dot(agg_ref[part, :], w_agg_ref[...])
    for part in parts:
        for at in pieces(part):
            preact = z_ref[at, :] + s0_ref[at, :]
            sig = 1.0 / (1.0 + jnp.exp(-preact))
            hidden_ref[at, :] = (preact * sig).astype(BF16)
            dact_ref[at, :] = sig * (1.0 + preact * (1.0 - sig))
    for part in parts:
        s0_ref[part, :] = nn_dot(hidden_ref[part, :], w_out_ref[...])
    gain_sum = jnp.zeros((1, feat), F32)
    for m, part in enumerate(parts):
        for at in pieces(part):
            output = s0_ref[at, :]
            centred = output - row_mean(output)
            inv_std = lax.rsqrt(row_mean(centred * centred) + EPSILON)
            normed = centred * inv_std
            normed_ref[at, :] = normed
            inv_ref[at, :] = jnp.broadcast_to(inv_std, (PIECE, 128))
            g = g_ref[m, at.start - part.start : at.stop - part.start, :].astype(F32)
            gpn_ref[at, :] = norm_back(g, normed, inv_std, gain)
            gain_sum += jnp.sum(g * normed, axis=0, keepdims=True)
    for part in parts:
        s0_ref[part, :] = nt_dot(gpn_ref[part, :], w_out_ref[...])
    bias_sum = jnp.zeros((1, feat), F32)
    for part in parts:
        for at in pieces(part):
            gpre = (s0_ref[at, :] * dact_ref[at, :]).astype(BF16)
            gpre_ref[at, :] = gpre
            bias_sum += jnp.sum(gpre.astype(F32), axis=0, keepdims=True)
    for m, part in enumerate(parts):
        cols = slice(m * feat, (m + 1) * feat)
        gm = nt_dot(gpre_ref[part, :], w_agg_ref[...]).astype(BF16)
        both_ref[:rows, cols] = gm
        both_ref[rows:, cols] = gpre_ref[part, :]
        t_ref[:, cols] = two_dot(halo_back_ref, gm)
    put_halo_grads(t_ref, (o0, o1, o2, o3))
    sums_ref[...] = jnp.concatenate([bias_sum, gain_sum, jnp.zeros((EXTRA - 2, feat), F32)], 0)


def lower_kernel(g_ref, gpre_ref, gm_ref, back_ref, w_node_ref, cpart_ref, g_out):
    feat = g_ref.shape[1]

    @on_core(0)
    def _():
        g_out[...] = g_ref[...]
        for m, part in enumerate(parts_of(g_ref.shape[0], 2)):
            back = nt_dot(gpre_ref[part, :], w_node_ref[...])
            spread = two_dot(back_ref, gm_ref[:, m * feat : (m + 1) * feat])
            cpart_ref[part, :] = g_ref[part, :].astype(F32) + back + spread


def upper_kernel(g_ref, both_ref, back_ref, w_node_ref, cpart_ref):
    micro, rows, feat = g_ref.shape

    @on_core(0)
    def _():
        for m, part in enumerate(parts_of(micro * rows, micro)):
            cols = slice(m * feat, (m + 1) * feat)
            back = nt_dot(both_ref[rows:, cols], w_node_ref[...])
            spread = two_dot(back_ref, both_ref[:rows, cols])
            cpart_ref[part, :] = g_ref[m].astype(F32) + back + spread


def first_bit():
    return (lax.axis_index("dom") >> (1 - lax.axis_index("segment"))) & 1


def second_bit():
    return (lax.axis_index("dom") >> lax.axis_index("segment")) & 1


def chunk_order(chunks):
    core = lax.axis_index("segment")
    low = [d for d in range(chunks) if not d & 2]
    high = [d for d in range(chunks) if not d & 1]
    starts = [a + core * (b - a) for a, b in zip(low, high)]
    step, mine = 2 - core, first_bit()
    return [d + mine * step for d in starts] + [d + (1 - mine) * step for d in starts]


def weight_products(la_ref, lb_ref, gpre_ref, gpn_ref, sums, keep_ref, send_ref):
    n, rows, feat = keep_ref.shape
    share = (rows - EXTRA) // 3
    for base in (n, 0):
        a = nn_dot(la_ref[base * 2 * share : (base + n) * 2 * share, :], gpre_ref[...])
        b = nn_dot(lb_ref[base * share : (base + n) * share, :], gpn_ref[...])
        for i in range(n):
            for lo, v in (
                (0, a[i * 2 * share : (i + 1) * 2 * share]),
                (2 * share, b[i * share : (i + 1) * share]),
                (3 * share, sums),
            ):
                if base:
                    at = i * rows + lo
                    send_ref[at : at + v.shape[0], :] = v.astype(BF16)
                else:
                    keep_ref[i, lo : lo + v.shape[0], :] = v


def turn_kernel(
    chunks, x_ref, agg_ref, hidden_ref, gpre_ref, gpn_ref, sums_ref, la_ref, lb_ref,
    keep_ref, send_ref, turned_ref,
):
    micro, rows, feat = x_ref.shape
    share = feat // chunks
    for m in range(micro):
        turned_ref[:, m * rows : (m + 1) * rows] = x_ref[m].T
    places = [
        pl.ds(pl.multiple_of(d * share, share), share) for d in chunk_order(chunks)
    ]
    for i, at in enumerate(places):
        la_ref[2 * i * share : (2 * i + 1) * share, :] = turned_ref[at, :]
    turned_ref[...] = agg_ref[...].T
    for i, at in enumerate(places):
        la_ref[(2 * i + 1) * share : (2 * i + 2) * share, :] = turned_ref[at, :]
    turned_ref[...] = hidden_ref[...].T
    for i, at in enumerate(places):
        lb_ref[i * share : (i + 1) * share, :] = turned_ref[at, :]

    @on_core(1)
    def _():
        weight_products(la_ref, lb_ref, gpre_ref, gpn_ref, sums_ref[...], keep_ref, send_ref)


def second_kernel(*refs):
    @on_core(0)
    def _():
        second_layer(*refs)


def second_layer(
    onehot_ref, r0, r1, r2, r3, cin_ref, dact_ref, normed_ref, inv_ref, w_out_ref, gain_ref,
    g_ref, gpn_ref, gpre_ref, sums_ref, s0_ref,
):
    total, feat = dact_ref.shape
    parts = parts_of(total, 2)
    per_peer = r0.shape[0] // 2
    gain = gain_ref[...].astype(F32)
    for m, part in enumerate(parts):
        ret = jnp.concatenate([r[m * per_peer : (m + 1) * per_peer, :] for r in (r0, r1, r2, r3)], 0)
        s0_ref[part, :] = nn_dot(onehot_ref[...], ret)
    gain_sum = jnp.zeros((1, feat), F32)
    for part in parts:
        for at in pieces(part):
            g16 = (cin_ref[at, :] + s0_ref[at, :]).astype(BF16)
            g_ref[at, :] = g16
            g = g16.astype(F32)
            normed = normed_ref[at, :]
            gpn_ref[at, :] = norm_back(g, normed, inv_ref[at, 0:1], gain)
            gain_sum += jnp.sum(g * normed, axis=0, keepdims=True)
    for part in parts:
        s0_ref[part, :] = nt_dot(gpn_ref[part, :], w_out_ref[...])
    bias_sum = jnp.zeros((1, feat), F32)
    for part in parts:
        for at in pieces(part):
            gpre = (s0_ref[at, :] * dact_ref[at, :]).astype(BF16)
            gpre_ref[at, :] = gpre
            bias_sum += jnp.sum(gpre.astype(F32), axis=0, keepdims=True)
    sums_ref[...] = jnp.concatenate([bias_sum, gain_sum, jnp.zeros((EXTRA - 2, feat), F32)], 0)


def message_grads(gpre_ref, back_ref, w_agg_ref, gm_ref, t_ref):
    total, feat = gpre_ref.shape
    for m, part in enumerate(parts_of(total, 2)):
        cols = slice(m * feat, (m + 1) * feat)
        gm = nt_dot(gpre_ref[part, :], w_agg_ref[...]).astype(BF16)
        gm_ref[:, cols] = gm
        t_ref[:, cols] = two_dot(back_ref, gm)


def third_kernel(
    gpre_ref, gpn_ref, sums_ref, back_ref, w_agg_ref, la_ref, lb_ref, keep1_ref, send1_ref,
    keep_ref, send_ref, near_ref, far_ref, gm_ref, t_ref,
):
    ride = near_ref.shape[0]
    first = send1_ref.shape[0]

    @on_core(0)
    def _():
        weight_products(la_ref, lb_ref, gpre_ref, gpn_ref, sums_ref[...], keep_ref, send_ref)
        message_grads(gpre_ref, back_ref, w_agg_ref, gm_ref, t_ref)
        below, cross = (send_ref.at[pl.ds(first + i * ride, ride), :] for i in (0, 1))
        put_halo_grads(t_ref, (near_ref, cross, below, far_ref.at[pl.ds(0, ride), :]))
        far_ref[ride:, :] = send_ref[first + ride :, :]

    @on_core(1)
    def _():
        keep_ref[...] = keep1_ref[...]
        send_ref[:first, :] = send1_ref[...]


def plain_third_kernel(gpre_ref, back_ref, w_agg_ref, o0, o1, o2, o3, gm_ref, t_ref):
    message_grads(gpre_ref, back_ref, w_agg_ref, gm_ref, t_ref)
    put_halo_grads(t_ref, (o0, o1, o2, o3))


def halve_job(mine, keep, recv, keep2, send2):
    n, rows, _ = keep2.shape
    for i in range(n):
        d, o = 2 * i + mine, 2 * i + 1 - mine
        at = pl.ds(pl.multiple_of(o * rows, 8), rows)
        send2[i * rows : (i + 1) * rows, :] = (keep[o] + recv[at, :].astype(F32)).astype(BF16)
        at = pl.ds(pl.multiple_of(d * rows, 8), rows)
        keep2[i] = keep[d] + recv[at, :].astype(F32)


def carry_kernel(keep, recv, near_ref, _, keep2, send2):
    ride = near_ref.shape[0]
    halve_job(second_bit(), keep, recv, keep2, send2)
    at = keep2.shape[0] * keep2.shape[1]

    @on_core(0)
    def _():
        send2[at : at + ride, :] = near_ref[...]
        send2[at + ride :, :] = recv[recv.shape[0] - ride :, :]


def halve_kernel(keep, recv, _, keep2, send2):
    halve_job(dom_bit(2), keep, recv, keep2, send2)


def sums_out(keep, recv, node_ref, agg_ref, out_ref, bias_ref, gain_ref):
    share = node_ref.shape[0]
    total = keep[0] + recv[...].astype(F32)
    node_ref[...] = total[0:share]
    agg_ref[...] = total[share : 2 * share]
    out_ref[...] = total[2 * share : 3 * share]
    bias_ref[...] = total[3 * share : 3 * share + 1]
    gain_ref[...] = total[3 * share + 1 : 3 * share + 2]


def cot_out(skips, onehot_ref, sources, cpart_ref, other_ref, cot_ref):
    micro, rows, feat = cot_ref.shape
    n = onehot_ref.shape[1] // PEERS
    inner = dom_bit(0) != dom_bit(1)

    @on_core(1)
    def _():
        for m in range(micro):
            cot_ref[m] = other_ref[m * rows : (m + 1) * rows, :]

    @on_core(0)
    def _():
        for m in range(micro):
            got = [r[s + m * n : s + (m + 1) * n, :] for r, s in zip(sources, skips)]
            if len(got) > PEERS:
                got[1] = jnp.where(inner, got[1], got.pop())
            ret = jnp.concatenate(got, 0)
            cot_ref[m] = (
                cpart_ref[m * rows : (m + 1) * rows, :] + nn_dot(onehot_ref[...], ret)
            ).astype(BF16)


def final_kernel(skips, onehot_ref, *rest):
    *sources, cpart_ref, other_ref, keep, recv, cot_ref, node_ref, agg_ref, out_ref, bias_ref, gain_ref = rest
    cot_out(skips, onehot_ref, sources, cpart_ref, other_ref, cot_ref)
    sums_out(keep, recv, node_ref, agg_ref, out_ref, bias_ref, gain_ref)


def cot_kernel(skips, onehot_ref, *rest):
    *sources, cpart_ref, other_ref, cot_ref = rest
    cot_out(skips, onehot_ref, sources, cpart_ref, other_ref, cot_ref)


def whole_kernel(x_ref, agg_ref, hidden_ref, gpn_ref, gpre_ref, node_ref, agg_out, out_ref):
    rows = x_ref.shape[1]
    gpre = gpre_ref[...]
    node_ref[...] = tn_dot(x_ref[0], gpre[:rows]) + tn_dot(x_ref[1], gpre[rows:])
    agg_out[...] = tn_dot(agg_ref[...], gpre)
    out_ref[...] = tn_dot(hidden_ref[...], gpn_ref[...])


def body(
    section_inputs,
    out_cot,
    w_node,
    w_agg,
    w_out,
    bias,
    gain,
    send_rows,
    blk_pairs,
    blk_count,
    blk_values,
):
    peers = lax.axis_size("dom")
    segment = lax.axis_index("segment")
    assert lax.axis_size("segment") == 2 and peers % 4 == 0
    x = section_inputs[0]
    micro, rows, feat = x.shape
    _, slots, per_peer = send_rows.shape
    assert slots * per_peer == 128 and slots == PEERS and micro == 2
    total = micro * rows
    values = blk_values[0]
    row_blocks = rows // 128
    wide = micro * feat
    w_n, w_a, w_o = w_node[0], w_agg[0], w_out[0]
    matmul = 2 * total * feat * feat
    size = total * feat
    chunk = shape((micro * per_peer, feat), BF16)

    def swap_partner(p, k):
        if k == 0:
            return p ^ 1
        if k == 1:
            return (p + 1 if p & 1 else p - 1) % peers
        up = (p >> 1) & 1
        return (p + 2 if up == (k == 3) else p - 2) % peers

    def swapped(v, k, cores):
        return lax.ppermute(
            v,
            ("dom", "segment"),
            [(2 * p + s, 2 * swap_partner(p, k) + d) for p in range(peers) for s, d in cores],
        )

    def across(v):
        return lax.ppermute(v, "segment", [(0, 1), (1, 0)])

    def flipped(v, bits):
        return lax.ppermute(
            v,
            ("dom", "segment"),
            [(2 * p + s, 2 * (p ^ (1 << bits[s])) + s) for p in range(peers) for s in (0, 1)],
        )

    f_full, b_full = shape((total, feat), F32), shape((total, feat), BF16)
    s_sums = shape((EXTRA, feat), F32)
    dma = pltpu.SemaphoreType.DMA
    *outgoing, x, onehot = call(
        gather_kernel,
        [chunk] * slots + [shape(x.shape, BF16), shape((rows, slots * per_peer), BF16)],
        [pltpu.VMEM(send_rows.shape, jnp.int32), dma((2,))],
        matmul // 8, 2 * size, send_rows, x,
        raw=2,
    )
    same, other_core = ((0, 0), (1, 1)), ((0, 1), (1, 0))
    w_other = across(w_n)
    halos = [swapped(v, k, same) for k, v in enumerate(outgoing)]
    halo_rows = slots * per_peer
    loaded = (w_n, w_a, w_o, gain, out_cot)
    z, acc, halo_in, local_back, halo_back, w_n, w_a, w_o, gain, g_last = call(
        node_kernel,
        [f_full, shape((rows, wide), F32), shape((2, rows, halo_rows), BF16)]
        + [shape((2, rows, rows), BF16), shape((2, halo_rows, rows), BF16)]
        + [shape(v.shape, BF16) for v in loaded],
        [
            pltpu.VMEM(values.shape, BF16), pltpu.VMEM((rows, wide), BF16), pltpu.VMEM(bias.shape, BF16),
            pltpu.VMEM((row_blocks, row_blocks + 1, 128, 128), F32), pltpu.VMEM((2, rows, rows), BF16),
            dma((7,)),
        ],
        2 * matmul, 8 * size,
        blk_pairs, blk_count, values, w_n, bias, w_a, w_o, gain, out_cot, x,
        scalars=2, raw=7,
    )
    first = call(
        first_kernel,
        [chunk] * slots
        + [shape((2 * rows, wide), BF16), f_full, f_full, shape((total, 128), F32)]
        + [b_full] * 4 + [s_sums],
        [
            pltpu.VMEM((halo_rows, wide), BF16),
            pltpu.VMEM((total, feat), F32),
            pltpu.VMEM((halo_rows, wide), F32),
        ],
        4 * matmul, 20 * size,
        *halos, halo_in, halo_back, z, acc, g_last, w_a, w_o, gain, w_other,
        after=1,
    )
    to_return = first[:slots]
    both, dact, normed, inv_std, agg, hidden, gpn1, gpre1, sums1 = first[slots:]
    returned = [swapped(v, k, other_core) for k, v in enumerate(to_return)]
    c_in = call(
        upper_kernel, f_full, [], matmul, 10 * size, g_last, across(both), local_back, w_other
    )
    share = feat // peers
    rows_each = 3 * share + EXTRA
    halving = peers == 8

    def kept(n, extra=0):
        return [shape((n, rows_each, feat), F32), shape((n * rows_each + extra, feat), BF16)]

    if halving:
        turned = call(
            functools.partial(turn_kernel, peers),
            [shape((16 * share, total), BF16), shape((8 * share, total), BF16)] + kept(4),
            [pltpu.VMEM((feat, total), BF16)],
            3 * matmul, 20 * size,
            x, agg, hidden, gpre1, gpn1, sums1,
        )
    g_low, gpn, gpre, sums = call(
        second_kernel,
        [b_full, b_full, b_full, s_sums],
        [pltpu.VMEM((total, feat), F32)],
        2 * matmul, 16 * size,
        onehot, *returned, c_in, dact, normed, inv_std, w_o, gain,
    )
    scr_t, gm_out = pltpu.VMEM((halo_rows, wide), F32), shape((rows, wide), BF16)
    if halving:
        ride = chunk.shape[0]
        ride = chunk.shape[0]
        keep, send, near, far, gm = call(
            third_kernel,
            kept(4, 2 * ride) + [chunk, shape((2 * ride, feat), BF16), gm_out],
            [scr_t], 4 * matmul, 16 * size,
            gpre, gpn, sums, halo_back, w_a, *turned,
        )
        recv = flipped(send, (1, 0))
        far = swapped(far, 3, ((0, 0),))
    else:
        *to_return, gm = call(
            plain_third_kernel, [chunk] * slots + [gm_out], [scr_t],
            2 * matmul, 8 * size, gpre, halo_back, w_a,
        )
    cpart0, g_low = call(
        lower_kernel, [f_full, b_full], [], matmul, 10 * size, g_low, gpre, gm, local_back, w_n
    )
    other = across(g_low)
    cot_shape = shape((micro, rows, feat), BF16)
    if halving:
        up = recv
        keep, send = call(
            carry_kernel, kept(2, 2 * ride), [], size, 8 * size, keep, recv, near, cpart0,
            after=1,
        )
        recv = flipped(send, (0, 1))
        hop = swapped(far, 0, ((0, 0),))
        first = 2 * rows_each
        returned = (recv, recv, up, far, hop)
        skips = (first, first + ride, 2 * first, 0, ride)
        keep, send = call(
            halve_kernel, kept(1), [], size, 4 * size, keep, recv, far,
            after=1,
        )
        recv = flipped(send, (2, 2))
        part, row = shape((share, feat), F32), shape((1, feat), F32)
        cot, grad_node, grad_agg, grad_out, grad_bias, grad_gain = call(
            functools.partial(final_kernel, skips), [cot_shape, part, part, part, row, row],
            [], matmul // 4, 6 * size,
            onehot, *returned, cpart0, other, keep, recv,
        )
    else:
        is_last = segment == 1
        gpn, gpre = jnp.where(is_last, gpn1, gpn), jnp.where(is_last, gpre1, gpre)
        sums = jnp.where(is_last, sums1, sums)
        square = shape((feat, feat), F32)
        full = call(
            whole_kernel, [square] * 3, [], 3 * matmul, 12 * size, x, agg, hidden, gpn, gpre
        )
        grad_node, grad_agg, grad_out = [
            lax.psum_scatter(v, "dom", scatter_dimension=0, tiled=True) for v in full
        ]
        sums = lax.psum(sums, "dom")
        grad_bias, grad_gain = sums[0:1], sums[1:2]
        returned = [swapped(v, k, ((0, 0),)) for k, v in enumerate(to_return)]
        cot = call(
            functools.partial(cot_kernel, (0,) * slots), cot_shape, [], matmul // 4, 4 * size,
            onehot, *returned, cpart0, other,
        )
    return (
        cot[None],
        grad_node[None],
        grad_agg[None],
        grad_out[None],
        grad_bias,
        grad_gain,
    )


def solution(mesh):
    placed = (
        P("segment", None, ("grp", "dom"), None),
        P(None, ("grp", "dom"), None),
        P("segment", None, None),
        P("segment", None, None),
        P("segment", None, None),
        P("segment", None),
        P("segment", None),
        P("dom", None, None),
        P("dom", None, None),
        P("dom"),
        P("dom", None, None, None),
    )
    return jax.shard_map(
        body,
        mesh=mesh,
        in_specs=placed,
        out_specs=(
            P("segment", None, ("grp", "dom"), None),
            P("segment", ("grp", "dom"), None),
            P("segment", ("grp", "dom"), None),
            P("segment", ("grp", "dom"), None),
            P("segment", "grp"),
            P("segment", "grp"),
        ),
        check_vma=False,
    )
```

```python
import functools

import jax
import jax.numpy as jnp
from jax import lax
from jax.experimental import pallas as pl
from jax.experimental.pallas import tpu as pltpu
from jax.sharding import PartitionSpec as P

EPSILON = 1e-05
F32 = jnp.float32
BF16 = jnp.bfloat16
VMEM = pl.BlockSpec(memory_space=pltpu.VMEM)
SMEM = pl.BlockSpec(memory_space=pltpu.SMEM)
HBM = pl.BlockSpec(memory_space=pltpu.HBM)
ANY = pl.BlockSpec(memory_space=pl.ANY)
PEERS = 4
EXTRA = 8
PIECE = 64


def nn_dot(a, b):
    return jnp.dot(a, b, preferred_element_type=F32)


def nt_dot(a, b):
    return lax.dot_general(a, b, (((1,), (1,)), ((), ())), preferred_element_type=F32)


def tn_dot(a, b):
    return lax.dot_general(a, b, (((0,), (0,)), ((), ())), preferred_element_type=F32)


def shape(dims, dtype):
    return jax.ShapeDtypeStruct(dims, dtype)


def call(kernel, outs, scratch, flops, byts, *args, scalars=0, raw=0, after=0):
    blocks = len(args) - scalars - raw - after
    args = list(args)
    for i in range(scalars, scalars + raw):
        args[i] = pltpu.with_memory_space_constraint(args[i], pltpu.HBM)
    return pl.pallas_call(
        kernel,
        out_shape=outs,
        in_specs=[SMEM] * scalars + [HBM] * raw + [VMEM] * blocks + [ANY] * after,
        out_specs=jax.tree.map(lambda _: VMEM, outs),
        scratch_shapes=scratch,
        compiler_params=pltpu.CompilerParams(vmem_limit_bytes=24 * 1024 * 1024),
        cost_estimate=pl.CostEstimate(flops=flops, bytes_accessed=byts, transcendentals=0),
    )(*args)


def on_core(core):
    return pl.when(lax.axis_index("segment") == core)


def two_dot(pair_ref, b):
    return nn_dot(pair_ref[0], b) + nn_dot(pair_ref[1], b)


def dom_bit(i):
    return (lax.axis_index("dom") >> i) & 1


def sent_slots():
    x, z = dom_bit(0), dom_bit(1)
    return x, 1 - x, 2 + z, 3 - z


def read_slots():
    x, z = dom_bit(0), dom_bit(1)
    return 1 - x, x, 3 - z, 2 + z


def target_onehot(targets_ref, rows):
    ids = jnp.concatenate([targets_ref[0, pl.ds(s, 1), :] for s in sent_slots()], 1)
    return (lax.broadcasted_iota(jnp.int32, (rows, ids.shape[1]), 0) == ids).astype(BF16)


def gather_kernel(targets_hbm, x_hbm, o0, o1, o2, o3, x_ref, onehot_ref, targets_ref, sems):
    copies = [
        pltpu.make_async_copy(targets_hbm, targets_ref, sems.at[0]),
        pltpu.make_async_copy(x_hbm, x_ref, sems.at[1]),
    ]
    for c in copies:
        c.start()
    micro, rows, _ = x_ref.shape
    per_peer = o0.shape[0] // micro
    copies[0].wait()
    onehot = target_onehot(targets_ref, rows)
    onehot_ref[...] = onehot
    copies[1].wait()
    for m in range(micro):
        picked = tn_dot(onehot, x_ref[m]).astype(BF16)
        for k, out in enumerate((o0, o1, o2, o3)):
            out[m * per_peer : (m + 1) * per_peer, :] = picked[k * per_peer : (k + 1) * per_peer]


def node_kernel(
    pairs_ref, count_ref, values_hbm, w_hbm, bias_hbm, w_agg_hbm, w_out_hbm, gain_hbm, g_hbm, x_ref,
    z_ref, acc_ref, halo_in_ref, local_back_ref, halo_back_ref, w_ref, w_agg_ref, w_out_ref, gain_ref,
    g_ref,
    values_ref, src_ref, bias_ref, dense_ref, local_ref, sems,
):
    copies = [
        pltpu.make_async_copy(a, b, sems.at[i])
        for i, (a, b) in enumerate(
            (
                (values_hbm, values_ref), (w_hbm, w_ref), (bias_hbm, bias_ref),
                (w_agg_hbm, w_agg_ref), (w_out_hbm, w_out_ref), (gain_hbm, gain_ref), (g_hbm, g_ref),
            )
        )
    ]
    for c in copies:
        c.start()
    micro, rows, feat = x_ref.shape
    row_blocks, blocks = dense_ref.shape[:2]
    for m in range(micro):
        src_ref[:, m * feat : (m + 1) * feat] = x_ref[m]
    dense_ref[...] = jnp.zeros_like(dense_ref)
    copies[0].wait()
    for k in range(values_ref.shape[0]):

        @pl.when(k < count_ref[0])
        def _():
            dense_ref[pairs_ref[0, 0, k], pairs_ref[0, 1, k]] += values_ref[k].astype(F32)

    copies[1].wait()
    copies[2].wait()
    for m in range(micro):
        z_ref[m * rows : (m + 1) * rows, :] = nn_dot(x_ref[m], w_ref[...]) + bias_ref[
            ...
        ].astype(F32)
    for d in range(row_blocks):
        down = slice(d * 128, (d + 1) * 128)
        for c in range(blocks):
            block = dense_ref[d, c]
            high = block.astype(BF16)
            for i, v in enumerate((high, (block - high.astype(F32)).astype(BF16))):
                if c < row_blocks:
                    across_to = slice(c * 128, (c + 1) * 128)
                    local_ref[i, down, across_to] = v
                    local_back_ref[i, across_to, down] = v.T
                else:
                    halo_in_ref[i, down, :] = v
                    halo_back_ref[i, :, down] = v.T
    acc_ref[...] = two_dot(local_ref, src_ref[...])
    for c in copies[3:]:
        c.wait()


def pieces(part):
    return [slice(r, r + PIECE) for r in range(part.start, part.stop, PIECE)]


def row_mean(v):
    return jnp.mean(v, axis=1, keepdims=True)


def norm_back(g, normed, inv_std, gain):
    e = g * gain
    return (inv_std * (e - row_mean(e) - normed * row_mean(e * normed))).astype(BF16)


def parts_of(total, micro):
    rows = total // micro
    return [slice(m * rows, (m + 1) * rows) for m in range(micro)]


def put_halo_grads(t_ref, outs):
    feat = outs[0].shape[1]
    per_peer = outs[0].shape[0] // 2
    for slot, out in zip(read_slots(), outs):
        for m in range(2):
            at = pl.ds(pl.multiple_of(slot * per_peer, per_peer), per_peer)
            out[m * per_peer : (m + 1) * per_peer, :] = t_ref[
                at, m * feat : (m + 1) * feat
            ].astype(BF16)


def first_kernel(
    h0, h1, h2, h3, halo_in_ref, halo_back_ref, z_ref, acc_ref, g_ref, w_agg_ref, w_out_ref, gain_ref, _,
    o0, o1, o2, o3, both_ref, dact_ref, normed_ref, inv_ref, agg_ref, hidden_ref, gpn_ref,
    gpre_ref, sums_ref,
    src_ref, s0_ref, t_ref,
):
    micro, rows, feat = g_ref.shape
    per_peer = h0.shape[0] // micro
    for slot, h in zip(read_slots(), (h0, h1, h2, h3)):
        for m in range(micro):
            at = pl.ds(pl.multiple_of(slot * per_peer, per_peer), per_peer)
            src_ref[at, m * feat : (m + 1) * feat] = h[m * per_peer : (m + 1) * per_peer, :]
    gain = gain_ref[...].astype(F32)
    parts = parts_of(micro * rows, micro)
    for m, part in enumerate(parts):
        cols = slice(m * feat, (m + 1) * feat)
        agg_ref[part, :] = (acc_ref[:, cols] + two_dot(halo_in_ref, src_ref[:, cols])).astype(BF16)
    for part in parts:
        s0_ref[part, :] = nn_dot(agg_ref[part, :], w_agg_ref[...])
    for part in parts:
        for at in pieces(part):
            preact = z_ref[at, :] + s0_ref[at, :]
            sig = 1.0 / (1.0 + jnp.exp(-preact))
            hidden_ref[at, :] = (preact * sig).astype(BF16)
            dact_ref[at, :] = sig * (1.0 + preact * (1.0 - sig))
    for part in parts:
        s0_ref[part, :] = nn_dot(hidden_ref[part, :], w_out_ref[...])
    def normalize(at):
        output = s0_ref[at, :]
        centred = output - row_mean(output)
        inv_std = lax.rsqrt(row_mean(centred * centred) + EPSILON)
        normed = centred * inv_std
        normed_ref[at, :] = normed
        inv_ref[at, :] = jnp.broadcast_to(inv_std, (PIECE, 128))
        return normed, inv_std

    @on_core(0)
    def _():
        for part in parts:
            for at in pieces(part):
                normalize(at)

    @on_core(1)
    def _():
        gain_sum = jnp.zeros((1, feat), F32)
        for m, part in enumerate(parts):
            for at in pieces(part):
                normed, inv_std = normalize(at)
                g = g_ref[m, at.start - part.start : at.stop - part.start, :].astype(F32)
                gpn_ref[at, :] = norm_back(g, normed, inv_std, gain)
                gain_sum += jnp.sum(g * normed, axis=0, keepdims=True)
        for part in parts:
            s0_ref[part, :] = nt_dot(gpn_ref[part, :], w_out_ref[...])
        bias_sum = jnp.zeros((1, feat), F32)
        for part in parts:
            for at in pieces(part):
                gpre = (s0_ref[at, :] * dact_ref[at, :]).astype(BF16)
                gpre_ref[at, :] = gpre
                bias_sum += jnp.sum(gpre.astype(F32), axis=0, keepdims=True)
        for m, part in enumerate(parts):
            cols = slice(m * feat, (m + 1) * feat)
            gm = nt_dot(gpre_ref[part, :], w_agg_ref[...]).astype(BF16)
            both_ref[:rows, cols] = gm
            both_ref[rows:, cols] = gpre_ref[part, :]
            t_ref[:, cols] = two_dot(halo_back_ref, gm)
        put_halo_grads(t_ref, (o0, o1, o2, o3))
        sums_ref[...] = jnp.concatenate([bias_sum, gain_sum, jnp.zeros((EXTRA - 2, feat), F32)], 0)


def lower_kernel(g_ref, gpre_ref, gm_ref, back_ref, w_node_ref, cpart_ref, g_out):
    feat = g_ref.shape[1]

    @on_core(0)
    def _():
        g_out[...] = g_ref[...]
        for m, part in enumerate(parts_of(g_ref.shape[0], 2)):
            back = nt_dot(gpre_ref[part, :], w_node_ref[...])
            spread = two_dot(back_ref, gm_ref[:, m * feat : (m + 1) * feat])
            cpart_ref[part, :] = g_ref[part, :].astype(F32) + back + spread


def upper_kernel(g_ref, both_ref, back_ref, w_node_ref, cpart_ref):
    micro, rows, feat = g_ref.shape

    @on_core(0)
    def _():
        for m, part in enumerate(parts_of(micro * rows, micro)):
            cols = slice(m * feat, (m + 1) * feat)
            back = nt_dot(both_ref[rows:, cols], w_node_ref[...])
            spread = two_dot(back_ref, both_ref[:rows, cols])
            cpart_ref[part, :] = g_ref[m].astype(F32) + back + spread


def first_bit():
    return (lax.axis_index("dom") >> (1 - lax.axis_index("segment"))) & 1


def second_bit():
    return (lax.axis_index("dom") >> lax.axis_index("segment")) & 1


def chunk_order(chunks):
    core = lax.axis_index("segment")
    low = [d for d in range(chunks) if not d & 2]
    high = [d for d in range(chunks) if not d & 1]
    starts = [a + core * (b - a) for a, b in zip(low, high)]
    step, mine = 2 - core, first_bit()
    return [d + mine * step for d in starts] + [d + (1 - mine) * step for d in starts]


def weight_products(la_ref, lb_ref, gpre_ref, gpn_ref, sums, keep_ref, send_ref):
    n, rows, feat = keep_ref.shape
    share = (rows - EXTRA) // 3
    for base in (n, 0):
        a = nn_dot(la_ref[base * 2 * share : (base + n) * 2 * share, :], gpre_ref[...])
        b = nn_dot(lb_ref[base * share : (base + n) * share, :], gpn_ref[...])
        for i in range(n):
            for lo, v in (
                (0, a[i * 2 * share : (i + 1) * 2 * share]),
                (2 * share, b[i * share : (i + 1) * share]),
                (3 * share, sums),
            ):
                if base:
                    at = i * rows + lo
                    send_ref[at : at + v.shape[0], :] = v.astype(BF16)
                else:
                    keep_ref[i, lo : lo + v.shape[0], :] = v


def turn_kernel(
    chunks, x_ref, agg_ref, hidden_ref, gpre_ref, gpn_ref, sums_ref, la_ref, lb_ref,
    keep_ref, send_ref, turned_ref,
):
    micro, rows, feat = x_ref.shape
    share = feat // chunks
    for m in range(micro):
        turned_ref[:, m * rows : (m + 1) * rows] = x_ref[m].T
    places = [
        pl.ds(pl.multiple_of(d * share, share), share) for d in chunk_order(chunks)
    ]
    for i, at in enumerate(places):
        la_ref[2 * i * share : (2 * i + 1) * share, :] = turned_ref[at, :]
    turned_ref[...] = agg_ref[...].T
    for i, at in enumerate(places):
        la_ref[(2 * i + 1) * share : (2 * i + 2) * share, :] = turned_ref[at, :]
    turned_ref[...] = hidden_ref[...].T
    for i, at in enumerate(places):
        lb_ref[i * share : (i + 1) * share, :] = turned_ref[at, :]

    @on_core(1)
    def _():
        weight_products(la_ref, lb_ref, gpre_ref, gpn_ref, sums_ref[...], keep_ref, send_ref)


def second_kernel(*refs):
    @on_core(0)
    def _():
        second_layer(*refs)


def second_layer(
    onehot_ref, r0, r1, r2, r3, cin_ref, dact_ref, normed_ref, inv_ref, w_out_ref, gain_ref,
    g_ref, gpn_ref, gpre_ref, sums_ref, s0_ref,
):
    total, feat = dact_ref.shape
    parts = parts_of(total, 2)
    per_peer = r0.shape[0] // 2
    gain = gain_ref[...].astype(F32)
    for m, part in enumerate(parts):
        ret = jnp.concatenate([r[m * per_peer : (m + 1) * per_peer, :] for r in (r0, r1, r2, r3)], 0)
        s0_ref[part, :] = nn_dot(onehot_ref[...], ret)
    gain_sum = jnp.zeros((1, feat), F32)
    for part in parts:
        for at in pieces(part):
            g16 = (cin_ref[at, :] + s0_ref[at, :]).astype(BF16)
            g_ref[at, :] = g16
            g = g16.astype(F32)
            normed = normed_ref[at, :]
            gpn_ref[at, :] = norm_back(g, normed, inv_ref[at, 0:1], gain)
            gain_sum += jnp.sum(g * normed, axis=0, keepdims=True)
    for part in parts:
        s0_ref[part, :] = nt_dot(gpn_ref[part, :], w_out_ref[...])
    bias_sum = jnp.zeros((1, feat), F32)
    for part in parts:
        for at in pieces(part):
            gpre = (s0_ref[at, :] * dact_ref[at, :]).astype(BF16)
            gpre_ref[at, :] = gpre
            bias_sum += jnp.sum(gpre.astype(F32), axis=0, keepdims=True)
    sums_ref[...] = jnp.concatenate([bias_sum, gain_sum, jnp.zeros((EXTRA - 2, feat), F32)], 0)


def message_grads(gpre_ref, back_ref, w_agg_ref, gm_ref, t_ref):
    total, feat = gpre_ref.shape
    for m, part in enumerate(parts_of(total, 2)):
        cols = slice(m * feat, (m + 1) * feat)
        gm = nt_dot(gpre_ref[part, :], w_agg_ref[...]).astype(BF16)
        gm_ref[:, cols] = gm
        t_ref[:, cols] = two_dot(back_ref, gm)


def third_kernel(
    gpre_ref, gpn_ref, sums_ref, back_ref, w_agg_ref, la_ref, lb_ref, keep1_ref, send1_ref,
    keep_ref, send_ref, near_ref, far_ref, gm_ref, t_ref,
):
    ride = near_ref.shape[0]
    first = send1_ref.shape[0]

    @on_core(0)
    def _():
        weight_products(la_ref, lb_ref, gpre_ref, gpn_ref, sums_ref[...], keep_ref, send_ref)
        message_grads(gpre_ref, back_ref, w_agg_ref, gm_ref, t_ref)
        below, cross = (send_ref.at[pl.ds(first + i * ride, ride), :] for i in (0, 1))
        put_halo_grads(t_ref, (near_ref, cross, below, far_ref.at[pl.ds(0, ride), :]))
        far_ref[ride:, :] = send_ref[first + ride :, :]

    @on_core(1)
    def _():
        keep_ref[...] = keep1_ref[...]
        send_ref[:first, :] = send1_ref[...]


def plain_third_kernel(gpre_ref, back_ref, w_agg_ref, o0, o1, o2, o3, gm_ref, t_ref):
    message_grads(gpre_ref, back_ref, w_agg_ref, gm_ref, t_ref)
    put_halo_grads(t_ref, (o0, o1, o2, o3))


def halve_job(mine, keep, recv, keep2, send2):
    n, rows, _ = keep2.shape
    for i in range(n):
        d, o = 2 * i + mine, 2 * i + 1 - mine
        at = pl.ds(pl.multiple_of(o * rows, 8), rows)
        send2[i * rows : (i + 1) * rows, :] = (keep[o] + recv[at, :].astype(F32)).astype(BF16)
        at = pl.ds(pl.multiple_of(d * rows, 8), rows)
        keep2[i] = keep[d] + recv[at, :].astype(F32)


def carry_kernel(keep, recv, near_ref, _, keep2, send2):
    ride = near_ref.shape[0]
    halve_job(second_bit(), keep, recv, keep2, send2)
    at = keep2.shape[0] * keep2.shape[1]

    @on_core(0)
    def _():
        send2[at : at + ride, :] = near_ref[...]
        send2[at + ride :, :] = recv[recv.shape[0] - ride :, :]


def halve_kernel(keep, recv, _, keep2, send2):
    halve_job(dom_bit(2), keep, recv, keep2, send2)


def sums_out(keep, recv, node_ref, agg_ref, out_ref, bias_ref, gain_ref):
    share = node_ref.shape[0]
    total = keep[0] + recv[...].astype(F32)
    node_ref[...] = total[0:share]
    agg_ref[...] = total[share : 2 * share]
    out_ref[...] = total[2 * share : 3 * share]
    bias_ref[...] = total[3 * share : 3 * share + 1]
    gain_ref[...] = total[3 * share + 1 : 3 * share + 2]


def cot_out(skips, onehot_ref, sources, cpart_ref, other_ref, cot_ref):
    micro, rows, feat = cot_ref.shape
    n = onehot_ref.shape[1] // PEERS
    inner = dom_bit(0) != dom_bit(1)

    @on_core(1)
    def _():
        for m in range(micro):
            cot_ref[m] = other_ref[m * rows : (m + 1) * rows, :]

    @on_core(0)
    def _():
        for m in range(micro):
            got = [r[s + m * n : s + (m + 1) * n, :] for r, s in zip(sources, skips)]
            if len(got) > PEERS:
                got[1] = jnp.where(inner, got[1], got.pop())
            ret = jnp.concatenate(got, 0)
            cot_ref[m] = (
                cpart_ref[m * rows : (m + 1) * rows, :] + nn_dot(onehot_ref[...], ret)
            ).astype(BF16)


def final_kernel(skips, onehot_ref, *rest):
    *sources, cpart_ref, other_ref, keep, recv, cot_ref, node_ref, agg_ref, out_ref, bias_ref, gain_ref = rest
    cot_out(skips, onehot_ref, sources, cpart_ref, other_ref, cot_ref)
    sums_out(keep, recv, node_ref, agg_ref, out_ref, bias_ref, gain_ref)


def cot_kernel(skips, onehot_ref, *rest):
    *sources, cpart_ref, other_ref, cot_ref = rest
    cot_out(skips, onehot_ref, sources, cpart_ref, other_ref, cot_ref)


def whole_kernel(x_ref, agg_ref, hidden_ref, gpn_ref, gpre_ref, node_ref, agg_out, out_ref):
    rows = x_ref.shape[1]
    gpre = gpre_ref[...]
    node_ref[...] = tn_dot(x_ref[0], gpre[:rows]) + tn_dot(x_ref[1], gpre[rows:])
    agg_out[...] = tn_dot(agg_ref[...], gpre)
    out_ref[...] = tn_dot(hidden_ref[...], gpn_ref[...])


def body(
    section_inputs,
    out_cot,
    w_node,
    w_agg,
    w_out,
    bias,
    gain,
    send_rows,
    blk_pairs,
    blk_count,
    blk_values,
):
    peers = lax.axis_size("dom")
    segment = lax.axis_index("segment")
    assert lax.axis_size("segment") == 2 and peers % 4 == 0
    x = section_inputs[0]
    micro, rows, feat = x.shape
    _, slots, per_peer = send_rows.shape
    assert slots * per_peer == 128 and slots == PEERS and micro == 2
    total = micro * rows
    values = blk_values[0]
    row_blocks = rows // 128
    wide = micro * feat
    w_n, w_a, w_o = w_node[0], w_agg[0], w_out[0]
    matmul = 2 * total * feat * feat
    size = total * feat
    chunk = shape((micro * per_peer, feat), BF16)

    def swap_partner(p, k):
        if k == 0:
            return p ^ 1
        if k == 1:
            return (p + 1 if p & 1 else p - 1) % peers
        up = (p >> 1) & 1
        return (p + 2 if up == (k == 3) else p - 2) % peers

    def swapped(v, k, cores):
        return lax.ppermute(
            v,
            ("dom", "segment"),
            [(2 * p + s, 2 * swap_partner(p, k) + d) for p in range(peers) for s, d in cores],
        )

    def across(v):
        return lax.ppermute(v, "segment", [(0, 1), (1, 0)])

    def flipped(v, bits):
        return lax.ppermute(
            v,
            ("dom", "segment"),
            [(2 * p + s, 2 * (p ^ (1 << bits[s])) + s) for p in range(peers) for s in (0, 1)],
        )

    f_full, b_full = shape((total, feat), F32), shape((total, feat), BF16)
    s_sums = shape((EXTRA, feat), F32)
    dma = pltpu.SemaphoreType.DMA
    *outgoing, x, onehot = call(
        gather_kernel,
        [chunk] * slots + [shape(x.shape, BF16), shape((rows, slots * per_peer), BF16)],
        [pltpu.VMEM(send_rows.shape, jnp.int32), dma((2,))],
        matmul // 8, 2 * size, send_rows, x,
        raw=2,
    )
    same, other_core = ((0, 0), (1, 1)), ((0, 1), (1, 0))
    w_other = across(w_n)
    halos = [swapped(v, k, same) for k, v in enumerate(outgoing)]
    halo_rows = slots * per_peer
    loaded = (w_n, w_a, w_o, gain, out_cot)
    z, acc, halo_in, local_back, halo_back, w_n, w_a, w_o, gain, g_last = call(
        node_kernel,
        [f_full, shape((rows, wide), F32), shape((2, rows, halo_rows), BF16)]
        + [shape((2, rows, rows), BF16), shape((2, halo_rows, rows), BF16)]
        + [shape(v.shape, BF16) for v in loaded],
        [
            pltpu.VMEM(values.shape, BF16), pltpu.VMEM((rows, wide), BF16), pltpu.VMEM(bias.shape, BF16),
            pltpu.VMEM((row_blocks, row_blocks + 1, 128, 128), F32), pltpu.VMEM((2, rows, rows), BF16),
            dma((7,)),
        ],
        2 * matmul, 8 * size,
        blk_pairs, blk_count, values, w_n, bias, w_a, w_o, gain, out_cot, x,
        scalars=2, raw=7,
    )
    first = call(
        first_kernel,
        [chunk] * slots
        + [shape((2 * rows, wide), BF16), f_full, f_full, shape((total, 128), F32)]
        + [b_full] * 4 + [s_sums],
        [
            pltpu.VMEM((halo_rows, wide), BF16),
            pltpu.VMEM((total, feat), F32),
            pltpu.VMEM((halo_rows, wide), F32),
        ],
        4 * matmul, 20 * size,
        *halos, halo_in, halo_back, z, acc, g_last, w_a, w_o, gain, w_other,
        after=1,
    )
    to_return = first[:slots]
    both, dact, normed, inv_std, agg, hidden, gpn1, gpre1, sums1 = first[slots:]
    returned = [swapped(v, k, other_core) for k, v in enumerate(to_return)]
    c_in = call(
        upper_kernel, f_full, [], matmul, 10 * size, g_last, across(both), local_back, w_other
    )
    share = feat // peers
    rows_each = 3 * share + EXTRA
    halving = peers == 8

    def kept(n, extra=0):
        return [shape((n, rows_each, feat), F32), shape((n * rows_each + extra, feat), BF16)]

    if halving:
        turned = call(
            functools.partial(turn_kernel, peers),
            [shape((16 * share, total), BF16), shape((8 * share, total), BF16)] + kept(4),
            [pltpu.VMEM((feat, total), BF16)],
            3 * matmul, 20 * size,
            x, agg, hidden, gpre1, gpn1, sums1,
        )
    g_low, gpn, gpre, sums = call(
        second_kernel,
        [b_full, b_full, b_full, s_sums],
        [pltpu.VMEM((total, feat), F32)],
        2 * matmul, 16 * size,
        onehot, *returned, c_in, dact, normed, inv_std, w_o, gain,
    )
    scr_t, gm_out = pltpu.VMEM((halo_rows, wide), F32), shape((rows, wide), BF16)
    if halving:
        ride = chunk.shape[0]
        ride = chunk.shape[0]
        keep, send, near, far, gm = call(
            third_kernel,
            kept(4, 2 * ride) + [chunk, shape((2 * ride, feat), BF16), gm_out],
            [scr_t], 4 * matmul, 16 * size,
            gpre, gpn, sums, halo_back, w_a, *turned,
        )
        recv = flipped(send, (1, 0))
        far = swapped(far, 3, ((0, 0),))
    else:
        *to_return, gm = call(
            plain_third_kernel, [chunk] * slots + [gm_out], [scr_t],
            2 * matmul, 8 * size, gpre, halo_back, w_a,
        )
    cpart0, g_low = call(
        lower_kernel, [f_full, b_full], [], matmul, 10 * size, g_low, gpre, gm, local_back, w_n
    )
    other = across(g_low)
    cot_shape = shape((micro, rows, feat), BF16)
    if halving:
        up = recv
        keep, send = call(
            carry_kernel, kept(2, 2 * ride), [], size, 8 * size, keep, recv, near, cpart0,
            after=1,
        )
        recv = flipped(send, (0, 1))
        hop = swapped(far, 0, ((0, 0),))
        first = 2 * rows_each
        returned = (recv, recv, up, far, hop)
        skips = (first, first + ride, 2 * first, 0, ride)
        keep, send = call(
            halve_kernel, kept(1), [], size, 4 * size, keep, recv, far,
            after=1,
        )
        recv = flipped(send, (2, 2))
        part, row = shape((share, feat), F32), shape((1, feat), F32)
        cot, grad_node, grad_agg, grad_out, grad_bias, grad_gain = call(
            functools.partial(final_kernel, skips), [cot_shape, part, part, part, row, row],
            [], matmul // 4, 6 * size,
            onehot, *returned, cpart0, other, keep, recv,
        )
    else:
        is_last = segment == 1
        gpn, gpre = jnp.where(is_last, gpn1, gpn), jnp.where(is_last, gpre1, gpre)
        sums = jnp.where(is_last, sums1, sums)
        square = shape((feat, feat), F32)
        full = call(
            whole_kernel, [square] * 3, [], 3 * matmul, 12 * size, x, agg, hidden, gpn, gpre
        )
        grad_node, grad_agg, grad_out = [
            lax.psum_scatter(v, "dom", scatter_dimension=0, tiled=True) for v in full
        ]
        sums = lax.psum(sums, "dom")
        grad_bias, grad_gain = sums[0:1], sums[1:2]
        returned = [swapped(v, k, ((0, 0),)) for k, v in enumerate(to_return)]
        cot = call(
            functools.partial(cot_kernel, (0,) * slots), cot_shape, [], matmul // 4, 4 * size,
            onehot, *returned, cpart0, other,
        )
    return (
        cot[None],
        grad_node[None],
        grad_agg[None],
        grad_out[None],
        grad_bias,
        grad_gain,
    )


def solution(mesh):
    placed = (
        P("segment", None, ("grp", "dom"), None),
        P(None, ("grp", "dom"), None),
        P("segment", None, None),
        P("segment", None, None),
        P("segment", None, None),
        P("segment", None),
        P("segment", None),
        P("dom", None, None),
        P("dom", None, None),
        P("dom"),
        P("dom", None, None, None),
    )
    return jax.shard_map(
        body,
        mesh=mesh,
        in_specs=placed,
        out_specs=(
            P("segment", None, ("grp", "dom"), None),
            P("segment", ("grp", "dom"), None),
            P("segment", ("grp", "dom"), None),
            P("segment", ("grp", "dom"), None),
            P("segment", "grp"),
            P("segment", "grp"),
        ),
        check_vma=False,
    )
```

```python
import functools

import jax
import jax.numpy as jnp
from jax import lax
from jax.experimental import pallas as pl
from jax.experimental.pallas import tpu as pltpu
from jax.sharding import PartitionSpec as P

EPSILON = 1e-05
F32 = jnp.float32
BF16 = jnp.bfloat16
VMEM = pl.BlockSpec(memory_space=pltpu.VMEM)
SMEM = pl.BlockSpec(memory_space=pltpu.SMEM)
HBM = pl.BlockSpec(memory_space=pltpu.HBM)
ANY = pl.BlockSpec(memory_space=pl.ANY)
PEERS = 4
EXTRA = 8
PIECE = 64


def nn_dot(a, b):
    return jnp.dot(a, b, preferred_element_type=F32)


def nt_dot(a, b):
    return lax.dot_general(a, b, (((1,), (1,)), ((), ())), preferred_element_type=F32)


def tn_dot(a, b):
    return lax.dot_general(a, b, (((0,), (0,)), ((), ())), preferred_element_type=F32)


def shape(dims, dtype):
    return jax.ShapeDtypeStruct(dims, dtype)


def call(kernel, outs, scratch, flops, byts, *args, scalars=0, raw=0, after=0):
    blocks = len(args) - scalars - raw - after
    args = list(args)
    for i in range(scalars, scalars + raw):
        args[i] = pltpu.with_memory_space_constraint(args[i], pltpu.HBM)
    return pl.pallas_call(
        kernel,
        out_shape=outs,
        in_specs=[SMEM] * scalars + [HBM] * raw + [VMEM] * blocks + [ANY] * after,
        out_specs=jax.tree.map(lambda _: VMEM, outs),
        scratch_shapes=scratch,
        compiler_params=pltpu.CompilerParams(vmem_limit_bytes=24 * 1024 * 1024),
        cost_estimate=pl.CostEstimate(flops=flops, bytes_accessed=byts, transcendentals=0),
    )(*args)


def on_core(core):
    return pl.when(lax.axis_index("segment") == core)


def two_dot(pair_ref, b):
    return nn_dot(pair_ref[0], b) + nn_dot(pair_ref[1], b)


def dom_bit(i):
    return (lax.axis_index("dom") >> i) & 1


def sent_slots():
    x, z = dom_bit(0), dom_bit(1)
    return x, 1 - x, 2 + z, 3 - z


def read_slots():
    x, z = dom_bit(0), dom_bit(1)
    return 1 - x, x, 3 - z, 2 + z


def target_onehot(targets_ref, rows):
    ids = jnp.concatenate([targets_ref[0, pl.ds(s, 1), :] for s in sent_slots()], 1)
    return (lax.broadcasted_iota(jnp.int32, (rows, ids.shape[1]), 0) == ids).astype(BF16)


def gather_kernel(targets_hbm, x_hbm, o0, o1, o2, o3, x_ref, onehot_ref, targets_ref, sems):
    copies = [
        pltpu.make_async_copy(targets_hbm, targets_ref, sems.at[0]),
        pltpu.make_async_copy(x_hbm, x_ref, sems.at[1]),
    ]
    for c in copies:
        c.start()
    micro, rows, _ = x_ref.shape
    per_peer = o0.shape[0] // micro
    copies[0].wait()
    onehot = target_onehot(targets_ref, rows)
    onehot_ref[...] = onehot
    copies[1].wait()
    for m in range(micro):
        picked = tn_dot(onehot, x_ref[m]).astype(BF16)
        for k, out in enumerate((o0, o1, o2, o3)):
            out[m * per_peer : (m + 1) * per_peer, :] = picked[k * per_peer : (k + 1) * per_peer]


def node_kernel(
    pairs_ref, count_ref, values_hbm, w_hbm, bias_hbm, w_agg_hbm, w_out_hbm, gain_hbm, g_hbm, x_ref,
    z_ref, acc_ref, halo_in_ref, local_back_ref, halo_back_ref, w_ref, w_agg_ref, w_out_ref, gain_ref,
    g_ref,
    values_ref, src_ref, bias_ref, dense_ref, local_ref, sems,
):
    copies = [
        pltpu.make_async_copy(a, b, sems.at[i])
        for i, (a, b) in enumerate(
            (
                (values_hbm, values_ref), (w_hbm, w_ref), (bias_hbm, bias_ref),
                (w_agg_hbm, w_agg_ref), (w_out_hbm, w_out_ref), (gain_hbm, gain_ref), (g_hbm, g_ref),
            )
        )
    ]
    for c in copies:
        c.start()
    micro, rows, feat = x_ref.shape
    row_blocks, blocks = dense_ref.shape[:2]
    for m in range(micro):
        src_ref[:, m * feat : (m + 1) * feat] = x_ref[m]
    dense_ref[...] = jnp.zeros_like(dense_ref)
    copies[0].wait()
    for k in range(values_ref.shape[0]):

        @pl.when(k < count_ref[0])
        def _():
            dense_ref[pairs_ref[0, 0, k], pairs_ref[0, 1, k]] += values_ref[k].astype(F32)

    copies[1].wait()
    copies[2].wait()
    for m in range(micro):
        z_ref[m * rows : (m + 1) * rows, :] = nn_dot(x_ref[m], w_ref[...]) + bias_ref[
            ...
        ].astype(F32)
    for d in range(row_blocks):
        down = slice(d * 128, (d + 1) * 128)
        for c in range(blocks):
            block = dense_ref[d, c]
            high = block.astype(BF16)
            for i, v in enumerate((high, (block - high.astype(F32)).astype(BF16))):
                if c < row_blocks:
                    across_to = slice(c * 128, (c + 1) * 128)
                    local_ref[i, down, across_to] = v
                    local_back_ref[i, across_to, down] = v.T
                else:
                    halo_in_ref[i, down, :] = v
                    halo_back_ref[i, :, down] = v.T
    acc_ref[...] = two_dot(local_ref, src_ref[...])
    for c in copies[3:]:
        c.wait()


def pieces(part):
    return [slice(r, r + PIECE) for r in range(part.start, part.stop, PIECE)]


def row_mean(v):
    return jnp.mean(v, axis=1, keepdims=True)


def norm_back(g, normed, inv_std, gain):
    e = g * gain
    return (inv_std * (e - row_mean(e) - normed * row_mean(e * normed))).astype(BF16)


def parts_of(total, micro):
    rows = total // micro
    return [slice(m * rows, (m + 1) * rows) for m in range(micro)]


def put_halo_grads(t_ref, outs):
    feat = outs[0].shape[1]
    per_peer = outs[0].shape[0] // 2
    for slot, out in zip(read_slots(), outs):
        for m in range(2):
            at = pl.ds(pl.multiple_of(slot * per_peer, per_peer), per_peer)
            out[m * per_peer : (m + 1) * per_peer, :] = t_ref[
                at, m * feat : (m + 1) * feat
            ].astype(BF16)


def first_kernel(
    h0, h1, h2, h3, halo_in_ref, halo_back_ref, z_ref, acc_ref, g_ref, w_agg_ref, w_out_ref, gain_ref, _,
    o0, o1, o2, o3, both_ref, dact_ref, normed_ref, inv_ref, agg_ref, hidden_ref, gpn_ref,
    gpre_ref, sums_ref,
    src_ref, s0_ref, t_ref,
):
    micro, rows, feat = g_ref.shape
    per_peer = h0.shape[0] // micro
    for slot, h in zip(read_slots(), (h0, h1, h2, h3)):
        for m in range(micro):
            at = pl.ds(pl.multiple_of(slot * per_peer, per_peer), per_peer)
            src_ref[at, m * feat : (m + 1) * feat] = h[m * per_peer : (m + 1) * per_peer, :]
    gain = gain_ref[...].astype(F32)
    parts = parts_of(micro * rows, micro)
    for m, part in enumerate(parts):
        cols = slice(m * feat, (m + 1) * feat)
        agg_ref[part, :] = (acc_ref[:, cols] + two_dot(halo_in_ref, src_ref[:, cols])).astype(BF16)
    for part in parts:
        s0_ref[part, :] = nn_dot(agg_ref[part, :], w_agg_ref[...])
    for part in parts:
        for at in pieces(part):
            preact = z_ref[at, :] + s0_ref[at, :]
            sig = 1.0 / (1.0 + jnp.exp(-preact))
            hidden_ref[at, :] = (preact * sig).astype(BF16)
            dact_ref[at, :] = sig * (1.0 + preact * (1.0 - sig))
    for part in parts:
        s0_ref[part, :] = nn_dot(hidden_ref[part, :], w_out_ref[...])
    def normalize(at, keep):
        output = s0_ref[at, :]
        centred = output - row_mean(output)
        inv_std = lax.rsqrt(row_mean(centred * centred) + EPSILON)
        normed = centred * inv_std
        if keep:
            normed_ref[at, :] = normed
            inv_ref[at, :] = jnp.broadcast_to(inv_std, (PIECE, 128))
        return normed, inv_std

    @on_core(0)
    def _():
        for part in parts:
            for at in pieces(part):
                normalize(at, True)

    @on_core(1)
    def _():
        gain_sum = jnp.zeros((1, feat), F32)
        for m, part in enumerate(parts):
            for at in pieces(part):
                normed, inv_std = normalize(at, False)
                g = g_ref[m, at.start - part.start : at.stop - part.start, :].astype(F32)
                gpn_ref[at, :] = norm_back(g, normed, inv_std, gain)
                gain_sum += jnp.sum(g * normed, axis=0, keepdims=True)
        for part in parts:
            s0_ref[part, :] = nt_dot(gpn_ref[part, :], w_out_ref[...])
        bias_sum = jnp.zeros((1, feat), F32)
        for part in parts:
            for at in pieces(part):
                gpre = (s0_ref[at, :] * dact_ref[at, :]).astype(BF16)
                gpre_ref[at, :] = gpre
                bias_sum += jnp.sum(gpre.astype(F32), axis=0, keepdims=True)
        for m, part in enumerate(parts):
            cols = slice(m * feat, (m + 1) * feat)
            gm = nt_dot(gpre_ref[part, :], w_agg_ref[...]).astype(BF16)
            both_ref[:rows, cols] = gm
            both_ref[rows:, cols] = gpre_ref[part, :]
            t_ref[:, cols] = two_dot(halo_back_ref, gm)
        put_halo_grads(t_ref, (o0, o1, o2, o3))
        sums_ref[...] = jnp.concatenate([bias_sum, gain_sum, jnp.zeros((EXTRA - 2, feat), F32)], 0)


def lower_kernel(g_ref, gpre_ref, gm_ref, back_ref, w_node_ref, cpart_ref, g_out):
    feat = g_ref.shape[1]

    @on_core(0)
    def _():
        g_out[...] = g_ref[...]
        for m, part in enumerate(parts_of(g_ref.shape[0], 2)):
            back = nt_dot(gpre_ref[part, :], w_node_ref[...])
            spread = two_dot(back_ref, gm_ref[:, m * feat : (m + 1) * feat])
            cpart_ref[part, :] = g_ref[part, :].astype(F32) + back + spread


def upper_kernel(g_ref, both_ref, back_ref, w_node_ref, cpart_ref):
    micro, rows, feat = g_ref.shape

    @on_core(0)
    def _():
        for m, part in enumerate(parts_of(micro * rows, micro)):
            cols = slice(m * feat, (m + 1) * feat)
            back = nt_dot(both_ref[rows:, cols], w_node_ref[...])
            spread = two_dot(back_ref, both_ref[:rows, cols])
            cpart_ref[part, :] = g_ref[m].astype(F32) + back + spread


def first_bit():
    return (lax.axis_index("dom") >> (1 - lax.axis_index("segment"))) & 1


def second_bit():
    return (lax.axis_index("dom") >> lax.axis_index("segment")) & 1


def chunk_order(chunks):
    core = lax.axis_index("segment")
    low = [d for d in range(chunks) if not d & 2]
    high = [d for d in range(chunks) if not d & 1]
    starts = [a + core * (b - a) for a, b in zip(low, high)]
    step, mine = 2 - core, first_bit()
    return [d + mine * step for d in starts] + [d + (1 - mine) * step for d in starts]


def weight_products(la_ref, lb_ref, gpre_ref, gpn_ref, sums, keep_ref, send_ref):
    n, rows, feat = keep_ref.shape
    share = (rows - EXTRA) // 3
    for base in (n, 0):
        a = nn_dot(la_ref[base * 2 * share : (base + n) * 2 * share, :], gpre_ref[...])
        b = nn_dot(lb_ref[base * share : (base + n) * share, :], gpn_ref[...])
        for i in range(n):
            for lo, v in (
                (0, a[i * 2 * share : (i + 1) * 2 * share]),
                (2 * share, b[i * share : (i + 1) * share]),
                (3 * share, sums),
            ):
                if base:
                    at = i * rows + lo
                    send_ref[at : at + v.shape[0], :] = v.astype(BF16)
                else:
                    keep_ref[i, lo : lo + v.shape[0], :] = v


def turn_kernel(
    chunks, x_ref, agg_ref, hidden_ref, gpre_ref, gpn_ref, sums_ref, la_ref, lb_ref,
    keep_ref, send_ref, turned_ref,
):
    micro, rows, feat = x_ref.shape
    share = feat // chunks
    for m in range(micro):
        turned_ref[:, m * rows : (m + 1) * rows] = x_ref[m].T
    places = [
        pl.ds(pl.multiple_of(d * share, share), share) for d in chunk_order(chunks)
    ]
    for i, at in enumerate(places):
        la_ref[2 * i * share : (2 * i + 1) * share, :] = turned_ref[at, :]
    turned_ref[...] = agg_ref[...].T
    for i, at in enumerate(places):
        la_ref[(2 * i + 1) * share : (2 * i + 2) * share, :] = turned_ref[at, :]
    turned_ref[...] = hidden_ref[...].T
    for i, at in enumerate(places):
        lb_ref[i * share : (i + 1) * share, :] = turned_ref[at, :]

    @on_core(1)
    def _():
        weight_products(la_ref, lb_ref, gpre_ref, gpn_ref, sums_ref[...], keep_ref, send_ref)


def second_kernel(*refs):
    @on_core(0)
    def _():
        second_layer(*refs)


def second_layer(
    onehot_ref, r0, r1, r2, r3, cin_ref, dact_ref, normed_ref, inv_ref, w_out_ref, gain_ref,
    g_ref, gpn_ref, gpre_ref, sums_ref, s0_ref,
):
    total, feat = dact_ref.shape
    parts = parts_of(total, 2)
    per_peer = r0.shape[0] // 2
    gain = gain_ref[...].astype(F32)
    for m, part in enumerate(parts):
        ret = jnp.concatenate([r[m * per_peer : (m + 1) * per_peer, :] for r in (r0, r1, r2, r3)], 0)
        s0_ref[part, :] = nn_dot(onehot_ref[...], ret)
    gain_sum = jnp.zeros((1, feat), F32)
    for part in parts:
        for at in pieces(part):
            g16 = (cin_ref[at, :] + s0_ref[at, :]).astype(BF16)
            g_ref[at, :] = g16
            g = g16.astype(F32)
            normed = normed_ref[at, :]
            gpn_ref[at, :] = norm_back(g, normed, inv_ref[at, 0:1], gain)
            gain_sum += jnp.sum(g * normed, axis=0, keepdims=True)
    for part in parts:
        s0_ref[part, :] = nt_dot(gpn_ref[part, :], w_out_ref[...])
    bias_sum = jnp.zeros((1, feat), F32)
    for part in parts:
        for at in pieces(part):
            gpre = (s0_ref[at, :] * dact_ref[at, :]).astype(BF16)
            gpre_ref[at, :] = gpre
            bias_sum += jnp.sum(gpre.astype(F32), axis=0, keepdims=True)
    sums_ref[...] = jnp.concatenate([bias_sum, gain_sum, jnp.zeros((EXTRA - 2, feat), F32)], 0)


def message_grads(gpre_ref, back_ref, w_agg_ref, gm_ref, t_ref):
    total, feat = gpre_ref.shape
    for m, part in enumerate(parts_of(total, 2)):
        cols = slice(m * feat, (m + 1) * feat)
        gm = nt_dot(gpre_ref[part, :], w_agg_ref[...]).astype(BF16)
        gm_ref[:, cols] = gm
        t_ref[:, cols] = two_dot(back_ref, gm)


def third_kernel(
    gpre_ref, gpn_ref, sums_ref, back_ref, w_agg_ref, la_ref, lb_ref, keep1_ref, send1_ref,
    keep_ref, send_ref, near_ref, far_ref, gm_ref, t_ref,
):
    ride = near_ref.shape[0]
    first = send1_ref.shape[0]

    @on_core(0)
    def _():
        weight_products(la_ref, lb_ref, gpre_ref, gpn_ref, sums_ref[...], keep_ref, send_ref)
        message_grads(gpre_ref, back_ref, w_agg_ref, gm_ref, t_ref)
        below, cross = (send_ref.at[pl.ds(first + i * ride, ride), :] for i in (0, 1))
        put_halo_grads(t_ref, (near_ref, cross, below, far_ref.at[pl.ds(0, ride), :]))
        far_ref[ride:, :] = send_ref[first + ride :, :]

    @on_core(1)
    def _():
        keep_ref[...] = keep1_ref[...]
        send_ref[:first, :] = send1_ref[...]


def plain_third_kernel(gpre_ref, back_ref, w_agg_ref, o0, o1, o2, o3, gm_ref, t_ref):
    message_grads(gpre_ref, back_ref, w_agg_ref, gm_ref, t_ref)
    put_halo_grads(t_ref, (o0, o1, o2, o3))


def halve_job(mine, keep, recv, keep2, send2):
    n, rows, _ = keep2.shape
    for i in range(n):
        d, o = 2 * i + mine, 2 * i + 1 - mine
        at = pl.ds(pl.multiple_of(o * rows, 8), rows)
        send2[i * rows : (i + 1) * rows, :] = (keep[o] + recv[at, :].astype(F32)).astype(BF16)
        at = pl.ds(pl.multiple_of(d * rows, 8), rows)
        keep2[i] = keep[d] + recv[at, :].astype(F32)


def carry_kernel(keep, recv, near_ref, _, keep2, send2):
    ride = near_ref.shape[0]
    halve_job(second_bit(), keep, recv, keep2, send2)
    at = keep2.shape[0] * keep2.shape[1]

    @on_core(0)
    def _():
        send2[at : at + ride, :] = near_ref[...]
        send2[at + ride :, :] = recv[recv.shape[0] - ride :, :]


def halve_kernel(keep, recv, _, keep2, send2):
    halve_job(dom_bit(2), keep, recv, keep2, send2)


def sums_out(keep, recv, node_ref, agg_ref, out_ref, bias_ref, gain_ref):
    share = node_ref.shape[0]
    total = keep[0] + recv[...].astype(F32)
    node_ref[...] = total[0:share]
    agg_ref[...] = total[share : 2 * share]
    out_ref[...] = total[2 * share : 3 * share]
    bias_ref[...] = total[3 * share : 3 * share + 1]
    gain_ref[...] = total[3 * share + 1 : 3 * share + 2]


def cot_out(skips, onehot_ref, sources, cpart_ref, other_ref, cot_ref):
    micro, rows, feat = cot_ref.shape
    n = onehot_ref.shape[1] // PEERS
    inner = dom_bit(0) != dom_bit(1)

    @on_core(1)
    def _():
        for m in range(micro):
            cot_ref[m] = other_ref[m * rows : (m + 1) * rows, :]

    @on_core(0)
    def _():
        for m in range(micro):
            got = [r[s + m * n : s + (m + 1) * n, :] for r, s in zip(sources, skips)]
            if len(got) > PEERS:
                got[1] = jnp.where(inner, got[1], got.pop())
            ret = jnp.concatenate(got, 0)
            cot_ref[m] = (
                cpart_ref[m * rows : (m + 1) * rows, :] + nn_dot(onehot_ref[...], ret)
            ).astype(BF16)


def final_kernel(skips, onehot_ref, *rest):
    *sources, cpart_ref, other_ref, keep, recv, cot_ref, node_ref, agg_ref, out_ref, bias_ref, gain_ref = rest
    cot_out(skips, onehot_ref, sources, cpart_ref, other_ref, cot_ref)
    sums_out(keep, recv, node_ref, agg_ref, out_ref, bias_ref, gain_ref)


def cot_kernel(skips, onehot_ref, *rest):
    *sources, cpart_ref, other_ref, cot_ref = rest
    cot_out(skips, onehot_ref, sources, cpart_ref, other_ref, cot_ref)


def whole_kernel(x_ref, agg_ref, hidden_ref, gpn_ref, gpre_ref, node_ref, agg_out, out_ref):
    rows = x_ref.shape[1]
    gpre = gpre_ref[...]
    node_ref[...] = tn_dot(x_ref[0], gpre[:rows]) + tn_dot(x_ref[1], gpre[rows:])
    agg_out[...] = tn_dot(agg_ref[...], gpre)
    out_ref[...] = tn_dot(hidden_ref[...], gpn_ref[...])


def body(
    section_inputs,
    out_cot,
    w_node,
    w_agg,
    w_out,
    bias,
    gain,
    send_rows,
    blk_pairs,
    blk_count,
    blk_values,
):
    peers = lax.axis_size("dom")
    segment = lax.axis_index("segment")
    assert lax.axis_size("segment") == 2 and peers % 4 == 0
    x = section_inputs[0]
    micro, rows, feat = x.shape
    _, slots, per_peer = send_rows.shape
    assert slots * per_peer == 128 and slots == PEERS and micro == 2
    total = micro * rows
    values = blk_values[0]
    row_blocks = rows // 128
    wide = micro * feat
    w_n, w_a, w_o = w_node[0], w_agg[0], w_out[0]
    matmul = 2 * total * feat * feat
    size = total * feat
    chunk = shape((micro * per_peer, feat), BF16)

    def swap_partner(p, k):
        if k == 0:
            return p ^ 1
        if k == 1:
            return (p + 1 if p & 1 else p - 1) % peers
        up = (p >> 1) & 1
        return (p + 2 if up == (k == 3) else p - 2) % peers

    def swapped(v, k, cores):
        return lax.ppermute(
            v,
            ("dom", "segment"),
            [(2 * p + s, 2 * swap_partner(p, k) + d) for p in range(peers) for s, d in cores],
        )

    def across(v):
        return lax.ppermute(v, "segment", [(0, 1), (1, 0)])

    def flipped(v, bits):
        return lax.ppermute(
            v,
            ("dom", "segment"),
            [(2 * p + s, 2 * (p ^ (1 << bits[s])) + s) for p in range(peers) for s in (0, 1)],
        )

    f_full, b_full = shape((total, feat), F32), shape((total, feat), BF16)
    s_sums = shape((EXTRA, feat), F32)
    dma = pltpu.SemaphoreType.DMA
    *outgoing, x, onehot = call(
        gather_kernel,
        [chunk] * slots + [shape(x.shape, BF16), shape((rows, slots * per_peer), BF16)],
        [pltpu.VMEM(send_rows.shape, jnp.int32), dma((2,))],
        matmul // 8, 2 * size, send_rows, x,
        raw=2,
    )
    same, other_core = ((0, 0), (1, 1)), ((0, 1), (1, 0))
    w_other = across(w_n)
    halos = [swapped(v, k, same) for k, v in enumerate(outgoing)]
    halo_rows = slots * per_peer
    loaded = (w_n, w_a, w_o, gain, out_cot)
    z, acc, halo_in, local_back, halo_back, w_n, w_a, w_o, gain, g_last = call(
        node_kernel,
        [f_full, shape((rows, wide), F32), shape((2, rows, halo_rows), BF16)]
        + [shape((2, rows, rows), BF16), shape((2, halo_rows, rows), BF16)]
        + [shape(v.shape, BF16) for v in loaded],
        [
            pltpu.VMEM(values.shape, BF16), pltpu.VMEM((rows, wide), BF16), pltpu.VMEM(bias.shape, BF16),
            pltpu.VMEM((row_blocks, row_blocks + 1, 128, 128), F32), pltpu.VMEM((2, rows, rows), BF16),
            dma((7,)),
        ],
        2 * matmul, 8 * size,
        blk_pairs, blk_count, values, w_n, bias, w_a, w_o, gain, out_cot, x,
        scalars=2, raw=7,
    )
    first = call(
        first_kernel,
        [chunk] * slots
        + [shape((2 * rows, wide), BF16), f_full, f_full, shape((total, 128), F32)]
        + [b_full] * 4 + [s_sums],
        [
            pltpu.VMEM((halo_rows, wide), BF16),
            pltpu.VMEM((total, feat), F32),
            pltpu.VMEM((halo_rows, wide), F32),
        ],
        4 * matmul, 20 * size,
        *halos, halo_in, halo_back, z, acc, g_last, w_a, w_o, gain, w_other,
        after=1,
    )
    to_return = first[:slots]
    both, dact, normed, inv_std, agg, hidden, gpn1, gpre1, sums1 = first[slots:]
    returned = [swapped(v, k, other_core) for k, v in enumerate(to_return)]
    c_in = call(
        upper_kernel, f_full, [], matmul, 10 * size, g_last, across(both), local_back, w_other
    )
    share = feat // peers
    rows_each = 3 * share + EXTRA
    halving = peers == 8

    def kept(n, extra=0):
        return [shape((n, rows_each, feat), F32), shape((n * rows_each + extra, feat), BF16)]

    if halving:
        turned = call(
            functools.partial(turn_kernel, peers),
            [shape((16 * share, total), BF16), shape((8 * share, total), BF16)] + kept(4),
            [pltpu.VMEM((feat, total), BF16)],
            3 * matmul, 20 * size,
            x, agg, hidden, gpre1, gpn1, sums1,
        )
    g_low, gpn, gpre, sums = call(
        second_kernel,
        [b_full, b_full, b_full, s_sums],
        [pltpu.VMEM((total, feat), F32)],
        2 * matmul, 16 * size,
        onehot, *returned, c_in, dact, normed, inv_std, w_o, gain,
    )
    scr_t, gm_out = pltpu.VMEM((halo_rows, wide), F32), shape((rows, wide), BF16)
    if halving:
        ride = chunk.shape[0]
        ride = chunk.shape[0]
        keep, send, near, far, gm = call(
            third_kernel,
            kept(4, 2 * ride) + [chunk, shape((2 * ride, feat), BF16), gm_out],
            [scr_t], 4 * matmul, 16 * size,
            gpre, gpn, sums, halo_back, w_a, *turned,
        )
        recv = flipped(send, (1, 0))
        far = swapped(far, 3, ((0, 0),))
    else:
        *to_return, gm = call(
            plain_third_kernel, [chunk] * slots + [gm_out], [scr_t],
            2 * matmul, 8 * size, gpre, halo_back, w_a,
        )
    cpart0, g_low = call(
        lower_kernel, [f_full, b_full], [], matmul, 10 * size, g_low, gpre, gm, local_back, w_n
    )
    other = across(g_low)
    cot_shape = shape((micro, rows, feat), BF16)
    if halving:
        up = recv
        keep, send = call(
            carry_kernel, kept(2, 2 * ride), [], size, 8 * size, keep, recv, near, cpart0,
            after=1,
        )
        recv = flipped(send, (0, 1))
        hop = swapped(far, 0, ((0, 0),))
        first = 2 * rows_each
        returned = (recv, recv, up, far, hop)
        skips = (first, first + ride, 2 * first, 0, ride)
        keep, send = call(
            halve_kernel, kept(1), [], size, 4 * size, keep, recv, far,
            after=1,
        )
        recv = flipped(send, (2, 2))
        part, row = shape((share, feat), F32), shape((1, feat), F32)
        cot, grad_node, grad_agg, grad_out, grad_bias, grad_gain = call(
            functools.partial(final_kernel, skips), [cot_shape, part, part, part, row, row],
            [], matmul // 4, 6 * size,
            onehot, *returned, cpart0, other, keep, recv,
        )
    else:
        is_last = segment == 1
        gpn, gpre = jnp.where(is_last, gpn1, gpn), jnp.where(is_last, gpre1, gpre)
        sums = jnp.where(is_last, sums1, sums)
        square = shape((feat, feat), F32)
        full = call(
            whole_kernel, [square] * 3, [], 3 * matmul, 12 * size, x, agg, hidden, gpn, gpre
        )
        grad_node, grad_agg, grad_out = [
            lax.psum_scatter(v, "dom", scatter_dimension=0, tiled=True) for v in full
        ]
        sums = lax.psum(sums, "dom")
        grad_bias, grad_gain = sums[0:1], sums[1:2]
        returned = [swapped(v, k, ((0, 0),)) for k, v in enumerate(to_return)]
        cot = call(
            functools.partial(cot_kernel, (0,) * slots), cot_shape, [], matmul // 4, 4 * size,
            onehot, *returned, cpart0, other,
        )
    return (
        cot[None],
        grad_node[None],
        grad_agg[None],
        grad_out[None],
        grad_bias,
        grad_gain,
    )


def solution(mesh):
    placed = (
        P("segment", None, ("grp", "dom"), None),
        P(None, ("grp", "dom"), None),
        P("segment", None, None),
        P("segment", None, None),
        P("segment", None, None),
        P("segment", None),
        P("segment", None),
        P("dom", None, None),
        P("dom", None, None),
        P("dom"),
        P("dom", None, None, None),
    )
    return jax.shard_map(
        body,
        mesh=mesh,
        in_specs=placed,
        out_specs=(
            P("segment", None, ("grp", "dom"), None),
            P("segment", ("grp", "dom"), None),
            P("segment", ("grp", "dom"), None),
            P("segment", ("grp", "dom"), None),
            P("segment", "grp"),
            P("segment", "grp"),
        ),
        check_vma=False,
    )
```
